32 devices in a mesh: solver: 8 (over y, x, core), group: 4 (over z).
Axes of the slice: x: 2, y: 2, z: 4, core: 2. Of those that a mesh axis runs over, the one named last changes fastest.
Arguments:
- field: float32 [8, 8, 8, 8192], P(None, None, None, ('solver', 'group')), may hold values from -6 to 6
- first_weight: bfloat16 [8, 1024], replicated, may hold values from -2 to 2
- second_weight: bfloat16 [1024, 1], replicated, may hold values from -0.1875 to 0.1875
- face_edges: int32 [2, 256], replicated, may hold values from 0 to 63, as said below
- sample_index: int32 [2048], P(('solver', 'group')), may hold values from 0 to 31
- route: int32 [2048, 1], P(('solver', 'group')), may hold values from 0 to 7; in each aligned block of 64 rows (0 to 63, 64 to 127, ...) at most 16 rows name the same one
Outputs:
- new_field: float32 [8, 8, 8, 8192], P(None, None, None, ('solver', 'group'))
- new_first: bfloat16 [8, 1024], replicated
- new_second: bfloat16 [1024, 1], replicated
The draws below stay inside these ranges and needn't reach their ends.
Inputs may be any that keep to these rules, and one draw needn't show every extreme that they name: `sample_index`: indices of wall elements (ey = 0) of the sample's own device, in the order ex * 8 + ez; they may repeat. `route`: at most 16 of the samples of one device name one learner, a bound that some block reaches by some device in every draw. `face_edges`: no edge joins a node to itself; edges may repeat.
All inputs are finite; a program needn't handle non-finite values.
Results may differ from the reference program's by a relative error of at most 0.001.
The reference program's roundings to bfloat16 on the way (of `features`) count: a program that leaves them out, or rounds other values in their place, can miss the bound.
Values sent between devices are 32-bit elements; how exact they have to be, the bound alone decides.
A program may use at most 128 MiB of HBM per device.

```python
import math
import jax
import jax.numpy as jnp
import numpy as np
from jax import lax

P_SIZE = 8
HID = 1024
EDGES = 256
FLOW_STEPS = 5
EXL = 4
EZL = 8
EY = 8
SAMPLES_DEV = 64
CAP = 16
ELEMS = 8192
N_SOLVER = 8
N_GROUP = 4


def draw_face_edges(key, part):
    first, second = jax.random.split(jax.random.fold_in(key, 11))
    source = jax.random.randint(first, (EDGES,), 0, P_SIZE * P_SIZE)
    offset = jax.random.randint(second, (EDGES,), 1, P_SIZE * P_SIZE)
    return jnp.stack([source, (source + offset) % (P_SIZE * P_SIZE)]).astype(jnp.int32)


def with_ends(values, rng, smallest, largest):
    index_at = [jax.random.randint(jax.random.fold_in(rng, axis), (), 0, length) for axis, length in enumerate(values.shape)]
    main_axis = values.shape.index(max(values.shape))
    next_to = index_at[:main_axis] + [(index_at[main_axis] + 1) % values.shape[main_axis]] + index_at[main_axis + 1:]
    return values.at[tuple(index_at)].set(smallest).at[tuple(next_to)].set(largest)


def block_scale(key, extent, shards, least, largest):
    def one(axis_at, shards_of):
        heights = jax.random.uniform(jax.random.fold_in(jax.random.fold_in(key, 6), axis_at), (shards_of,), jnp.float32, least / len(shards), largest / len(shards))
        return jnp.repeat(jnp.exp(heights), extent[axis_at] // shards_of).reshape((-1,) + (1,) * (len(extent) - axis_at - 1))

    factor_of = one(*shards[0])
    for cut in shards[1:]:
        factor_of = factor_of * one(*cut)
    return factor_of


def routed_block(own_key, own, number, rows, amount, top, most, lean):
    ranking = jax.random.permutation(own_key, amount)
    crowded, common = shares(amount, rows * top, most, lean, True), shares(amount, rows * top, most, lean, False)
    places = jnp.arange(amount)

    def named(lengths, turn):
        used = int((lengths > 0).sum())
        fixed = max(1, used // 4)
        shifted = fixed + (places - fixed + turn * (used - fixed)) % max(1, amount - fixed)
        return jnp.zeros((amount,), jnp.int32).at[ranking[jnp.where(places < fixed, places, shifted)]].set(jnp.asarray(lengths, jnp.int32))

    lengths = jnp.where(number % 4 == 0, named(crowded, number // 4), named(common, number - number // 4 - 1))
    mixed = jax.random.permutation(jax.random.fold_in(own, 3), amount)
    source_of, taker = mixed[0:amount // 2 * 2:2], mixed[1:amount // 2 * 2:2]
    slack = jnp.minimum(lengths[source_of] - 1, most - lengths[taker]) // 2
    slack = jnp.where((source_of == ranking[0]) | (taker == ranking[0]) | (lengths[taker] == 0), 0, jnp.maximum(slack, 0))
    shifted = jax.random.randint(jax.random.fold_in(own, 4), (amount // 2,), 0, 1 << 20) % (slack + 1)
    lengths = lengths.at[source_of].add(-shifted).at[taker].add(shifted)
    labels = jnp.searchsorted(jnp.cumsum(lengths), jnp.arange(rows * top), side="right").astype(jnp.int32)
    table = labels.reshape(top, rows).T
    table = table[jax.random.permutation(jax.random.fold_in(own, 1), rows)]
    turn = jax.random.randint(jax.random.fold_in(own, 2), (rows, 1), 0, top)
    return jnp.take_along_axis(table, (jnp.arange(top)[None, :] + turn) % top, axis=1)


def shares(amount, total, reach, lean, full):
    weights = [(1 << 20) // math.isqrt(standing ** lean) + 1 for standing in range(1, amount + 1)]
    largest = reach if full else min(reach, max(-(-total // amount), total * weights[0] // sum(weights)))
    least = 1 if total - largest >= amount - 1 else 0
    given, spare = [largest] + [least] * (amount - 1), total - largest - least * (amount - 1)
    while spare > 0:
        movable = [i for i in range(1, amount) if given[i] < largest] or [i for i in range(1, amount) if given[i] < reach]
        mass, remaining = sum([weights[i] for i in movable]), spare
        for i in movable:
            more = min(reach - given[i], max(1, remaining * weights[i] // mass), spare)
            given[i] = given[i] + more
            spare = spare - more
    return np.array(given)


def centred(key, extent, scale, bound, cuts=(), held_as=jnp.bfloat16):
    values = scale * jax.random.normal(key, extent, jnp.float32)
    if cuts:
        values = values * block_scale(key, extent, cuts, -0.22, 0.18)
    return jnp.clip(values, -bound, bound).astype(held_as)


def setup_inputs(seed: int = 0) -> dict:
    key_list = jax.random.split(jax.random.key(seed), 7)
    field = centred(key_list[0], (P_SIZE, P_SIZE, P_SIZE, ELEMS), 1.0, 6.0, ((3, 32),), jnp.float32)
    first_weight = centred(key_list[1], (P_SIZE, HID), P_SIZE ** -0.5, 2.0)
    second_weight = centred(key_list[2], (HID, 1), HID ** -0.5, 0.1875)
    face_edges = draw_face_edges(jax.random.fold_in(key_list[6], 71), 0)
    sample_index = with_ends(jax.random.randint(key_list[4], (N_SOLVER * N_GROUP * SAMPLES_DEV,), 0, EXL * EZL), jax.random.fold_in(key_list[4], 1), 0, (EXL * EZL) - 1).astype(jnp.int32)
    route_keys = jax.random.split(jax.random.fold_in(key_list[5], 1), (N_SOLVER * N_GROUP * SAMPLES_DEV) // SAMPLES_DEV)
    route_turns = jax.random.permutation(jax.random.fold_in(key_list[5], 3), (N_SOLVER * N_GROUP * SAMPLES_DEV) // SAMPLES_DEV)
    route = jax.vmap(lambda own, number: routed_block(jax.random.fold_in(key_list[5], 2), own, number, SAMPLES_DEV, N_SOLVER, 1, CAP, 2))(route_keys, route_turns).reshape((N_SOLVER * N_GROUP * SAMPLES_DEV, 1))
    return dict(field=field, first_weight=first_weight, second_weight=second_weight, face_edges=face_edges, sample_index=sample_index, route=route)


HIGH = lax.Precision.HIGHEST
TIME_STEP = 0.002
VISCOSITY = 0.01
VELOCITY = 1.0
PENALTY = 1.0
STRESS_SCALE = 0.1
LEARN_RATE = 0.05


def legendre_table(points_x, points):
    table = np.zeros((points_x.shape[0], points))
    table[:, 0] = 1.0
    table[:, 1] = points_x
    for degree in range(2, points):
        table[:, degree] = ((2 * degree - 1) * points_x * table[:, degree - 1] - (degree - 1) * table[:, degree - 2]) / degree
    return table


def gll_tables(points):
    order = points - 1
    guess = np.cos(np.pi * np.arange(points) / order)
    for sweep in range(100):
        table = legendre_table(guess, points)
        guess = guess - (guess * table[:, order] - table[:, order - 1]) / (points * table[:, order])
    nodes = guess[::-1]
    values = legendre_table(nodes, points)[:, order]
    matrix = np.zeros((points, points))
    for row in range(points):
        for column in range(points):
            if row != column:
                matrix[row, column] = values[row] / (values[column] * (nodes[row] - nodes[column]))
    matrix[0, 0] = -order * (order + 1) / 4.0
    matrix[order, order] = order * (order + 1) / 4.0
    return jnp.asarray(matrix, jnp.float32), 2.0 / (order * (order + 1))


def face_adjacency(face_edges, nodes):
    columns = jnp.arange(nodes, dtype=jnp.int32)
    source = (face_edges[0][:, None] == columns[None, :]).astype(jnp.float32)
    target = (face_edges[1][:, None] == columns[None, :]).astype(jnp.float32)
    single = jnp.dot(source.T, target, precision=HIGH)
    tile = 128 // nodes
    return (0.25 * jnp.kron(jnp.eye(tile, dtype=jnp.float32), single)).astype(jnp.bfloat16)


def network_output(first_weight, second_weight, adjacency, features):
    width = first_weight.shape[1]
    tile = adjacency.shape[0]
    inputs = jnp.transpose(features, (1, 0, 2)).reshape(features.shape[1], -1)
    before = jnp.dot(first_weight.T, inputs, preferred_element_type=jnp.float32)
    hidden = jnp.maximum(before, 0.0).astype(jnp.bfloat16)
    spread = jnp.einsum('hbn,nm->hbm', hidden.reshape(width, -1, tile).astype(jnp.float32), adjacency.astype(jnp.float32)).reshape(width, -1)
    mixed = (hidden.astype(jnp.float32) + spread).astype(jnp.bfloat16)
    output = jnp.dot(second_weight.T, mixed, preferred_element_type=jnp.float32)
    return inputs, before, mixed, output


def block_grads(first_weight, second_weight, adjacency, features, target, share):
    width = first_weight.shape[1]
    tile = adjacency.shape[0]
    inputs, before, mixed, output = network_output(first_weight, second_weight, adjacency, features)
    node_share = jnp.repeat(share, features.shape[2])[None, :]
    error = ((output - target.reshape(1, -1).astype(jnp.float32)) * node_share).astype(jnp.bfloat16)
    grad_second = lax.dot_general(mixed, error, (((1,), (1,)), ((), ())), preferred_element_type=jnp.float32)
    back_mixed = jnp.dot(second_weight, error, preferred_element_type=jnp.float32).astype(jnp.bfloat16)
    back_spread = jnp.einsum('hbm,nm->hbn', back_mixed.reshape(width, -1, tile).astype(jnp.float32), adjacency.astype(jnp.float32)).reshape(width, -1)
    back_hidden = jnp.where(before > 0.0, back_mixed.astype(jnp.float32) + back_spread, 0.0).astype(jnp.bfloat16)
    grad_first = lax.dot_general(inputs, back_hidden, (((1,), (1,)), ((), ())), preferred_element_type=jnp.float32)
    return grad_first, grad_second


def learner_grads(first_weight, second_weight, adjacency, features, target, share):
    group_size = 32
    blocks = features.shape[0] // group_size
    points = features.shape[1]
    face = features.shape[2]

    def one_block(carry, pieces):
        grads = block_grads(first_weight, second_weight, adjacency, pieces[0], pieces[1], pieces[2])
        return (carry[0] + grads[0], carry[1] + grads[1]), None

    start = (jnp.zeros(first_weight.shape, jnp.float32), jnp.zeros(second_weight.shape, jnp.float32))
    pieces = (features.reshape(blocks, group_size, points, face), target.reshape(blocks, group_size, face), share.reshape(blocks, group_size))
    result, unused = lax.scan(one_block, start, pieces)
    return result


def flow_step(field, stress, deriv, second_deriv, gain):
    points = field.shape[0]
    last = points - 1
    along_x = jnp.einsum('ai,ijkxzy->ajkxzy', deriv, field, precision=HIGH)
    curve = (jnp.einsum('ai,ijkxzy->ajkxzy', second_deriv, field, precision=HIGH)
             + jnp.einsum('aj,ijkxzy->iakxzy', second_deriv, field, precision=HIGH)
             + jnp.einsum('ak,ijkxzy->ijaxzy', second_deriv, field, precision=HIGH))
    change = -2.0 * VELOCITY * along_x + 4.0 * VISCOSITY * curve
    before_x = jnp.roll(field[last], 1, axis=2)
    after_x = jnp.roll(field[0], -1, axis=2)
    before_z = jnp.roll(field[:, :, last], 1, axis=3)
    after_z = jnp.roll(field[:, :, 0], -1, axis=3)
    lower = field[:, 0]
    upper = field[:, last]
    lower_jump = PENALTY * (upper[..., :-1] - lower[..., 1:])
    lower_term = jnp.concatenate([stress[..., None], lower_jump], axis=4)
    above = jnp.concatenate([lower[..., 1:], jnp.zeros_like(lower[..., :1])], axis=4)
    upper_term = PENALTY * (above - upper)
    change = change.at[0].add(gain * (VELOCITY + PENALTY) * (before_x - field[0]))
    change = change.at[last].add(gain * PENALTY * (after_x - field[last]))
    change = change.at[:, :, 0].add(gain * PENALTY * (before_z - field[:, :, 0]))
    change = change.at[:, :, last].add(gain * PENALTY * (after_z - field[:, :, last]))
    change = change.at[:, 0].add(gain * lower_term)
    change = change.at[:, last].add(gain * upper_term)
    return field + TIME_STEP * change


def reference(field, first_weight, second_weight, face_edges, sample_index, route):
    points = P_SIZE
    face = points * points
    deriv, end_weight = gll_tables(points)
    second_deriv = jnp.dot(deriv, deriv, precision=HIGH)
    gain = 2.0 / end_weight
    devices = N_SOLVER * N_GROUP
    walls = EXL * EZL
    adjacency = face_adjacency(face_edges, face)
    blocks = field.reshape(points, points, points, devices, EXL, EZL, EY)
    wall_field = blocks[..., 0].reshape(points, points, points, devices, walls)
    features = jnp.transpose(wall_field, (3, 4, 1, 0, 2)).reshape(devices, walls, points, face).astype(jnp.bfloat16)
    slope = jnp.einsum('j,ijkdw->dwik', deriv[0], wall_field, precision=HIGH)
    target = (STRESS_SCALE * slope).reshape(devices, walls, face).astype(jnp.bfloat16)
    index = sample_index.reshape(devices, SAMPLES_DEV)
    owners = jnp.arange(devices, dtype=jnp.int32)[:, None]
    sample_features = features[owners, index].reshape(-1, points, face)
    sample_target = target[owners, index].reshape(-1, face)
    destination = route[:, 0].reshape(N_SOLVER, N_GROUP, SAMPLES_DEV)
    learners = jnp.arange(N_SOLVER, dtype=jnp.int32)
    hits = (destination[..., None] == learners[None, None, None, :]).astype(jnp.float32)
    counts = jnp.sum(hits, axis=(0, 2))
    share = jnp.einsum('sgrl,gl->sgr', hits, 1.0 / (jnp.maximum(counts, 1.0) * devices), precision=HIGH).reshape(-1)
    grad_first, grad_second = learner_grads(first_weight, second_weight, adjacency, sample_features, sample_target, share)
    new_first = (first_weight.astype(jnp.float32) - LEARN_RATE * grad_first).astype(jnp.bfloat16)
    new_second = (second_weight.astype(jnp.float32) - LEARN_RATE * grad_second).astype(jnp.bfloat16)
    every_wall = features.reshape(-1, 32, points, face)

    def infer(block):
        return network_output(new_first, new_second, adjacency, block)[3]

    outputs = lax.map(infer, every_wall)
    stress = outputs.reshape(N_SOLVER, N_GROUP, EXL, EZL, points, points)
    stress = jnp.transpose(stress, (4, 5, 0, 2, 1, 3)).reshape(points, points, N_SOLVER * EXL, N_GROUP * EZL)
    grid = field.reshape(points, points, points, N_SOLVER, N_GROUP, EXL, EZL, EY)
    grid = jnp.transpose(grid, (0, 1, 2, 3, 5, 4, 6, 7)).reshape(points, points, points, N_SOLVER * EXL, N_GROUP * EZL, EY)
    for step in range(FLOW_STEPS):
        grid = flow_step(grid, stress, deriv, second_deriv, gain)
    grid = grid.reshape(points, points, points, N_SOLVER, EXL, N_GROUP, EZL, EY)
    new_field = jnp.transpose(grid, (0, 1, 2, 3, 5, 4, 6, 7)).reshape(points, points, points, -1)
    return new_field, new_first, new_second
```

```python
import math

import jax
import jax.numpy as jnp
import numpy as np
from jax import lax
from jax.experimental import pallas as pl
from jax.experimental.pallas import tpu as pltpu
from jax.sharding import PartitionSpec as P

FLOW_STEPS = 5
EXL = 4
EZL = 8
EY = 8

HIGH = lax.Precision.HIGHEST
TIME_STEP = 0.002
VISCOSITY = 0.01
VELOCITY = 1.0
PENALTY = 1.0
STRESS_SCALE = 0.1
LEARN_RATE = 0.05
LANES = 128
F32 = jnp.float32
BF16 = jnp.bfloat16


def legendre_table(points_x, points):
    table = np.zeros((points_x.shape[0], points))
    table[:, 0] = 1.0
    table[:, 1] = points_x
    for degree in range(2, points):
        table[:, degree] = (
            (2 * degree - 1) * points_x * table[:, degree - 1] - (degree - 1) * table[:, degree - 2]
        ) / degree
    return table


def gll_tables(points):
    order = points - 1
    guess = np.cos(np.pi * np.arange(points) / order)
    for sweep in range(100):
        table = legendre_table(guess, points)
        guess = guess - (guess * table[:, order] - table[:, order - 1]) / (points * table[:, order])
    nodes = guess[::-1]
    values = legendre_table(nodes, points)[:, order]
    matrix = np.zeros((points, points))
    for row in range(points):
        for column in range(points):
            if row != column:
                matrix[row, column] = values[row] / (values[column] * (nodes[row] - nodes[column]))
    matrix[0, 0] = -order * (order + 1) / 4.0
    matrix[order, order] = order * (order + 1) / 4.0
    return matrix.astype(np.float32), 2.0 / (order * (order + 1))


def element_operator(deriv, gain):
    points = deriv.shape[0]
    last = points - 1
    deriv = deriv.astype(np.float64)
    second = 4.0 * VISCOSITY * (deriv @ deriv)
    along_i = -2.0 * VELOCITY * deriv + second
    along_i[0, 0] -= gain * (VELOCITY + PENALTY)
    along_i[last, last] -= gain * PENALTY
    other = second.copy()
    other[0, 0] -= gain * PENALTY
    other[last, last] -= gain * PENALTY
    eye = np.eye(points)
    whole = (
        np.kron(np.kron(along_i, eye), eye)
        + np.kron(np.kron(eye, other), eye)
        + np.kron(np.kron(eye, eye), other)
    )
    whole = (TIME_STEP * whole).astype(np.float32)
    high = whole.astype(jnp.bfloat16)
    low = (whole - high.astype(np.float32)).astype(jnp.bfloat16)
    return high, low


def split_np(value):
    value = value.astype(np.float32)
    high = value.astype(jnp.bfloat16)
    return high, (value - high.astype(np.float32)).astype(jnp.bfloat16)


def chain(local, from_before, from_after, count):
    points = local.shape[0]
    whole = np.kron(np.eye(count), local)
    for e in range(1, count):
        whole[e * points, e * points - 1] += from_before
        whole[e * points - 1, e * points] += from_after
    return whole


def response_tables(deriv, gain):
    points = deriv.shape[0]
    last = points - 1
    reach = FLOW_STEPS - 1
    deriv = deriv.astype(np.float64)
    second = TIME_STEP * 4.0 * VISCOSITY * (deriv @ deriv)
    one = TIME_STEP * gain * PENALTY
    two = TIME_STEP * gain * (VELOCITY + PENALTY)
    x_local = -TIME_STEP * 2.0 * VELOCITY * deriv + second
    x_local[0, 0] -= two
    x_local[last, last] -= one
    z_local = second.copy()
    z_local[0, 0] -= one
    z_local[last, last] -= one
    x_whole = chain(x_local, two, one, 3 * EXL)
    z_whole = np.eye(2 * EZL * points) + chain(z_local, one, one, 2 * EZL)
    y_whole = chain(z_local, one, one, EY)
    y_whole[0, 0] += one
    wide = LANES
    x_points = EXL * points
    z_points = EZL * points
    x_middle = slice(x_points, 2 * x_points)
    z_middle = slice(z_points // 2, z_points // 2 + z_points)
    z_left = np.concatenate(
        [np.linalg.matrix_power(z_whole, c)[z_middle] for c in range(reach + 1)], axis=0)
    x_right = np.zeros((reach + 1, wide, 2 * LANES))
    for m in range(reach + 1):
        for c in range(m + 1):
            power = np.linalg.matrix_power(x_whole, m - c)[x_middle]
            x_right[c, :3 * x_points, m * x_points:(m + 1) * x_points] = (
                math.comb(m, m - c) * power.T)
    x_right = x_right.reshape((reach + 1) * wide, 2 * LANES)
    first = np.zeros(EY * points)
    first[0] = one
    weights = np.zeros((reach + 1, EY * points))
    for m in range(reach + 1):
        value = first.copy()
        for b in range(reach - m + 1):
            weights[m] += math.comb(m + b, b) * value
            value = y_whole @ value
    weights = weights.reshape(reach + 1, EY, points).transpose(0, 2, 1)
    weights = np.tile(weights, (1, 1, LANES // EY))
    weights = np.repeat(weights.reshape(-1, 1, LANES), points, axis=1).reshape(-1, LANES)
    z_high, z_low = split_np(z_left)
    x_high, x_low = split_np(x_right)
    ez, k = np.divmod(np.arange(2 * EZL * points), points)
    q, rest = np.divmod(np.arange(EZL * 2 * points * points), 2 * points * points)
    h, rest = np.divmod(rest, points * points)
    gather = (ez[:, None] == (2 * q + h)[None]) & (k[:, None] == (rest % points)[None])
    row_z, rest = np.divmod(np.arange(EZL * EXL * points), EXL * points)
    row_x = rest // points
    col_x, rest = np.divmod(np.arange(EXL * EZL * EY), EZL * EY)
    col_z = rest // EY
    spread = (row_z[:, None] == col_z[None]) & (row_x[:, None] == col_x[None])
    return (
        gather.astype(jnp.bfloat16),
        np.concatenate([z_high, z_high, z_low], axis=1),
        np.concatenate([x_high, x_high, x_low], axis=0),
        np.concatenate([spread, spread], axis=0).astype(jnp.bfloat16),
        weights.astype(np.float32),
    )


def make_kernel(learners, groups, points, width, deriv, gain, tables):
    face = points * points
    last = points - 1
    nodes = face * points
    walls = EXL * EZL
    elements = walls * EY
    pairs = walls * face // (2 * LANES)
    owners = min(learners, width // LANES)
    owned = width // owners
    devices = learners * groups
    block = EZL * EY
    half = LANES // 2
    step_gain = float(TIME_STEP * gain * PENALTY)
    step_gain_x = float(TIME_STEP * gain * (VELOCITY + PENALTY))
    first_row = [float(value) for value in deriv[0]]

    def roll(value, shift):
        shift = shift % LANES
        return value if shift == 0 else pltpu.roll(value, shift, 1)

    rows_sent = points
    reach = FLOW_STEPS - 1
    around = [(dx, dz) for dx in (0, 1, -1) for dz in (0, 1, -1) if dx or dz]
    lane_rows = walls * face // LANES

    def kernel(
        field_ref, first_ref, second_ref, edges_ref, index_ref, route_ref, high_hbm, low_hbm,
        gather_hbm, zleft_hbm, xright_hbm, spread_hbm, weights_hbm,
        out_ref, new_first_ref, new_second_ref,
        u_ref, high_ref, low_ref, gather_ref, zleft_ref, xright_ref, spread_ref, weights_ref,
        mask_ref, feat_ref, turn_ref, z_ref, g_ref, e_ref, w2_ref,
        count_ref, tile_ref, part_ref, cross_ref, total_ref, stress_ref, place_ref, plane_ref,
        xs_ref, xr_ref, zs_ref, zr_ref,
        load_sem, count_send, count_recv, part_send, part_recv, cross_send, cross_recv,
        total_send, total_recv, stress_send, stress_recv, xs_send, xr_recv, zs_send, zr_recv,
    ):
        me = lax.axis_index("solver")
        mine = lax.axis_index("group")

        def peer_s(offset):
            return lax.rem(me + offset, learners)

        def peer_g(offset):
            return lax.rem(mine + offset, groups)

        loads = [
            pltpu.make_async_copy(
                field_ref.at[:, pl.ds(part * LANES, LANES)], u_ref.at[0, part], load_sem.at[part])
            for part in range(2)
        ]
        loads.append(pltpu.make_async_copy(high_hbm, high_ref, load_sem.at[2]))
        loads.append(pltpu.make_async_copy(low_hbm, low_ref, load_sem.at[3]))
        for at, (table, held_table) in enumerate((
            (gather_hbm, gather_ref), (zleft_hbm, zleft_ref), (xright_hbm, xright_ref),
            (spread_hbm, spread_ref), (weights_hbm, weights_ref),
        )):
            loads.append(pltpu.make_async_copy(table, held_table, load_sem.at[4 + at]))
        for load in loads:
            load.start()

        barrier = pltpu.get_barrier_semaphore()
        for offset in range(1, learners):
            pl.semaphore_signal(
                barrier, inc=1, device_id={"solver": peer_s(offset)},
                device_id_type=pl.DeviceIdType.MESH,
            )
        for offset in range(1, groups):
            pl.semaphore_signal(
                barrier, inc=1, device_id={"group": peer_g(offset)},
                device_id_type=pl.DeviceIdType.MESH,
            )
        for dx, dz in around:
            if dx and dz:
                pl.semaphore_signal(
                    barrier, inc=1,
                    device_id={"solver": peer_s(dx % learners), "group": peer_g(dz % groups)},
                    device_id_type=pl.DeviceIdType.MESH,
                )

        def remote(source, target, send, recv, where):
            return pltpu.make_async_remote_copy(
                src_ref=source, dst_ref=target, send_sem=send, recv_sem=recv,
                device_id=where, device_id_type=pl.DeviceIdType.MESH,
            )

        lane = lax.broadcasted_iota(jnp.int32, (1, LANES), 1)
        low_half = lane < half
        slot = lax.rem(lane, block) // EY
        level = lax.rem(lane, EY)
        contract = (((1,), (1,)), ((), ()))

        learner_rows = lax.broadcasted_iota(jnp.int32, (learners, route_ref.shape[1]), 0)
        hits = (route_ref[...] == learner_rows).astype(F32)
        count_ref[me] = jnp.broadcast_to(jnp.sum(hits, axis=1, keepdims=True), (learners, LANES))

        edge_rows = lax.rem(
            lax.broadcasted_iota(jnp.int32, (LANES, edges_ref.shape[1]), 0), face)
        source = (edges_ref[0:1, :] == edge_rows).astype(F32).astype(BF16)
        sink = (edges_ref[1:2, :] == edge_rows).astype(F32).astype(BF16)
        node_rows = lax.broadcasted_iota(jnp.int32, (LANES, LANES), 0)
        node_cols = lax.broadcasted_iota(jnp.int32, (LANES, LANES), 1)
        small = 0.25 * lax.dot_general(source, sink, contract, preferred_element_type=F32)
        small = jnp.where(node_rows // face == node_cols // face, small, 0.0)
        small = small + (node_rows == node_cols).astype(F32)
        first = first_ref[...].astype(F32)
        second = second_ref[...].astype(F32)

        def copies(step):
            right, left = {"solver": peer_s(1)}, {"solver": peer_s(learners - 1)}
            up, down = {"group": peer_g(1)}, {"group": peer_g(groups - 1)}
            result = []
            for side, where in ((0, right), (1, left)):
                result.append(remote(
                    xs_ref.at[step, side], xr_ref.at[step, side],
                    xs_send.at[step, side], xr_recv.at[step, side], where))
            for side, where in ((0, up), (1, down)):
                result.append(remote(
                    zs_ref.at[step, side], zr_ref.at[step, side],
                    zs_send.at[step, side], zr_recv.at[step, side], where))
            return result

        half_face = face // 2

        def near(i):
            return pl.ds(i * face, points, stride=points)

        def far(i):
            return pl.ds(i * face + last, points, stride=points)

        def send_z(step, bottoms, tops):
            for part in range(2):
                high_pack = jnp.zeros((points, LANES), F32)
                low_pack = jnp.zeros((points, LANES), F32)
                for i in range(points):
                    high_pack = jnp.where(slot == i, roll(tops[part][i], EY * (i + 1)), high_pack)
                    low_pack = jnp.where(slot == i, roll(bottoms[part][i], EY * i), low_pack)
                zs_ref[step, 0, part] = high_pack
                zs_ref[step, 1, part] = low_pack
            every = copies(step)
            every[2].start()
            every[3].start()

        def send_x(step, u):
            upper = u[1, pl.ds(nodes - face, face), :]
            xs_ref[step, 0] = jnp.where(low_half, roll(upper[:half_face], half), upper[half_face:])
            lower = u[0, pl.ds(0, face), :]
            xs_ref[step, 1] = jnp.where(low_half, lower[:half_face], roll(lower[half_face:], half))
            every = copies(step)
            every[0].start()
            every[1].start()

        def send_faces(step, u):
            send_z(step, [[u[part, near(i), :] for i in range(points)] for part in range(2)],
                   [[u[part, far(i), :] for i in range(points)] for part in range(2)])
            send_x(step, u)

        start = u_ref.at[0]
        for load in loads[:2]:
            load.wait()

        def face_rows(value_of):
            rows = jnp.concatenate([value_of(i) for i in range(points)], axis=0)
            return jnp.concatenate([rows, rows], axis=0).astype(BF16)

        def plane(i, j):
            at = pl.ds(i * face + j * points, points)
            return jnp.concatenate([start[0, at, :], start[1, at, :]], axis=1)

        def slope(i):
            total = None
            for j in range(points):
                term = first_row[j] * plane(i, j)
                total = term if total is None else total + term
            return STRESS_SCALE * total

        wall_rows = lax.broadcasted_iota(jnp.int32, (walls, elements), 0)
        wall_cols = lax.broadcasted_iota(jnp.int32, (walls, elements), 1)
        wall_at = (
            lax.rem(wall_rows // 2, EXL) * EZL + wall_rows // (2 * EXL) * 2 + lax.rem(wall_rows, 2))
        select = (wall_cols == wall_at * EY).astype(F32).astype(BF16)
        for j in range(points):
            turn_ref[pl.ds(j * walls, walls), :] = lax.dot_general(
                select, face_rows(lambda i: plane(i, j)), contract, preferred_element_type=F32)
        turn_ref[pl.ds(points * walls, walls), :] = lax.dot_general(
            select, face_rows(slope), contract, preferred_element_type=F32)
        for row in range(lane_rows):
            even = turn_ref[pl.ds(2 * row, points, stride=walls), :]
            odd = turn_ref[pl.ds(2 * row + 1, points, stride=walls), :]
            feat_ref[row // 2, :, pl.ds((row % 2) * LANES, LANES)] = jnp.where(low_half, even, odd)
        target = jnp.where(
            low_half,
            turn_ref[pl.ds(points * walls, lane_rows, stride=2), :],
            turn_ref[pl.ds(points * walls + 1, lane_rows, stride=2), :],
        )

        pl.semaphore_wait(barrier, learners + groups + 2)
        for offset in range(1, learners):
            remote(count_ref.at[me], count_ref.at[me], count_send.at[offset], count_recv.at[me],
                   {"solver": peer_s(offset)}).start()
        send_faces(0, start)

        def network(first, second, learn):
            turned = jnp.transpose(first).astype(BF16)
            w2_ref[...] = jnp.transpose(jnp.broadcast_to(second, (LANES, width)))

            def one(pair, carry):
                before = jnp.dot(turned, feat_ref[pair].astype(BF16), preferred_element_type=F32)
                hidden = jnp.maximum(before, 0.0)
                if learn:
                    mask_ref[pair] = jnp.where(before > 0.0, 1.0, 0.0).astype(BF16)
                weight = w2_ref[...]
                z_ref[pl.ds(2 * pair, 1), :] = jnp.sum(
                    hidden[:, :LANES] * weight, axis=0, keepdims=True)
                z_ref[pl.ds(2 * pair + 1, 1), :] = jnp.sum(
                    hidden[:, LANES:] * weight, axis=0, keepdims=True)
                return carry

            lax.fori_loop(0, pairs, one, 0, unroll=pairs)
            return jnp.dot(z_ref[...], small, precision=HIGH, preferred_element_type=F32)

        output = network(first, second, True)

        for offset in range(1, learners):
            origin = peer_s(offset)
            remote(count_ref.at[me], count_ref.at[origin], count_send.at[offset],
                   count_recv.at[origin], {"solver": origin}).wait_recv()
        counts = count_ref[0]
        for other in range(1, learners):
            counts = counts + count_ref[other]
        inverse = 1.0 / (jnp.maximum(counts, 1.0) * devices)
        places = 2 * lax.broadcasted_iota(jnp.int32, (lane_rows, index_ref.shape[1]), 0)
        taken = index_ref[...]
        taken = 2 * (lax.rem(taken, EZL) // 2 * EXL + taken // EZL) + lax.rem(taken, 2)
        chosen = (taken == places).astype(F32)
        even = lax.dot_general(chosen, hits, contract, preferred_element_type=F32)
        chosen = (taken == places + 1).astype(F32)
        odd = lax.dot_general(chosen, hits, contract, preferred_element_type=F32)
        difference = output - target
        error = jnp.zeros((lane_rows, LANES), F32)
        for learner in range(learners):
            times = jnp.where(low_half, even[:, learner:learner + 1], odd[:, learner:learner + 1])
            single = (difference * inverse[learner:learner + 1]).astype(BF16).astype(F32)
            error = error + times * single
        e_ref[...] = error
        g_ref[...] = lax.dot_general(
            error, small, contract, precision=HIGH, preferred_element_type=F32)

        def split(value):
            upper = value.astype(BF16).astype(F32)
            return jnp.concatenate([upper, value - upper], axis=0).astype(BF16)

        def row_pair(ref, pair):
            return jnp.concatenate([ref[pl.ds(2 * pair, 1), :], ref[pl.ds(2 * pair + 1, 1), :]], axis=1)

        moment = None
        for pair in range(pairs):
            term = lax.dot_general(
                split(feat_ref[pair] * row_pair(g_ref, pair)), mask_ref[pair], contract,
                preferred_element_type=F32)
            moment = term if moment is None else moment + term
        moment = moment[0:points] + moment[points:2 * points]
        for t in range(owners):
            tile_ref[t] = moment[:, t * owned:(t + 1) * owned]

        def when_owner(which, action):
            if owners == learners:
                action()
            else:
                pl.when(which < owners)(action)

        def clamp(which):
            return which if owners == learners else jnp.minimum(which, owners - 1)

        def part_copy(offset):
            where = peer_s(offset)
            return where, remote(tile_ref.at[clamp(where)], part_ref.at[me], part_send.at[offset],
                                 part_recv.at[me], {"solver": where})

        for offset in range(1, learners):
            where, copy = part_copy(offset)
            when_owner(where, copy.start)

        def local(source, target):
            u = jnp.concatenate([source[0], source[1]], axis=1)
            upper = u.astype(BF16)
            lower = (u - upper.astype(F32)).astype(BF16)
            u = u + (
                jnp.dot(high_ref[...], upper, preferred_element_type=F32)
                + jnp.dot(high_ref[...], lower, preferred_element_type=F32)
                + jnp.dot(low_ref[...], upper, preferred_element_type=F32)
            )
            for part in range(2):
                target[part] = u[:, part * LANES:(part + 1) * LANES]
            for part in range(2):
                for i in range(points):
                    base = i * face
                    bottom = source[part, pl.ds(base, points), :]
                    top = source[part, pl.ds(base + face - points, points), :]
                    below = jnp.where(level == 0, bottom, roll(top, 1))
                    above = jnp.where(level == EY - 1, 0.0, roll(bottom, -1))
                    target[part, pl.ds(base, points), :] += step_gain * below
                    target[part, pl.ds(base + face - points, points), :] += step_gain * above
            low0 = roll(source[0, pl.ds(nodes - face, face), :], half)
            low1 = roll(source[1, pl.ds(nodes - face, face), :], half)
            target[0, pl.ds(0, face), :] += step_gain_x * jnp.where(low_half, 0.0, low0)
            target[1, pl.ds(0, face), :] += step_gain_x * jnp.where(low_half, low0, low1)
            high0 = roll(source[0, pl.ds(0, face), :], half)
            high1 = roll(source[1, pl.ds(0, face), :], half)
            target[0, pl.ds(nodes - face, face), :] += step_gain * jnp.where(low_half, high0, high1)
            target[1, pl.ds(nodes - face, face), :] += step_gain * jnp.where(low_half, high1, 0.0)
            for part in range(2):
                for i in range(points):
                    before = jnp.where(slot == 0, 0.0, roll(source[part, far(i), :], EY))
                    after = jnp.where(slot == EZL - 1, 0.0, roll(source[part, near(i), :], -EY))
                    target[part, near(i), :] = target[part, near(i), :] + step_gain * before
                    target[part, far(i), :] = target[part, far(i), :] + step_gain * after

        def halo(step, target, send):
            every = copies(step)
            every[0].wait_recv()
            every[1].wait_recv()
            ghost = xr_ref[step, 0]
            ghost = jnp.concatenate([ghost, roll(ghost, half)], axis=0)
            target[0, pl.ds(0, face), :] += step_gain_x * jnp.where(low_half, ghost, 0.0)
            ghost = xr_ref[step, 1]
            ghost = jnp.concatenate([roll(ghost, half), ghost], axis=0)
            target[1, pl.ds(nodes - face, face), :] += step_gain * jnp.where(low_half, 0.0, ghost)
            every[2].wait_recv()
            every[3].wait_recv()
            bottoms, tops = [], []
            for part in range(2):
                before_pack = step_gain * zr_ref[step, 0, part]
                after_pack = step_gain * zr_ref[step, 1, part]
                for i in range(points):
                    before = jnp.where(slot == 0, roll(before_pack, half - EY * i), 0.0)
                    after = jnp.where(
                        slot == EZL - 1, roll(after_pack, EY * (EZL - 1 - i)), 0.0)
                    bottoms.append(target[part, near(i), :] + before)
                    tops.append(target[part, far(i), :] + after)
                    target[part, near(i), :] = bottoms[-1]
                    target[part, far(i), :] = tops[-1]
            if send:
                send_z(step + 1, [bottoms[:points], bottoms[points:]], [tops[:points], tops[points:]])
                send_x(step + 1, target)

        for load in loads[2:]:
            load.wait()
        held = [start, u_ref.at[1]]

        def flow(step):
            source, target = held[step % 2], held[(step + 1) % 2]
            local(source, target)
            halo(step, target, step < FLOW_STEPS - 1)

        flow(0)

        def reduce_part():
            total = tile_ref[clamp(me)]
            for offset in range(1, learners):
                origin = peer_s(offset)
                remote(tile_ref.at[0], part_ref.at[origin], part_send.at[offset],
                       part_recv.at[origin], {"solver": origin}).wait_recv()
            for offset in range(1, learners):
                total = total + part_ref[peer_s(offset)]
            cross_ref[mine] = total
            for offset in range(1, groups):
                remote(cross_ref.at[mine], cross_ref.at[mine], cross_send.at[offset],
                       cross_recv.at[mine], {"group": peer_g(offset)}).start()

        def reduce_cross():
            for offset in range(1, groups):
                origin = peer_g(offset)
                remote(cross_ref.at[mine], cross_ref.at[origin], cross_send.at[offset],
                       cross_recv.at[origin], {"group": origin}).wait_recv()
            total = cross_ref[0]
            for origin in range(1, groups):
                total = total + cross_ref[origin]
            at = clamp(me)
            total_ref[at] = total
            for offset in range(1, learners):
                remote(total_ref.at[at], total_ref.at[at], total_send.at[offset],
                       total_recv.at[at], {"solver": peer_s(offset)}).start()

        when_owner(me, reduce_part)
        flow(1)
        when_owner(me, reduce_cross)
        flow(2)
        for offset in range(1, learners):
            origin = peer_s(offset)
            at = clamp(origin)
            copy = remote(total_ref.at[at], total_ref.at[at], total_send.at[offset],
                          total_recv.at[at], {"solver": origin})
            when_owner(origin, copy.wait_recv)

        sums = jnp.concatenate([total_ref[t] for t in range(owners)], axis=1)
        grad_second = jnp.sum(first * sums, axis=0, keepdims=True)
        new_first = (first - LEARN_RATE * (sums * second)).astype(BF16)
        new_second = (second - LEARN_RATE * grad_second).astype(BF16)
        new_first_ref[...] = new_first
        new_second_ref[...] = new_second

        middle = pl.ds(lane_rows // 2, lane_rows)
        stress_ref[1, middle, :] = network(new_first.astype(F32), new_second.astype(F32), False)
        stress_copies = []
        for way, (dx, dz) in enumerate(around):
            rows = {
                0: (middle, middle),
                1: (pl.ds(lane_rows, lane_rows // 2), pl.ds(0, lane_rows // 2)),
                -1: (pl.ds(lane_rows // 2, lane_rows // 2), pl.ds(3 * lane_rows // 2, lane_rows // 2)),
            }[dz]
            stress_copies.append(remote(
                stress_ref.at[1, rows[0]], stress_ref.at[1 - dx, rows[1]],
                stress_send.at[way], stress_recv.at[way],
                {"solver": peer_s(dx % learners), "group": peer_g(dz % groups)}))
        for copy in stress_copies:
            copy.start()
        for step in range(3, FLOW_STEPS):
            flow(step)
        for copy in stress_copies:
            copy.wait_recv()

        def halves(value):
            upper = value.astype(BF16)
            return upper, (value - upper.astype(F32)).astype(BF16)

        within = lax.rem(lane, face) // points
        sub = lax.broadcasted_iota(jnp.int32, (points, LANES), 0)
        own_row = within == sub
        place_ref[...] = jnp.zeros_like(place_ref)
        for q in range(EZL):
            for e in range(0, 3 * EXL, 2):
                blocks = []
                for at in (e, e + 1):
                    row = stress_ref[at // EXL, pl.ds(q * EXL + at % EXL, 1), :]
                    blocks.append(jnp.where(own_row, jnp.broadcast_to(row, (points, LANES)), 0.0))
                upper, lower = halves(jnp.concatenate(blocks, axis=0))
                columns = pl.ds(q * LANES, LANES)
                place_ref[pl.ds(e * points, 2 * points), columns] = upper
                place_ref[pl.ds(LANES + e * points, 2 * points), columns] = lower
        both = lax.dot_general(
            gather_ref[...], place_ref[...], contract, preferred_element_type=F32)
        upper, lower = halves(both[:, :LANES] + both[:, LANES:])
        ladder = jnp.dot(
            zleft_ref[...], jnp.concatenate([upper, lower, upper], axis=0),
            preferred_element_type=F32)
        z_points = EZL * points
        upper, lower = halves(jnp.concatenate(
            [ladder[c * z_points:(c + 1) * z_points] for c in range(reach + 1)], axis=1))
        plane_t = jnp.dot(
            jnp.concatenate([upper, lower, upper], axis=1), xright_ref[...],
            preferred_element_type=F32)
        span = EXL * points
        per = LANES // span
        quarter = lane // span
        rows = []
        for m in range(reach + 1):
            sides = []
            for t in range(EZL // per):
                value = None
                for e in range(per):
                    z_at = (t * per + e) * points
                    piece = roll(
                        plane_t[z_at:z_at + points, (m // per) * LANES:(m // per + 1) * LANES],
                        (e - m % per) * span)
                    value = piece if value is None else jnp.where(quarter == e, piece, value)
                sides.append(value)
            value = jnp.concatenate(sides, axis=1)
            upper = value.astype(BF16).astype(F32)
            value = jnp.concatenate([upper, value - upper], axis=1)
            node = lax.rem(lax.broadcasted_iota(jnp.int32, value.shape, 1), points)
            rows += [jnp.where(node == i, value, 0.0) for i in range(points)]
        plane_ref[...] = jnp.dot(
            jnp.concatenate(rows, axis=0).astype(BF16), spread_ref[...],
            preferred_element_type=F32)
        ended = held[FLOW_STEPS % 2]
        for part in range(2):
            columns = slice(part * LANES, (part + 1) * LANES)
            for i in range(points):
                planes = [
                    plane_ref[pl.ds((m * points + i) * points, points), columns]
                    for m in range(reach + 1)
                ]
                for j in range(points):
                    at = pl.ds(i * face + j * points, points)
                    value = ended[part, at, :]
                    for m in range(reach + 1):
                        value = value + (
                            weights_ref[pl.ds((m * points + j) * points, points), :] * planes[m])
                    out_ref[at, columns] = value

        for offset in range(1, learners):
            remote(count_ref.at[me], count_ref.at[me], count_send.at[offset], count_recv.at[me],
                   {"solver": peer_s(offset)}).wait_send()
            where, copy = part_copy(offset)
            when_owner(where, copy.wait_send)

        def drain_owned():
            at = clamp(me)
            for offset in range(1, groups):
                remote(cross_ref.at[mine], cross_ref.at[mine], cross_send.at[offset],
                       cross_recv.at[mine], {"group": peer_g(offset)}).wait_send()
            for offset in range(1, learners):
                remote(total_ref.at[at], total_ref.at[at], total_send.at[offset],
                       total_recv.at[at], {"solver": peer_s(offset)}).wait_send()

        when_owner(me, drain_owned)
        for copy in stress_copies:
            copy.wait_send()
        for step in range(FLOW_STEPS):
            for copy in copies(step):
                copy.wait_send()

    dma = pltpu.SemaphoreType.DMA
    scratch = [
        pltpu.VMEM((2, 2, nodes, LANES), F32),
        pltpu.VMEM((nodes, nodes), BF16),
        pltpu.VMEM((nodes, nodes), BF16),
        *[pltpu.VMEM(table.shape, table.dtype) for table in tables],
        pltpu.VMEM((pairs, width, 2 * LANES), BF16),
        pltpu.VMEM((pairs, points, 2 * LANES), F32),
        pltpu.VMEM((points * walls + walls, LANES), F32),
        pltpu.VMEM((lane_rows, LANES), F32),
        pltpu.VMEM((lane_rows, LANES), F32),
        pltpu.VMEM((lane_rows, LANES), F32),
        pltpu.VMEM((width, LANES), F32),
        pltpu.VMEM((learners, learners, LANES), F32),
        pltpu.VMEM((owners, rows_sent, owned), F32),
        pltpu.VMEM((learners, rows_sent, owned), F32),
        pltpu.VMEM((groups, rows_sent, owned), F32),
        pltpu.VMEM((owners, rows_sent, owned), F32),
        pltpu.VMEM((3, 2 * lane_rows, LANES), F32),
        pltpu.VMEM((2 * LANES, EZL * LANES), BF16),
        pltpu.VMEM((FLOW_STEPS * face, 2 * LANES), F32),
        pltpu.VMEM((FLOW_STEPS, 2, face // 2, LANES), F32),
        pltpu.VMEM((FLOW_STEPS, 2, face // 2, LANES), F32),
        pltpu.VMEM((FLOW_STEPS, 2, 2, points, LANES), F32),
        pltpu.VMEM((FLOW_STEPS, 2, 2, points, LANES), F32),
        dma((4 + len(tables),)),
        dma((learners,)), dma((learners,)), dma((learners,)), dma((learners,)),
        dma((groups,)), dma((groups,)), dma((learners,)), dma((owners,)),
        dma((len(around),)), dma((len(around),)),
        dma((FLOW_STEPS, 2)), dma((FLOW_STEPS, 2)), dma((FLOW_STEPS, 2)), dma((FLOW_STEPS, 2)),
    ]
    return kernel, scratch


def shards(field, first_weight, second_weight, face_edges, sample_index, route):
    points = field.shape[0]
    elements = field.shape[3]
    nodes = points**3
    width = first_weight.shape[1]
    learners = lax.axis_size("solver")
    groups = lax.axis_size("group")
    deriv, end_weight = gll_tables(points)
    gain = 2.0 / end_weight
    high, low = element_operator(deriv, gain)
    tables = response_tables(deriv, gain)
    kernel, scratch = make_kernel(learners, groups, points, width, deriv, gain, tables)
    vmem = pl.BlockSpec(memory_space=pltpu.VMEM)
    hbm = pl.BlockSpec(memory_space=pltpu.HBM)
    new_field, new_first, new_second = pl.pallas_call(
        kernel,
        out_shape=(
            jax.ShapeDtypeStruct((nodes, elements), F32),
            jax.ShapeDtypeStruct(first_weight.shape, BF16),
            jax.ShapeDtypeStruct((1, width), BF16),
        ),
        in_specs=[hbm] + [vmem] * 5 + [hbm] * (2 + len(tables)),
        out_specs=(vmem, vmem, vmem),
        scratch_shapes=scratch,
        compiler_params=pltpu.CompilerParams(
            collective_id=0, has_side_effects=True, vmem_limit_bytes=67_043_328
        ),
        name="step",
    )(
        field.reshape(nodes, elements),
        first_weight,
        second_weight.reshape(1, width),
        face_edges,
        sample_index.reshape(1, -1),
        route.reshape(1, -1),
        jnp.asarray(high),
        jnp.asarray(low),
        *[jnp.asarray(table) for table in tables],
    )
    return (new_field.reshape(field.shape), new_first, new_second.reshape(second_weight.shape))


def solution(mesh):
    return jax.shard_map(
        shards,
        mesh=mesh,
        in_specs=(
            P(None, None, None, ("solver", "group")),
            P(),
            P(),
            P(),
            P(("solver", "group")),
            P(("solver", "group"), None),
        ),
        out_specs=(P(None, None, None, ("solver", "group")), P(), P()),
        check_vma=False,
    )
```

```python
import math

import jax
import jax.numpy as jnp
import numpy as np
from jax import lax
from jax.experimental import pallas as pl
from jax.experimental.pallas import tpu as pltpu
from jax.sharding import PartitionSpec as P

FLOW_STEPS = 5
EXL = 4
EZL = 8
EY = 8

HIGH = lax.Precision.HIGHEST
TIME_STEP = 0.002
VISCOSITY = 0.01
VELOCITY = 1.0
PENALTY = 1.0
STRESS_SCALE = 0.1
LEARN_RATE = 0.05
LANES = 128
CHUNKS = 4
F32 = jnp.float32
BF16 = jnp.bfloat16


def legendre_table(points_x, points):
    table = np.zeros((points_x.shape[0], points))
    table[:, 0] = 1.0
    table[:, 1] = points_x
    for degree in range(2, points):
        table[:, degree] = (
            (2 * degree - 1) * points_x * table[:, degree - 1] - (degree - 1) * table[:, degree - 2]
        ) / degree
    return table


def gll_tables(points):
    order = points - 1
    guess = np.cos(np.pi * np.arange(points) / order)
    for sweep in range(100):
        table = legendre_table(guess, points)
        guess = guess - (guess * table[:, order] - table[:, order - 1]) / (points * table[:, order])
    nodes = guess[::-1]
    values = legendre_table(nodes, points)[:, order]
    matrix = np.zeros((points, points))
    for row in range(points):
        for column in range(points):
            if row != column:
                matrix[row, column] = values[row] / (values[column] * (nodes[row] - nodes[column]))
    matrix[0, 0] = -order * (order + 1) / 4.0
    matrix[order, order] = order * (order + 1) / 4.0
    return matrix.astype(np.float32), 2.0 / (order * (order + 1))


def element_operator(deriv, gain):
    points = deriv.shape[0]
    last = points - 1
    deriv = deriv.astype(np.float64)
    second = 4.0 * VISCOSITY * (deriv @ deriv)
    along_i = -2.0 * VELOCITY * deriv + second
    along_i[0, 0] -= gain * (VELOCITY + PENALTY)
    along_i[last, last] -= gain * PENALTY
    other = second.copy()
    other[0, 0] -= gain * PENALTY
    other[last, last] -= gain * PENALTY
    eye = np.eye(points)
    whole = (
        np.kron(np.kron(along_i, eye), eye)
        + np.kron(np.kron(eye, other), eye)
        + np.kron(np.kron(eye, eye), other)
    )
    whole = (TIME_STEP * whole).astype(np.float32)
    high = whole.astype(jnp.bfloat16)
    low = (whole - high.astype(np.float32)).astype(jnp.bfloat16)
    return high, low


def split_np(value):
    value = value.astype(np.float32)
    high = value.astype(jnp.bfloat16)
    return high, (value - high.astype(np.float32)).astype(jnp.bfloat16)


def chain(local, from_before, from_after, count):
    points = local.shape[0]
    whole = np.kron(np.eye(count), local)
    for e in range(1, count):
        whole[e * points, e * points - 1] += from_before
        whole[e * points - 1, e * points] += from_after
    return whole


def response_tables(deriv, gain):
    points = deriv.shape[0]
    last = points - 1
    reach = FLOW_STEPS - 1
    deriv = deriv.astype(np.float64)
    second = TIME_STEP * 4.0 * VISCOSITY * (deriv @ deriv)
    one = TIME_STEP * gain * PENALTY
    two = TIME_STEP * gain * (VELOCITY + PENALTY)
    x_local = -TIME_STEP * 2.0 * VELOCITY * deriv + second
    x_local[0, 0] -= two
    x_local[last, last] -= one
    z_local = second.copy()
    z_local[0, 0] -= one
    z_local[last, last] -= one
    x_whole = chain(x_local, two, one, 3 * EXL)
    z_whole = np.eye(2 * EZL * points) + chain(z_local, one, one, 2 * EZL)
    y_whole = chain(z_local, one, one, EY)
    y_whole[0, 0] += one
    wide = LANES
    x_points = EXL * points
    z_points = EZL * points
    x_middle = slice(x_points, 2 * x_points)
    z_middle = slice(z_points // 2, z_points // 2 + z_points)
    z_left = np.concatenate(
        [np.linalg.matrix_power(z_whole, c)[z_middle] for c in range(reach + 1)], axis=0)
    x_right = np.zeros((reach + 1, wide, 2 * LANES))
    for m in range(reach + 1):
        for c in range(m + 1):
            power = np.linalg.matrix_power(x_whole, m - c)[x_middle]
            x_right[c, :3 * x_points, m * x_points:(m + 1) * x_points] = (
                math.comb(m, m - c) * power.T)
    x_right = x_right.reshape((reach + 1) * wide, 2 * LANES)
    first = np.zeros(EY * points)
    first[0] = one
    weights = np.zeros((reach + 1, EY * points))
    for m in range(reach + 1):
        value = first.copy()
        for b in range(reach - m + 1):
            weights[m] += math.comb(m + b, b) * value
            value = y_whole @ value
    weights = weights.reshape(reach + 1, EY, points).transpose(0, 2, 1)
    weights = np.tile(weights, (1, 1, LANES // EY))
    weights = np.repeat(weights.reshape(-1, 1, LANES), points, axis=1).reshape(-1, LANES)
    z_high, z_low = split_np(z_left)
    x_high, x_low = split_np(x_right)
    ez, k = np.divmod(np.arange(2 * EZL * points), points)
    q, rest = np.divmod(np.arange(EZL * 2 * points * points), 2 * points * points)
    h, rest = np.divmod(rest, points * points)
    gather = (ez[:, None] == (2 * q + h)[None]) & (k[:, None] == (rest % points)[None])
    row_z, rest = np.divmod(np.arange(EZL * EXL * points), EXL * points)
    row_x = rest // points
    col_x, rest = np.divmod(np.arange(EXL * EZL * EY), EZL * EY)
    col_z = rest // EY
    spread = (row_z[:, None] == col_z[None]) & (row_x[:, None] == col_x[None])
    return (
        gather.astype(jnp.bfloat16),
        np.concatenate([z_high, z_high, z_low], axis=1),
        np.concatenate([x_high, x_high, x_low], axis=0),
        np.concatenate([spread, spread], axis=0).astype(jnp.bfloat16),
        weights.astype(np.float32),
    )


def make_kernel(learners, groups, points, width, deriv, gain, tables):
    face = points * points
    last = points - 1
    nodes = face * points
    walls = EXL * EZL
    elements = walls * EY
    pairs = walls * face // (2 * LANES)
    owners = min(learners, width // LANES)
    owned = width // owners
    devices = learners * groups
    block = EZL * EY
    half = LANES // 2
    step_gain = float(TIME_STEP * gain * PENALTY)
    step_gain_x = float(TIME_STEP * gain * (VELOCITY + PENALTY))
    first_row = [float(value) for value in deriv[0]]

    def roll(value, shift):
        shift = shift % LANES
        return value if shift == 0 else pltpu.roll(value, shift, 1)

    rows_sent = points + 1
    reach = FLOW_STEPS - 1
    around = [(dx, dz) for dx in (0, 1, -1) for dz in (0, 1, -1) if dx or dz]
    lane_rows = walls * face // LANES

    def kernel(
        field_ref, first_ref, second_ref, edges_ref, index_ref, route_ref, high_hbm, low_hbm,
        gather_hbm, zleft_hbm, xright_hbm, spread_hbm, weights_hbm,
        out_ref, new_first_ref, new_second_ref,
        u_ref, high_ref, low_ref, gather_ref, zleft_ref, xright_ref, spread_ref, weights_ref,
        result_ref, mask_ref, mixed_ref, feat_ref, turn_ref, z_ref, g_ref, e_ref, w2_ref,
        count_ref, tile_ref, part_ref, cross_ref, total_ref, stress_ref, place_ref, plane_ref,
        xs_ref, xr_ref, zs_ref, zr_ref,
        load_sem, out_sem, count_send, count_recv, part_send, part_recv, cross_send, cross_recv,
        total_send, total_recv, stress_send, stress_recv, xs_send, xr_recv, zs_send, zr_recv,
    ):
        me = lax.axis_index("solver")
        mine = lax.axis_index("group")

        def peer_s(offset):
            return lax.rem(me + offset, learners)

        def peer_g(offset):
            return lax.rem(mine + offset, groups)

        loads = [
            pltpu.make_async_copy(
                field_ref.at[:, pl.ds(part * LANES, LANES)], u_ref.at[0, part], load_sem.at[part])
            for part in range(2)
        ]
        loads.append(pltpu.make_async_copy(high_hbm, high_ref, load_sem.at[2]))
        loads.append(pltpu.make_async_copy(low_hbm, low_ref, load_sem.at[3]))
        for at, (table, held_table) in enumerate((
            (gather_hbm, gather_ref), (zleft_hbm, zleft_ref), (xright_hbm, xright_ref),
            (spread_hbm, spread_ref), (weights_hbm, weights_ref),
        )):
            loads.append(pltpu.make_async_copy(table, held_table, load_sem.at[4 + at]))
        for load in loads:
            load.start()

        barrier = pltpu.get_barrier_semaphore()
        for offset in range(1, learners):
            pl.semaphore_signal(
                barrier, inc=1, device_id={"solver": peer_s(offset)},
                device_id_type=pl.DeviceIdType.MESH,
            )
        for offset in range(1, groups):
            pl.semaphore_signal(
                barrier, inc=1, device_id={"group": peer_g(offset)},
                device_id_type=pl.DeviceIdType.MESH,
            )
        for dx, dz in around:
            if dx and dz:
                pl.semaphore_signal(
                    barrier, inc=1,
                    device_id={"solver": peer_s(dx % learners), "group": peer_g(dz % groups)},
                    device_id_type=pl.DeviceIdType.MESH,
                )

        def remote(source, target, send, recv, where):
            return pltpu.make_async_remote_copy(
                src_ref=source, dst_ref=target, send_sem=send, recv_sem=recv,
                device_id=where, device_id_type=pl.DeviceIdType.MESH,
            )

        lane = lax.broadcasted_iota(jnp.int32, (1, LANES), 1)
        low_half = lane < half
        slot = lax.rem(lane, block) // EY
        level = lax.rem(lane, EY)
        contract = (((1,), (1,)), ((), ()))

        learner_rows = lax.broadcasted_iota(jnp.int32, (learners, route_ref.shape[1]), 0)
        hits = (route_ref[...] == learner_rows).astype(F32)
        count_ref[me] = jnp.broadcast_to(jnp.sum(hits, axis=1, keepdims=True), (learners, LANES))

        big = 2 * LANES
        edge_rows = lax.rem(
            lax.broadcasted_iota(jnp.int32, (big, edges_ref.shape[1]), 0), face)
        source = (edges_ref[0:1, :] == edge_rows).astype(F32).astype(BF16)
        sink = (edges_ref[1:2, :] == edge_rows).astype(F32).astype(BF16)
        node_rows = lax.broadcasted_iota(jnp.int32, (big, big), 0)
        node_cols = lax.broadcasted_iota(jnp.int32, (big, big), 1)
        graph = 0.25 * lax.dot_general(source, sink, contract, preferred_element_type=F32)
        graph = jnp.where(node_rows // face == node_cols // face, graph, 0.0)
        graph = graph + (node_rows == node_cols).astype(F32)
        small = graph[:LANES, :LANES]
        graph = graph.astype(BF16)
        first = first_ref[...].astype(F32)
        second = second_ref[...].astype(F32)

        def copies(step):
            right, left = {"solver": peer_s(1)}, {"solver": peer_s(learners - 1)}
            up, down = {"group": peer_g(1)}, {"group": peer_g(groups - 1)}
            result = []
            for side, where in ((0, right), (1, left)):
                result.append(remote(
                    xs_ref.at[step, side], xr_ref.at[step, side],
                    xs_send.at[step, side], xr_recv.at[step, side], where))
            for side, where in ((0, up), (1, down)):
                result.append(remote(
                    zs_ref.at[step, side], zr_ref.at[step, side],
                    zs_send.at[step, side], zr_recv.at[step, side], where))
            return result

        half_face = face // 2

        def near(i):
            return pl.ds(i * face, points, stride=points)

        def far(i):
            return pl.ds(i * face + last, points, stride=points)

        def send_z(step, bottoms, tops):
            for part in range(2):
                high_pack = jnp.zeros((points, LANES), F32)
                low_pack = jnp.zeros((points, LANES), F32)
                for i in range(points):
                    high_pack = jnp.where(slot == i, roll(tops[part][i], EY * (i + 1)), high_pack)
                    low_pack = jnp.where(slot == i, roll(bottoms[part][i], EY * i), low_pack)
                zs_ref[step, 0, part] = high_pack
                zs_ref[step, 1, part] = low_pack
            every = copies(step)
            every[2].start()
            every[3].start()

        def send_x(step, u):
            upper = u[1, pl.ds(nodes - face, face), :]
            xs_ref[step, 0] = jnp.where(low_half, roll(upper[:half_face], half), upper[half_face:])
            lower = u[0, pl.ds(0, face), :]
            xs_ref[step, 1] = jnp.where(low_half, lower[:half_face], roll(lower[half_face:], half))
            every = copies(step)
            every[0].start()
            every[1].start()

        def send_faces(step, u):
            send_z(step, [[u[part, near(i), :] for i in range(points)] for part in range(2)],
                   [[u[part, far(i), :] for i in range(points)] for part in range(2)])
            send_x(step, u)

        start = u_ref.at[0]
        for load in loads[:2]:
            load.wait()

        def face_rows(value_of):
            rows = jnp.concatenate([value_of(i) for i in range(points)], axis=0)
            return jnp.concatenate([rows, rows], axis=0).astype(BF16)

        def plane(i, j):
            at = pl.ds(i * face + j * points, points)
            return jnp.concatenate([start[0, at, :], start[1, at, :]], axis=1)

        def slope(i):
            total = None
            for j in range(points):
                term = first_row[j] * plane(i, j)
                total = term if total is None else total + term
            return STRESS_SCALE * total

        wall_rows = lax.broadcasted_iota(jnp.int32, (walls, elements), 0)
        wall_cols = lax.broadcasted_iota(jnp.int32, (walls, elements), 1)
        wall_at = (
            lax.rem(wall_rows // 2, EXL) * EZL + wall_rows // (2 * EXL) * 2 + lax.rem(wall_rows, 2))
        select = (wall_cols == wall_at * EY).astype(F32).astype(BF16)
        for j in range(points):
            turn_ref[pl.ds(j * walls, walls), :] = lax.dot_general(
                select, face_rows(lambda i: plane(i, j)), contract, preferred_element_type=F32)
        turn_ref[pl.ds(points * walls, walls), :] = lax.dot_general(
            select, face_rows(slope), contract, preferred_element_type=F32)
        for row in range(lane_rows):
            even = turn_ref[pl.ds(2 * row, points, stride=walls), :]
            odd = turn_ref[pl.ds(2 * row + 1, points, stride=walls), :]
            feat_ref[row // 2, :, pl.ds((row % 2) * LANES, LANES)] = jnp.where(low_half, even, odd)
        target = jnp.where(
            low_half,
            turn_ref[pl.ds(points * walls, lane_rows, stride=2), :],
            turn_ref[pl.ds(points * walls + 1, lane_rows, stride=2), :],
        )

        pl.semaphore_wait(barrier, learners + groups + 2)
        for offset in range(1, learners):
            remote(count_ref.at[me], count_ref.at[me], count_send.at[offset], count_recv.at[me],
                   {"solver": peer_s(offset)}).start()
        send_faces(0, start)

        def network(first, second, learn):
            turned = jnp.transpose(first).astype(BF16)
            w2_ref[...] = jnp.transpose(jnp.broadcast_to(second, (LANES, width)))

            def one(pair, carry):
                before = jnp.dot(turned, feat_ref[pair].astype(BF16), preferred_element_type=F32)
                hidden = jnp.maximum(before, 0.0)
                if learn:
                    mask_ref[pair] = jnp.where(before > 0.0, 1.0, 0.0).astype(BF16)
                    mixed = jnp.dot(
                        hidden.astype(BF16), graph, preferred_element_type=F32).astype(BF16)
                    mixed_ref[pair] = mixed
                    hidden = mixed.astype(F32)
                weight = w2_ref[...]
                z_ref[pl.ds(2 * pair, 1), :] = jnp.sum(
                    hidden[:, :LANES] * weight, axis=0, keepdims=True)
                z_ref[pl.ds(2 * pair + 1, 1), :] = jnp.sum(
                    hidden[:, LANES:] * weight, axis=0, keepdims=True)
                return carry

            lax.fori_loop(0, pairs, one, 0, unroll=pairs)
            return z_ref[...]

        output = network(first, second, True)

        for offset in range(1, learners):
            origin = peer_s(offset)
            remote(count_ref.at[me], count_ref.at[origin], count_send.at[offset],
                   count_recv.at[origin], {"solver": origin}).wait_recv()
        counts = count_ref[0]
        for other in range(1, learners):
            counts = counts + count_ref[other]
        inverse = 1.0 / (jnp.maximum(counts, 1.0) * devices)
        places = 2 * lax.broadcasted_iota(jnp.int32, (lane_rows, index_ref.shape[1]), 0)
        taken = index_ref[...]
        taken = 2 * (lax.rem(taken, EZL) // 2 * EXL + taken // EZL) + lax.rem(taken, 2)
        chosen = (taken == places).astype(F32)
        even = lax.dot_general(chosen, hits, contract, preferred_element_type=F32)
        chosen = (taken == places + 1).astype(F32)
        odd = lax.dot_general(chosen, hits, contract, preferred_element_type=F32)
        difference = output - target
        error = jnp.zeros((lane_rows, LANES), F32)
        for learner in range(learners):
            times = jnp.where(low_half, even[:, learner:learner + 1], odd[:, learner:learner + 1])
            single = (difference * inverse[learner:learner + 1]).astype(BF16).astype(F32)
            error = error + times * single
        e_ref[...] = error
        g_ref[...] = lax.dot_general(
            error, small, contract, precision=HIGH, preferred_element_type=F32)

        def split(value):
            upper = value.astype(BF16).astype(F32)
            return jnp.concatenate([upper, value - upper], axis=0).astype(BF16)

        def row_pair(ref, pair):
            return jnp.concatenate([ref[pl.ds(2 * pair, 1), :], ref[pl.ds(2 * pair + 1, 1), :]], axis=1)

        moment = None
        for pair in range(pairs):
            term = lax.dot_general(
                split(feat_ref[pair] * row_pair(g_ref, pair)), mask_ref[pair], contract,
                preferred_element_type=F32)
            moment = term if moment is None else moment + term
        moment = moment[0:points] + moment[points:2 * points]
        error_rows = [
            jnp.broadcast_to(e_ref[pl.ds(row, 1), :], (16, LANES)) for row in range(lane_rows)
        ]
        for t in range(owners):
            blocks = []
            for at in range(t * owned, (t + 1) * owned, 16):
                total = None
                for row in range(lane_rows):
                    mixed = mixed_ref[
                        row // 2, pl.ds(at, 16), pl.ds(row % 2 * LANES, LANES)].astype(F32)
                    total = mixed * error_rows[row] if total is None else (
                        total + mixed * error_rows[row])
                blocks.append(total)
            turned = jnp.transpose(jnp.concatenate(blocks, axis=0))
            tile_ref[t, pl.ds(points, 1), :] = jnp.sum(turned, axis=0, keepdims=True)
            tile_ref[t, pl.ds(0, points), :] = moment[:, t * owned:(t + 1) * owned]

        def when_owner(which, action):
            if owners == learners:
                action()
            else:
                pl.when(which < owners)(action)

        def clamp(which):
            return which if owners == learners else jnp.minimum(which, owners - 1)

        def part_copy(offset):
            where = peer_s(offset)
            return where, remote(tile_ref.at[clamp(where)], part_ref.at[me], part_send.at[offset],
                                 part_recv.at[me], {"solver": where})

        for offset in range(1, learners):
            where, copy = part_copy(offset)
            when_owner(where, copy.start)

        def local(source, target):
            u = jnp.concatenate([source[0], source[1]], axis=1)
            upper = u.astype(BF16)
            lower = (u - upper.astype(F32)).astype(BF16)
            u = u + (
                jnp.dot(high_ref[...], upper, preferred_element_type=F32)
                + jnp.dot(high_ref[...], lower, preferred_element_type=F32)
                + jnp.dot(low_ref[...], upper, preferred_element_type=F32)
            )
            for part in range(2):
                target[part] = u[:, part * LANES:(part + 1) * LANES]
            for part in range(2):
                for i in range(points):
                    base = i * face
                    bottom = source[part, pl.ds(base, points), :]
                    top = source[part, pl.ds(base + face - points, points), :]
                    below = jnp.where(level == 0, bottom, roll(top, 1))
                    above = jnp.where(level == EY - 1, 0.0, roll(bottom, -1))
                    target[part, pl.ds(base, points), :] += step_gain * below
                    target[part, pl.ds(base + face - points, points), :] += step_gain * above
            low0 = roll(source[0, pl.ds(nodes - face, face), :], half)
            low1 = roll(source[1, pl.ds(nodes - face, face), :], half)
            target[0, pl.ds(0, face), :] += step_gain_x * jnp.where(low_half, 0.0, low0)
            target[1, pl.ds(0, face), :] += step_gain_x * jnp.where(low_half, low0, low1)
            high0 = roll(source[0, pl.ds(0, face), :], half)
            high1 = roll(source[1, pl.ds(0, face), :], half)
            target[0, pl.ds(nodes - face, face), :] += step_gain * jnp.where(low_half, high0, high1)
            target[1, pl.ds(nodes - face, face), :] += step_gain * jnp.where(low_half, high1, 0.0)
            for part in range(2):
                for i in range(points):
                    before = jnp.where(slot == 0, 0.0, roll(source[part, far(i), :], EY))
                    after = jnp.where(slot == EZL - 1, 0.0, roll(source[part, near(i), :], -EY))
                    target[part, near(i), :] = target[part, near(i), :] + step_gain * before
                    target[part, far(i), :] = target[part, far(i), :] + step_gain * after

        def halo(step, target, send):
            every = copies(step)
            every[0].wait_recv()
            every[1].wait_recv()
            ghost = xr_ref[step, 0]
            ghost = jnp.concatenate([ghost, roll(ghost, half)], axis=0)
            target[0, pl.ds(0, face), :] += step_gain_x * jnp.where(low_half, ghost, 0.0)
            ghost = xr_ref[step, 1]
            ghost = jnp.concatenate([roll(ghost, half), ghost], axis=0)
            target[1, pl.ds(nodes - face, face), :] += step_gain * jnp.where(low_half, 0.0, ghost)
            every[2].wait_recv()
            every[3].wait_recv()
            bottoms, tops = [], []
            for part in range(2):
                before_pack = step_gain * zr_ref[step, 0, part]
                after_pack = step_gain * zr_ref[step, 1, part]
                for i in range(points):
                    before = jnp.where(slot == 0, roll(before_pack, half - EY * i), 0.0)
                    after = jnp.where(
                        slot == EZL - 1, roll(after_pack, EY * (EZL - 1 - i)), 0.0)
                    bottoms.append(target[part, near(i), :] + before)
                    tops.append(target[part, far(i), :] + after)
                    target[part, near(i), :] = bottoms[-1]
                    target[part, far(i), :] = tops[-1]
            if send:
                send_z(step + 1, [bottoms[:points], bottoms[points:]], [tops[:points], tops[points:]])
                send_x(step + 1, target)

        for load in loads[2:]:
            load.wait()
        held = [start, u_ref.at[1]]

        def flow(step):
            source, target = held[step % 2], held[(step + 1) % 2]
            local(source, target)
            halo(step, target, step < FLOW_STEPS - 1)

        flow(0)

        def reduce_part():
            total = tile_ref[clamp(me)]
            for offset in range(1, learners):
                origin = peer_s(offset)
                remote(tile_ref.at[0], part_ref.at[origin], part_send.at[offset],
                       part_recv.at[origin], {"solver": origin}).wait_recv()
            for offset in range(1, learners):
                total = total + part_ref[peer_s(offset)]
            cross_ref[mine] = total
            for offset in range(1, groups):
                remote(cross_ref.at[mine], cross_ref.at[mine], cross_send.at[offset],
                       cross_recv.at[mine], {"group": peer_g(offset)}).start()

        def reduce_cross():
            for offset in range(1, groups):
                origin = peer_g(offset)
                remote(cross_ref.at[mine], cross_ref.at[origin], cross_send.at[offset],
                       cross_recv.at[origin], {"group": origin}).wait_recv()
            total = cross_ref[0]
            for origin in range(1, groups):
                total = total + cross_ref[origin]
            at = clamp(me)
            total_ref[at] = total
            for offset in range(1, learners):
                remote(total_ref.at[at], total_ref.at[at], total_send.at[offset],
                       total_recv.at[at], {"solver": peer_s(offset)}).start()

        when_owner(me, reduce_part)
        flow(1)
        when_owner(me, reduce_cross)
        flow(2)
        for offset in range(1, learners):
            origin = peer_s(offset)
            at = clamp(origin)
            copy = remote(total_ref.at[at], total_ref.at[at], total_send.at[offset],
                          total_recv.at[at], {"solver": origin})
            when_owner(origin, copy.wait_recv)

        sums = jnp.concatenate([total_ref[t] for t in range(owners)], axis=1)
        new_first = (first - LEARN_RATE * (sums[0:points] * second)).astype(BF16)
        new_second = (second - LEARN_RATE * sums[points:points + 1]).astype(BF16)
        new_first_ref[...] = new_first
        new_second_ref[...] = new_second

        middle = pl.ds(lane_rows // 2, lane_rows)
        plain = network(new_first.astype(F32), new_second.astype(F32), False)
        stress_ref[1, middle, :] = jnp.dot(
            plain, small, precision=HIGH, preferred_element_type=F32)
        stress_copies = []
        for way, (dx, dz) in enumerate(around):
            rows = {
                0: (middle, middle),
                1: (pl.ds(lane_rows, lane_rows // 2), pl.ds(0, lane_rows // 2)),
                -1: (pl.ds(lane_rows // 2, lane_rows // 2), pl.ds(3 * lane_rows // 2, lane_rows // 2)),
            }[dz]
            stress_copies.append(remote(
                stress_ref.at[1, rows[0]], stress_ref.at[1 - dx, rows[1]],
                stress_send.at[way], stress_recv.at[way],
                {"solver": peer_s(dx % learners), "group": peer_g(dz % groups)}))
        for copy in stress_copies:
            copy.start()
        for step in range(3, FLOW_STEPS):
            flow(step)
        for copy in stress_copies:
            copy.wait_recv()

        def halves(value):
            upper = value.astype(BF16)
            return upper, (value - upper.astype(F32)).astype(BF16)

        within = lax.rem(lane, face) // points
        sub = lax.broadcasted_iota(jnp.int32, (points, LANES), 0)
        own_row = within == sub
        place_ref[...] = jnp.zeros_like(place_ref)
        for q in range(EZL):
            for e in range(0, 3 * EXL, 2):
                blocks = []
                for at in (e, e + 1):
                    row = stress_ref[at // EXL, pl.ds(q * EXL + at % EXL, 1), :]
                    blocks.append(jnp.where(own_row, jnp.broadcast_to(row, (points, LANES)), 0.0))
                upper, lower = halves(jnp.concatenate(blocks, axis=0))
                columns = pl.ds(q * LANES, LANES)
                place_ref[pl.ds(e * points, 2 * points), columns] = upper
                place_ref[pl.ds(LANES + e * points, 2 * points), columns] = lower
        both = lax.dot_general(
            gather_ref[...], place_ref[...], contract, preferred_element_type=F32)
        upper, lower = halves(both[:, :LANES] + both[:, LANES:])
        ladder = jnp.dot(
            zleft_ref[...], jnp.concatenate([upper, lower, upper], axis=0),
            preferred_element_type=F32)
        z_points = EZL * points
        upper, lower = halves(jnp.concatenate(
            [ladder[c * z_points:(c + 1) * z_points] for c in range(reach + 1)], axis=1))
        plane_t = jnp.dot(
            jnp.concatenate([upper, lower, upper], axis=1), xright_ref[...],
            preferred_element_type=F32)
        span = EXL * points
        per = LANES // span
        quarter = lane // span
        rows = []
        for m in range(reach + 1):
            sides = []
            for t in range(EZL // per):
                value = None
                for e in range(per):
                    z_at = (t * per + e) * points
                    piece = roll(
                        plane_t[z_at:z_at + points, (m // per) * LANES:(m // per + 1) * LANES],
                        (e - m % per) * span)
                    value = piece if value is None else jnp.where(quarter == e, piece, value)
                sides.append(value)
            value = jnp.concatenate(sides, axis=1)
            upper = value.astype(BF16).astype(F32)
            value = jnp.concatenate([upper, value - upper], axis=1)
            node = lax.rem(lax.broadcasted_iota(jnp.int32, value.shape, 1), points)
            rows += [jnp.where(node == i, value, 0.0) for i in range(points)]
        plane_ref[...] = jnp.dot(
            jnp.concatenate(rows, axis=0).astype(BF16), spread_ref[...],
            preferred_element_type=F32)
        ended = held[FLOW_STEPS % 2]
        results = []
        for i in range(points):
            for part in range(2):
                columns = slice(part * LANES, (part + 1) * LANES)
                planes = [
                    plane_ref[pl.ds((m * points + i) * points, points), columns]
                    for m in range(reach + 1)
                ]
                for j in range(points):
                    at = pl.ds(i * face + j * points, points)
                    value = ended[part, at, :]
                    for m in range(reach + 1):
                        value = value + (
                            weights_ref[pl.ds((m * points + j) * points, points), :] * planes[m])
                    result_ref[at, columns] = value
            if i % 2:
                rows = pl.ds((i - 1) * face, 2 * face)
                results.append(pltpu.make_async_copy(
                    result_ref.at[rows], out_ref.at[rows], out_sem.at[i // 2]))
                results[-1].start()

        for offset in range(1, learners):
            remote(count_ref.at[me], count_ref.at[me], count_send.at[offset], count_recv.at[me],
                   {"solver": peer_s(offset)}).wait_send()
            where, copy = part_copy(offset)
            when_owner(where, copy.wait_send)

        def drain_owned():
            at = clamp(me)
            for offset in range(1, groups):
                remote(cross_ref.at[mine], cross_ref.at[mine], cross_send.at[offset],
                       cross_recv.at[mine], {"group": peer_g(offset)}).wait_send()
            for offset in range(1, learners):
                remote(total_ref.at[at], total_ref.at[at], total_send.at[offset],
                       total_recv.at[at], {"solver": peer_s(offset)}).wait_send()

        when_owner(me, drain_owned)
        for copy in results:
            copy.wait()
        for copy in stress_copies:
            copy.wait_send()
        for step in range(FLOW_STEPS):
            for copy in copies(step):
                copy.wait_send()

    dma = pltpu.SemaphoreType.DMA
    scratch = [
        pltpu.VMEM((2, 2, nodes, LANES), F32),
        pltpu.VMEM((nodes, nodes), BF16),
        pltpu.VMEM((nodes, nodes), BF16),
        *[pltpu.VMEM(table.shape, table.dtype) for table in tables],
        pltpu.VMEM((nodes, elements), F32),
        pltpu.VMEM((pairs, width, 2 * LANES), BF16),
        pltpu.VMEM((pairs, width, 2 * LANES), BF16),
        pltpu.VMEM((pairs, points, 2 * LANES), F32),
        pltpu.VMEM((points * walls + walls, LANES), F32),
        pltpu.VMEM((lane_rows, LANES), F32),
        pltpu.VMEM((lane_rows, LANES), F32),
        pltpu.VMEM((lane_rows, LANES), F32),
        pltpu.VMEM((width, LANES), F32),
        pltpu.VMEM((learners, learners, LANES), F32),
        pltpu.VMEM((owners, rows_sent, owned), F32),
        pltpu.VMEM((learners, rows_sent, owned), F32),
        pltpu.VMEM((groups, rows_sent, owned), F32),
        pltpu.VMEM((owners, rows_sent, owned), F32),
        pltpu.VMEM((3, 2 * lane_rows, LANES), F32),
        pltpu.VMEM((2 * LANES, EZL * LANES), BF16),
        pltpu.VMEM((FLOW_STEPS * face, 2 * LANES), F32),
        pltpu.VMEM((FLOW_STEPS, 2, face // 2, LANES), F32),
        pltpu.VMEM((FLOW_STEPS, 2, face // 2, LANES), F32),
        pltpu.VMEM((FLOW_STEPS, 2, 2, points, LANES), F32),
        pltpu.VMEM((FLOW_STEPS, 2, 2, points, LANES), F32),
        dma((4 + len(tables),)), dma((points // 2,)),
        dma((learners,)), dma((learners,)), dma((learners,)), dma((learners,)),
        dma((groups,)), dma((groups,)), dma((learners,)), dma((owners,)),
        dma((len(around),)), dma((len(around),)),
        dma((FLOW_STEPS, 2)), dma((FLOW_STEPS, 2)), dma((FLOW_STEPS, 2)), dma((FLOW_STEPS, 2)),
    ]
    return kernel, scratch


def finish(
    field_ref, first_ref, second_ref, out_ref, new_first_ref, new_second_ref,
    held_ref, held_first_ref, held_second_ref, in_sem, out_sem
):
    size = field_ref.shape[0] // CHUNKS
    ways = [(first_ref, held_first_ref, new_first_ref), (second_ref, held_second_ref, new_second_ref)]
    for chunk in range(CHUNKS):
        rows = pl.ds(chunk * size, size)
        ways.append((field_ref.at[rows], held_ref.at[rows], out_ref.at[rows]))
    loads = [
        pltpu.make_async_copy(way[0], way[1], in_sem.at[at]) for at, way in enumerate(ways)
    ]
    stores = [
        pltpu.make_async_copy(way[1], way[2], out_sem.at[at]) for at, way in enumerate(ways)
    ]
    for copy in loads:
        copy.start()
    for load, store in zip(loads, stores):
        load.wait()
        store.start()
    for copy in stores:
        copy.wait()


def shards(field, first_weight, second_weight, face_edges, sample_index, route):
    points = field.shape[0]
    elements = field.shape[3]
    nodes = points**3
    width = first_weight.shape[1]
    learners = lax.axis_size("solver")
    groups = lax.axis_size("group")
    deriv, end_weight = gll_tables(points)
    gain = 2.0 / end_weight
    high, low = element_operator(deriv, gain)
    tables = response_tables(deriv, gain)
    kernel, scratch = make_kernel(learners, groups, points, width, deriv, gain, tables)
    vmem = pl.BlockSpec(memory_space=pltpu.VMEM)
    hbm = pl.BlockSpec(memory_space=pltpu.HBM)
    new_field, new_first, new_second = pl.pallas_call(
        kernel,
        out_shape=(
            jax.ShapeDtypeStruct((nodes, elements), F32),
            jax.ShapeDtypeStruct(first_weight.shape, BF16),
            jax.ShapeDtypeStruct((1, width), BF16),
        ),
        in_specs=[hbm] + [vmem] * 5 + [hbm] * (2 + len(tables)),
        out_specs=(hbm, vmem, vmem),
        scratch_shapes=scratch,
        compiler_params=pltpu.CompilerParams(
            collective_id=0, has_side_effects=True, vmem_limit_bytes=67_043_328
        ),
        name="step",
    )(
        field.reshape(nodes, elements),
        first_weight,
        second_weight.reshape(1, width),
        face_edges,
        sample_index.reshape(1, -1),
        route.reshape(1, -1),
        jnp.asarray(high),
        jnp.asarray(low),
        *[jnp.asarray(table) for table in tables],
    )
    new_field, new_first, new_second = pl.pallas_call(
        finish,
        out_shape=tuple(
            jax.ShapeDtypeStruct(value.shape, value.dtype)
            for value in (new_field, new_first, new_second)),
        in_specs=[hbm, hbm, hbm],
        out_specs=(hbm, hbm, hbm),
        scratch_shapes=[
            pltpu.VMEM((nodes, elements), F32),
            pltpu.VMEM(new_first.shape, BF16),
            pltpu.VMEM(new_second.shape, BF16),
            pltpu.SemaphoreType.DMA((CHUNKS + 2,)),
            pltpu.SemaphoreType.DMA((CHUNKS + 2,)),
        ],
        compiler_params=pltpu.CompilerParams(vmem_limit_bytes=67_043_328),
        name="finish",
    )(new_field, new_first, new_second)
    return (new_field.reshape(field.shape), new_first, new_second.reshape(second_weight.shape))


def solution(mesh):
    return jax.shard_map(
        shards,
        mesh=mesh,
        in_specs=(
            P(None, None, None, ("solver", "group")),
            P(),
            P(),
            P(),
            P(("solver", "group")),
            P(("solver", "group"), None),
        ),
        out_specs=(P(None, None, None, ("solver", "group")), P(), P()),
        check_vma=False,
    )
```

```python
import math

import jax
import jax.numpy as jnp
import numpy as np
from jax import lax
from jax.experimental import pallas as pl
from jax.experimental.pallas import tpu as pltpu
from jax.sharding import PartitionSpec as P

FLOW_STEPS = 5
EXL = 4
EZL = 8
EY = 8

HIGH = lax.Precision.HIGHEST
TIME_STEP = 0.002
VISCOSITY = 0.01
VELOCITY = 1.0
PENALTY = 1.0
STRESS_SCALE = 0.1
LEARN_RATE = 0.05
LANES = 128
CHUNKS = 4
F32 = jnp.float32
BF16 = jnp.bfloat16


def legendre_table(points_x, points):
    table = np.zeros((points_x.shape[0], points))
    table[:, 0] = 1.0
    table[:, 1] = points_x
    for degree in range(2, points):
        table[:, degree] = (
            (2 * degree - 1) * points_x * table[:, degree - 1] - (degree - 1) * table[:, degree - 2]
        ) / degree
    return table


def gll_tables(points):
    order = points - 1
    guess = np.cos(np.pi * np.arange(points) / order)
    for sweep in range(100):
        table = legendre_table(guess, points)
        guess = guess - (guess * table[:, order] - table[:, order - 1]) / (points * table[:, order])
    nodes = guess[::-1]
    values = legendre_table(nodes, points)[:, order]
    matrix = np.zeros((points, points))
    for row in range(points):
        for column in range(points):
            if row != column:
                matrix[row, column] = values[row] / (values[column] * (nodes[row] - nodes[column]))
    matrix[0, 0] = -order * (order + 1) / 4.0
    matrix[order, order] = order * (order + 1) / 4.0
    return matrix.astype(np.float32), 2.0 / (order * (order + 1))


def element_operator(deriv, gain):
    points = deriv.shape[0]
    last = points - 1
    deriv = deriv.astype(np.float64)
    second = 4.0 * VISCOSITY * (deriv @ deriv)
    along_i = -2.0 * VELOCITY * deriv + second
    along_i[0, 0] -= gain * (VELOCITY + PENALTY)
    along_i[last, last] -= gain * PENALTY
    other = second.copy()
    other[0, 0] -= gain * PENALTY
    other[last, last] -= gain * PENALTY
    eye = np.eye(points)
    whole = (
        np.kron(np.kron(along_i, eye), eye)
        + np.kron(np.kron(eye, other), eye)
        + np.kron(np.kron(eye, eye), other)
    )
    whole = (TIME_STEP * whole).astype(np.float32)
    high = whole.astype(jnp.bfloat16)
    low = (whole - high.astype(np.float32)).astype(jnp.bfloat16)
    return high, low


def split_np(value):
    value = value.astype(np.float32)
    high = value.astype(jnp.bfloat16)
    return high, (value - high.astype(np.float32)).astype(jnp.bfloat16)


def chain(local, from_before, from_after, count):
    points = local.shape[0]
    whole = np.kron(np.eye(count), local)
    for e in range(1, count):
        whole[e * points, e * points - 1] += from_before
        whole[e * points - 1, e * points] += from_after
    return whole


def response_tables(deriv, gain):
    points = deriv.shape[0]
    last = points - 1
    reach = FLOW_STEPS - 1
    deriv = deriv.astype(np.float64)
    second = TIME_STEP * 4.0 * VISCOSITY * (deriv @ deriv)
    one = TIME_STEP * gain * PENALTY
    two = TIME_STEP * gain * (VELOCITY + PENALTY)
    x_local = -TIME_STEP * 2.0 * VELOCITY * deriv + second
    x_local[0, 0] -= two
    x_local[last, last] -= one
    z_local = second.copy()
    z_local[0, 0] -= one
    z_local[last, last] -= one
    x_whole = chain(x_local, two, one, 3 * EXL)
    z_whole = np.eye(2 * EZL * points) + chain(z_local, one, one, 2 * EZL)
    y_whole = chain(z_local, one, one, EY)
    y_whole[0, 0] += one
    wide = LANES
    x_points = EXL * points
    z_points = EZL * points
    x_middle = slice(x_points, 2 * x_points)
    z_middle = slice(z_points // 2, z_points // 2 + z_points)
    z_left = np.concatenate(
        [np.linalg.matrix_power(z_whole, c)[z_middle] for c in range(reach + 1)], axis=0)
    x_right = np.zeros((reach + 1, wide, 2 * LANES))
    for m in range(reach + 1):
        for c in range(m + 1):
            power = np.linalg.matrix_power(x_whole, m - c)[x_middle]
            x_right[c, :3 * x_points, m * x_points:(m + 1) * x_points] = (
                math.comb(m, m - c) * power.T)
    x_right = x_right.reshape((reach + 1) * wide, 2 * LANES)
    first = np.zeros(EY * points)
    first[0] = one
    weights = np.zeros((reach + 1, EY * points))
    for m in range(reach + 1):
        value = first.copy()
        for b in range(reach - m + 1):
            weights[m] += math.comb(m + b, b) * value
            value = y_whole @ value
    weights = weights.reshape(reach + 1, EY, points).transpose(0, 2, 1)
    weights = np.tile(weights, (1, 1, LANES // EY))
    weights = np.repeat(weights.reshape(-1, 1, LANES), points, axis=1).reshape(-1, LANES)
    z_high, z_low = split_np(z_left)
    x_high, x_low = split_np(x_right)
    ez, k = np.divmod(np.arange(2 * EZL * points), points)
    q, rest = np.divmod(np.arange(EZL * 2 * points * points), 2 * points * points)
    h, rest = np.divmod(rest, points * points)
    gather = (ez[:, None] == (2 * q + h)[None]) & (k[:, None] == (rest % points)[None])
    row_z, rest = np.divmod(np.arange(EZL * EXL * points), EXL * points)
    row_x = rest // points
    col_x, rest = np.divmod(np.arange(EXL * EZL * EY), EZL * EY)
    col_z = rest // EY
    spread = (row_z[:, None] == col_z[None]) & (row_x[:, None] == col_x[None])
    return (
        gather.astype(jnp.bfloat16),
        np.concatenate([z_high, z_high, z_low], axis=1),
        np.concatenate([x_high, x_high, x_low], axis=0),
        np.concatenate([spread, spread], axis=0).astype(jnp.bfloat16),
        weights.astype(np.float32),
    )


def make_kernel(learners, groups, points, width, deriv, gain, tables, small_shapes):
    face = points * points
    last = points - 1
    nodes = face * points
    walls = EXL * EZL
    elements = walls * EY
    pairs = walls * face // (2 * LANES)
    owners = min(learners, width // LANES)
    owned = width // owners
    devices = learners * groups
    block = EZL * EY
    half = LANES // 2
    step_gain = float(TIME_STEP * gain * PENALTY)
    step_gain_x = float(TIME_STEP * gain * (VELOCITY + PENALTY))
    first_row = [float(value) for value in deriv[0]]

    def roll(value, shift):
        shift = shift % LANES
        return value if shift == 0 else pltpu.roll(value, shift, 1)

    rows_sent = points + 1
    reach = FLOW_STEPS - 1
    around = [(dx, dz) for dz in (1, -1, 0) for dx in (1, -1, 0) if dx or dz]
    lane_rows = walls * face // LANES

    def kernel(
        field_ref, first_hbm, second_hbm, edges_hbm, index_hbm, route_hbm, high_hbm, low_hbm,
        gather_hbm, zleft_hbm, xright_hbm, spread_hbm, weights_hbm,
        out_ref, new_first_hbm, new_second_hbm,
        first_ref, second_ref, edges_ref, index_ref, route_ref, new_first_ref, new_second_ref,
        u_ref, high_ref, low_ref, gather_ref, zleft_ref, xright_ref, spread_ref, weights_ref,
        result_ref, mask_ref, mixed_ref, feat_ref, turn_ref, z_ref, g_ref, e_ref, w2_ref,
        count_ref, tile_ref, part_ref, cross_ref, total_ref, stress_ref, place_ref, plane_ref, first_tiles_ref, second_tiles_ref,
        xs_ref, xr_ref, zs_ref, zr_ref,
        load_sem, out_sem, count_send, count_recv, part_send, part_recv, cross_send, cross_recv,
        total_send, total_recv, stress_send, stress_recv, xs_send, xr_recv, zs_send, zr_recv,
    ):
        me = lax.axis_index("solver")
        mine = lax.axis_index("group")

        def peer_s(offset):
            return lax.rem(me + offset, learners)

        def peer_g(offset):
            return lax.rem(mine + offset, groups)

        loads = [
            pltpu.make_async_copy(
                field_ref.at[:, pl.ds(part * LANES, LANES)], u_ref.at[0, part], load_sem.at[part])
            for part in range(2)
        ]
        loads.append(pltpu.make_async_copy(high_hbm, high_ref, load_sem.at[2]))
        loads.append(pltpu.make_async_copy(low_hbm, low_ref, load_sem.at[3]))
        for at, (table, held_table) in enumerate((
            (gather_hbm, gather_ref), (zleft_hbm, zleft_ref), (xright_hbm, xright_ref),
            (spread_hbm, spread_ref), (weights_hbm, weights_ref),
        )):
            loads.append(pltpu.make_async_copy(table, held_table, load_sem.at[4 + at]))
        small_loads = [
            pltpu.make_async_copy(array, held_array, load_sem.at[4 + len(tables) + at])
            for at, (array, held_array) in enumerate((
                (edges_hbm, edges_ref), (route_hbm, route_ref), (first_hbm, first_ref),
                (second_hbm, second_ref), (index_hbm, index_ref),
            ))
        ]
        for load in loads[:2] + small_loads + loads[2:]:
            load.start()

        barrier = pltpu.get_barrier_semaphore()
        for offset in range(1, learners):
            pl.semaphore_signal(
                barrier, inc=1, device_id={"solver": peer_s(offset)},
                device_id_type=pl.DeviceIdType.MESH,
            )
        for offset in range(1, groups):
            pl.semaphore_signal(
                barrier, inc=1, device_id={"group": peer_g(offset)},
                device_id_type=pl.DeviceIdType.MESH,
            )
        for dx, dz in around:
            if dx and dz:
                pl.semaphore_signal(
                    barrier, inc=1,
                    device_id={"solver": peer_s(dx % learners), "group": peer_g(dz % groups)},
                    device_id_type=pl.DeviceIdType.MESH,
                )

        def remote(source, target, send, recv, where):
            return pltpu.make_async_remote_copy(
                src_ref=source, dst_ref=target, send_sem=send, recv_sem=recv,
                device_id=where, device_id_type=pl.DeviceIdType.MESH,
            )

        lane = lax.broadcasted_iota(jnp.int32, (1, LANES), 1)
        low_half = lane < half
        slot = lax.rem(lane, block) // EY
        level = lax.rem(lane, EY)
        contract = (((1,), (1,)), ((), ()))

        for load in small_loads:
            load.wait()
        learner_rows = lax.broadcasted_iota(jnp.int32, (learners, route_ref.shape[1]), 0)
        hits = (route_ref[...] == learner_rows).astype(F32)
        count_ref[me] = jnp.broadcast_to(jnp.sum(hits, axis=1, keepdims=True), (learners, LANES))

        big = 2 * LANES
        edge_rows = lax.rem(
            lax.broadcasted_iota(jnp.int32, (big, edges_ref.shape[1]), 0), face)
        source = (edges_ref[0:1, :] == edge_rows).astype(F32).astype(BF16)
        sink = (edges_ref[1:2, :] == edge_rows).astype(F32).astype(BF16)
        node_rows = lax.broadcasted_iota(jnp.int32, (big, big), 0)
        node_cols = lax.broadcasted_iota(jnp.int32, (big, big), 1)
        graph = 0.25 * lax.dot_general(source, sink, contract, preferred_element_type=F32)
        graph = jnp.where(node_rows // face == node_cols // face, graph, 0.0)
        graph = graph + (node_rows == node_cols).astype(F32)
        small = graph[:LANES, :LANES]
        graph = graph.astype(BF16)
        first = first_ref[...].astype(F32)
        second = second_ref[...].astype(F32)

        def copies(step):
            right, left = {"solver": peer_s(1)}, {"solver": peer_s(learners - 1)}
            up, down = {"group": peer_g(1)}, {"group": peer_g(groups - 1)}
            result = []
            for side, where in ((0, right), (1, left)):
                result.append(remote(
                    xs_ref.at[step, side], xr_ref.at[step, side],
                    xs_send.at[step, side], xr_recv.at[step, side], where))
            for side, where in ((0, up), (1, down)):
                result.append(remote(
                    zs_ref.at[step, side], zr_ref.at[step, side],
                    zs_send.at[step, side], zr_recv.at[step, side], where))
            return result

        half_face = face // 2

        def near(i):
            return pl.ds(i * face, points, stride=points)

        def far(i):
            return pl.ds(i * face + last, points, stride=points)

        def pack_z(step, bottoms, tops):
            for part in range(2):
                high_pack = jnp.zeros((points, LANES), F32)
                low_pack = jnp.zeros((points, LANES), F32)
                for i in range(points):
                    high_pack = jnp.where(slot == i, roll(tops[part][i], EY * (i + 1)), high_pack)
                    low_pack = jnp.where(slot == i, roll(bottoms[part][i], EY * i), low_pack)
                zs_ref[step, 0, part] = high_pack
                zs_ref[step, 1, part] = low_pack

        def pack_x(step, u):
            upper = u[1, pl.ds(nodes - face, face), :]
            xs_ref[step, 0] = jnp.where(low_half, roll(upper[:half_face], half), upper[half_face:])
            lower = u[0, pl.ds(0, face), :]
            xs_ref[step, 1] = jnp.where(low_half, lower[:half_face], roll(lower[half_face:], half))

        def pack_faces(step, u):
            pack_z(step, [[u[part, near(i), :] for i in range(points)] for part in range(2)],
                   [[u[part, far(i), :] for i in range(points)] for part in range(2)])
            pack_x(step, u)

        def send_faces(step):
            every = copies(step)
            for copy in every[2:] + every[:2]:
                copy.start()

        start = u_ref.at[0]
        for load in loads[:2]:
            load.wait()

        def face_rows(value_of):
            rows = jnp.concatenate([value_of(i) for i in range(points)], axis=0)
            return jnp.concatenate([rows, rows], axis=0).astype(BF16)

        def plane(i, j):
            at = pl.ds(i * face + j * points, points)
            return jnp.concatenate([start[0, at, :], start[1, at, :]], axis=1)

        def slope(i):
            total = None
            for j in range(points):
                term = first_row[j] * plane(i, j)
                total = term if total is None else total + term
            return STRESS_SCALE * total

        wall_rows = lax.broadcasted_iota(jnp.int32, (walls, elements), 0)
        wall_cols = lax.broadcasted_iota(jnp.int32, (walls, elements), 1)
        wall_at = (
            lax.rem(wall_rows // 2, EXL) * EZL + wall_rows // (2 * EXL) * 2 + lax.rem(wall_rows, 2))
        select = (wall_cols == wall_at * EY).astype(F32).astype(BF16)
        for j in range(points):
            turn_ref[pl.ds(j * walls, walls), :] = lax.dot_general(
                select, face_rows(lambda i: plane(i, j)), contract, preferred_element_type=F32)
        turn_ref[pl.ds(points * walls, walls), :] = lax.dot_general(
            select, face_rows(slope), contract, preferred_element_type=F32)
        for row in range(lane_rows):
            even = turn_ref[pl.ds(2 * row, points, stride=walls), :]
            odd = turn_ref[pl.ds(2 * row + 1, points, stride=walls), :]
            feat_ref[row // 2, :, pl.ds((row % 2) * LANES, LANES)] = jnp.where(low_half, even, odd)
        target = jnp.where(
            low_half,
            turn_ref[pl.ds(points * walls, lane_rows, stride=2), :],
            turn_ref[pl.ds(points * walls + 1, lane_rows, stride=2), :],
        )

        pack_faces(0, start)
        pl.semaphore_wait(barrier, learners + groups + 2)
        for offset in range(1, learners):
            remote(count_ref.at[me], count_ref.at[me], count_send.at[offset], count_recv.at[me],
                   {"solver": peer_s(offset)}).start()
        send_faces(0)

        def network(first, second):
            turned = jnp.transpose(first).astype(BF16)
            w2_ref[...] = jnp.transpose(jnp.broadcast_to(second, (LANES, width)))

            def one(pair, carry):
                before = jnp.dot(turned, feat_ref[pair].astype(BF16), preferred_element_type=F32)
                hidden = jnp.maximum(before, 0.0)
                mask_ref[pair] = jnp.where(before > 0.0, 1.0, 0.0).astype(BF16)
                mixed = jnp.dot(
                    hidden.astype(BF16), graph, preferred_element_type=F32).astype(BF16)
                mixed_ref[pair] = mixed
                hidden = mixed.astype(F32)
                weight = w2_ref[...]
                z_ref[pl.ds(2 * pair, 1), :] = jnp.sum(
                    hidden[:, :LANES] * weight, axis=0, keepdims=True)
                z_ref[pl.ds(2 * pair + 1, 1), :] = jnp.sum(
                    hidden[:, LANES:] * weight, axis=0, keepdims=True)
                return carry

            lax.fori_loop(0, pairs, one, 0, unroll=pairs)
            return z_ref[...]

        output = network(first, second)
        for t in range(owners):
            first_tiles_ref[t] = first[:, t * owned:(t + 1) * owned]
            second_tiles_ref[t] = jnp.broadcast_to(
                second[:, t * owned:(t + 1) * owned], (points, owned))

        for offset in range(1, learners):
            origin = peer_s(offset)
            remote(count_ref.at[me], count_ref.at[origin], count_send.at[offset],
                   count_recv.at[origin], {"solver": origin}).wait_recv()
        counts = count_ref[0]
        for other in range(1, learners):
            counts = counts + count_ref[other]
        inverse = 1.0 / (jnp.maximum(counts, 1.0) * devices)
        places = 2 * lax.broadcasted_iota(jnp.int32, (lane_rows, index_ref.shape[1]), 0)
        taken = index_ref[...]
        taken = 2 * (lax.rem(taken, EZL) // 2 * EXL + taken // EZL) + lax.rem(taken, 2)
        chosen = (taken == places).astype(F32)
        even = lax.dot_general(chosen, hits, contract, preferred_element_type=F32)
        chosen = (taken == places + 1).astype(F32)
        odd = lax.dot_general(chosen, hits, contract, preferred_element_type=F32)
        difference = output - target
        error = jnp.zeros((lane_rows, LANES), F32)
        for learner in range(learners):
            times = jnp.where(low_half, even[:, learner:learner + 1], odd[:, learner:learner + 1])
            single = (difference * inverse[learner:learner + 1]).astype(BF16).astype(F32)
            error = error + times * single
        e_ref[...] = error
        g_ref[...] = lax.dot_general(
            error, small, contract, precision=HIGH, preferred_element_type=F32)

        def split(value):
            upper = value.astype(BF16).astype(F32)
            return jnp.concatenate([upper, value - upper], axis=0).astype(BF16)

        def row_pair(ref, pair):
            return jnp.concatenate([ref[pl.ds(2 * pair, 1), :], ref[pl.ds(2 * pair + 1, 1), :]], axis=1)

        moment = None
        for pair in range(pairs):
            term = lax.dot_general(
                split(feat_ref[pair] * row_pair(g_ref, pair)), mask_ref[pair], contract,
                preferred_element_type=F32)
            moment = term if moment is None else moment + term
        moment = moment[0:points] + moment[points:2 * points]
        error_rows = [
            jnp.broadcast_to(e_ref[pl.ds(row, 1), :], (16, LANES)) for row in range(lane_rows)
        ]
        for t in range(owners):
            blocks = []
            for at in range(t * owned, (t + 1) * owned, 16):
                total = None
                for row in range(lane_rows):
                    mixed = mixed_ref[
                        row // 2, pl.ds(at, 16), pl.ds(row % 2 * LANES, LANES)].astype(F32)
                    total = mixed * error_rows[row] if total is None else (
                        total + mixed * error_rows[row])
                blocks.append(total)
            turned = jnp.transpose(jnp.concatenate(blocks, axis=0))
            tile_ref[t, pl.ds(points, 1), :] = jnp.sum(turned, axis=0, keepdims=True)
            tile_ref[t, pl.ds(0, points), :] = moment[:, t * owned:(t + 1) * owned]

        def when_owner(which, action):
            if owners == learners:
                action()
            else:
                pl.when(which < owners)(action)

        def clamp(which):
            return which if owners == learners else jnp.minimum(which, owners - 1)

        def part_copy(offset):
            where = peer_s(offset)
            return where, remote(tile_ref.at[clamp(where)], part_ref.at[me], part_send.at[offset],
                                 part_recv.at[me], {"solver": where})

        for offset in range(1, learners):
            where, copy = part_copy(offset)
            when_owner(where, copy.start)

        def local(source, target):
            u = jnp.concatenate([source[0], source[1]], axis=1)
            upper = u.astype(BF16)
            lower = (u - upper.astype(F32)).astype(BF16)
            u = u + (
                jnp.dot(high_ref[...], upper, preferred_element_type=F32)
                + jnp.dot(high_ref[...], lower, preferred_element_type=F32)
                + jnp.dot(low_ref[...], upper, preferred_element_type=F32)
            )
            for part in range(2):
                target[part] = u[:, part * LANES:(part + 1) * LANES]
            for part in range(2):
                for i in range(points):
                    base = i * face
                    bottom = source[part, pl.ds(base, points), :]
                    top = source[part, pl.ds(base + face - points, points), :]
                    below = jnp.where(level == 0, bottom, roll(top, 1))
                    above = jnp.where(level == EY - 1, 0.0, roll(bottom, -1))
                    target[part, pl.ds(base, points), :] += step_gain * below
                    target[part, pl.ds(base + face - points, points), :] += step_gain * above
            low0 = roll(source[0, pl.ds(nodes - face, face), :], half)
            low1 = roll(source[1, pl.ds(nodes - face, face), :], half)
            target[0, pl.ds(0, face), :] += step_gain_x * jnp.where(low_half, 0.0, low0)
            target[1, pl.ds(0, face), :] += step_gain_x * jnp.where(low_half, low0, low1)
            high0 = roll(source[0, pl.ds(0, face), :], half)
            high1 = roll(source[1, pl.ds(0, face), :], half)
            target[0, pl.ds(nodes - face, face), :] += step_gain * jnp.where(low_half, high0, high1)
            target[1, pl.ds(nodes - face, face), :] += step_gain * jnp.where(low_half, high1, 0.0)
            for part in range(2):
                for i in range(points):
                    before = jnp.where(slot == 0, 0.0, roll(source[part, far(i), :], EY))
                    after = jnp.where(slot == EZL - 1, 0.0, roll(source[part, near(i), :], -EY))
                    target[part, near(i), :] = target[part, near(i), :] + step_gain * before
                    target[part, far(i), :] = target[part, far(i), :] + step_gain * after

        def halo(step, target, send):
            every = copies(step)
            every[0].wait_recv()
            every[1].wait_recv()
            ghost = xr_ref[step, 0]
            ghost = jnp.concatenate([ghost, roll(ghost, half)], axis=0)
            target[0, pl.ds(0, face), :] += step_gain_x * jnp.where(low_half, ghost, 0.0)
            ghost = xr_ref[step, 1]
            ghost = jnp.concatenate([roll(ghost, half), ghost], axis=0)
            target[1, pl.ds(nodes - face, face), :] += step_gain * jnp.where(low_half, 0.0, ghost)
            every[2].wait_recv()
            every[3].wait_recv()
            bottoms, tops = [], []
            for part in range(2):
                before_pack = step_gain * zr_ref[step, 0, part]
                after_pack = step_gain * zr_ref[step, 1, part]
                for i in range(points):
                    before = jnp.where(slot == 0, roll(before_pack, half - EY * i), 0.0)
                    after = jnp.where(
                        slot == EZL - 1, roll(after_pack, EY * (EZL - 1 - i)), 0.0)
                    bottoms.append(target[part, near(i), :] + before)
                    tops.append(target[part, far(i), :] + after)
                    target[part, near(i), :] = bottoms[-1]
                    target[part, far(i), :] = tops[-1]
            if send:
                pack_z(step + 1, [bottoms[:points], bottoms[points:]], [tops[:points], tops[points:]])
                pack_x(step + 1, target)
                send_faces(step + 1)

        for load in loads[2:]:
            load.wait()
        held = [start, u_ref.at[1]]

        def flow(step):
            source, target = held[step % 2], held[(step + 1) % 2]
            local(source, target)
            halo(step, target, step < FLOW_STEPS - 1)

        flow(0)

        def reduce_part():
            total = tile_ref[clamp(me)]
            for offset in range(1, learners):
                origin = peer_s(offset)
                remote(tile_ref.at[0], part_ref.at[origin], part_send.at[offset],
                       part_recv.at[origin], {"solver": origin}).wait_recv()
            for offset in range(1, learners):
                total = total + part_ref[peer_s(offset)]
            cross_ref[mine] = total
            for offset in range(1, groups):
                remote(cross_ref.at[mine], cross_ref.at[mine], cross_send.at[offset],
                       cross_recv.at[mine], {"group": peer_g(offset)}).start()

        def reduce_cross():
            for offset in range(1, groups):
                origin = peer_g(offset)
                remote(cross_ref.at[mine], cross_ref.at[origin], cross_send.at[offset],
                       cross_recv.at[origin], {"group": origin}).wait_recv()
            total = cross_ref[0]
            for origin in range(1, groups):
                total = total + cross_ref[origin]
            at = clamp(me)
            total_ref[at] = total
            for offset in range(1, learners):
                remote(total_ref.at[at], total_ref.at[at], total_send.at[offset],
                       total_recv.at[at], {"solver": peer_s(offset)}).start()

        when_owner(me, reduce_part)
        flow(1)
        when_owner(me, reduce_cross)
        flow(2)
        if owners == learners and owners == 8:
            plus, half_chip = lax.rem(me, 2), lax.rem(me // 2, 2)
            core = me + 1 - 2 * plus
            chip = me // 4 * 4 + 2 - 2 * half_chip
            far_chip = lax.rem(me // 4 * 4 + 4 + 2 * half_chip, 8)
            last_chip = lax.rem(me // 4 * 4 + 6 - 2 * half_chip, 8)
            parts_of = [
                [me, core],
                [chip, chip + 1, far_chip, far_chip + 1],
                [last_chip, last_chip + 1],
            ]
        else:
            parts_of = [list(range(owners))]

        def arrive(at):
            copy = remote(total_ref.at[at], total_ref.at[at], total_send.at[1],
                          total_recv.at[at], {"solver": peer_s(1)})
            if isinstance(at, int):
                pl.when(me != at)(copy.wait_recv)
            elif at is not me:
                copy.wait_recv()

        features = [feat_ref[pair].astype(BF16) for pair in range(pairs)]
        sums = [None] * pairs
        for tiles in parts_of:
            turned, columns = [], []
            for at in tiles:
                arrive(at)
                before, weight = first_tiles_ref[at], second_tiles_ref[at]
                grad = total_ref[at]
                before = (before - LEARN_RATE * (grad[0:points] * weight)).astype(BF16).astype(F32)
                weight = (weight - LEARN_RATE * grad[points:points + 1]).astype(BF16).astype(F32)
                first_tiles_ref[at] = before
                second_tiles_ref[at] = weight
                turned.append(jnp.transpose(before))
                columns.append(jnp.transpose(jnp.broadcast_to(weight[0:1], (LANES, owned))))
            turned = jnp.concatenate(turned, axis=0).astype(BF16)
            columns = jnp.concatenate(columns, axis=0)
            for pair in range(pairs):
                hidden = jnp.maximum(
                    jnp.dot(turned, features[pair], preferred_element_type=F32), 0.0)
                hidden = hidden * jnp.concatenate([columns, columns], axis=1)
                hidden = jnp.sum(hidden.reshape(-1, points, 2 * LANES), axis=0)
                sums[pair] = hidden if sums[pair] is None else sums[pair] + hidden
        for pair in range(pairs):
            row = jnp.sum(sums[pair], axis=0, keepdims=True)
            z_ref[pl.ds(2 * pair, 1), :] = row[:, :LANES]
            z_ref[pl.ds(2 * pair + 1, 1), :] = row[:, LANES:]

        middle = pl.ds(lane_rows // 2, lane_rows)
        stress_ref[1, middle, :] = jnp.dot(
            z_ref[...], small, precision=HIGH, preferred_element_type=F32)
        stress_copies = []
        for way, (dx, dz) in enumerate(around):
            rows = {
                0: (middle, middle),
                1: (pl.ds(lane_rows, lane_rows // 2), pl.ds(0, lane_rows // 2)),
                -1: (pl.ds(lane_rows // 2, lane_rows // 2), pl.ds(3 * lane_rows // 2, lane_rows // 2)),
            }[dz]
            stress_copies.append(remote(
                stress_ref.at[1, rows[0]], stress_ref.at[1 - dx, rows[1]],
                stress_send.at[way], stress_recv.at[way],
                {"solver": peer_s(dx % learners), "group": peer_g(dz % groups)}))
        for copy in stress_copies:
            copy.start()
        new_first_ref[...] = jnp.concatenate(
            [first_tiles_ref[t] for t in range(owners)], axis=1).astype(BF16)
        new_second_ref[...] = jnp.concatenate(
            [second_tiles_ref[t][0:1] for t in range(owners)], axis=1).astype(BF16)
        updates = [
            pltpu.make_async_copy(new_first_ref, new_first_hbm, out_sem.at[points // 2]),
            pltpu.make_async_copy(new_second_ref, new_second_hbm, out_sem.at[points // 2 + 1]),
        ]
        for copy in updates:
            copy.start()
        for step in range(3, FLOW_STEPS):
            flow(step)
        for copy in stress_copies:
            copy.wait_recv()

        def halves(value):
            upper = value.astype(BF16)
            return upper, (value - upper.astype(F32)).astype(BF16)

        within = lax.rem(lane, face) // points
        sub = lax.broadcasted_iota(jnp.int32, (points, LANES), 0)
        own_row = within == sub
        place_ref[...] = jnp.zeros_like(place_ref)
        for q in range(EZL):
            for e in range(0, 3 * EXL, 2):
                blocks = []
                for at in (e, e + 1):
                    row = stress_ref[at // EXL, pl.ds(q * EXL + at % EXL, 1), :]
                    blocks.append(jnp.where(own_row, jnp.broadcast_to(row, (points, LANES)), 0.0))
                upper, lower = halves(jnp.concatenate(blocks, axis=0))
                columns = pl.ds(q * LANES, LANES)
                place_ref[pl.ds(e * points, 2 * points), columns] = upper
                place_ref[pl.ds(LANES + e * points, 2 * points), columns] = lower
        both = lax.dot_general(
            gather_ref[...], place_ref[...], contract, preferred_element_type=F32)
        upper, lower = halves(both[:, :LANES] + both[:, LANES:])
        ladder = jnp.dot(
            zleft_ref[...], jnp.concatenate([upper, lower, upper], axis=0),
            preferred_element_type=F32)
        z_points = EZL * points
        upper, lower = halves(jnp.concatenate(
            [ladder[c * z_points:(c + 1) * z_points] for c in range(reach + 1)], axis=1))
        plane_t = jnp.dot(
            jnp.concatenate([upper, lower, upper], axis=1), xright_ref[...],
            preferred_element_type=F32)
        span = EXL * points
        per = LANES // span
        quarter = lane // span
        rows = []
        for m in range(reach + 1):
            sides = []
            for t in range(EZL // per):
                value = None
                for e in range(per):
                    z_at = (t * per + e) * points
                    piece = roll(
                        plane_t[z_at:z_at + points, (m // per) * LANES:(m // per + 1) * LANES],
                        (e - m % per) * span)
                    value = piece if value is None else jnp.where(quarter == e, piece, value)
                sides.append(value)
            value = jnp.concatenate(sides, axis=1)
            upper = value.astype(BF16).astype(F32)
            value = jnp.concatenate([upper, value - upper], axis=1)
            node = lax.rem(lax.broadcasted_iota(jnp.int32, value.shape, 1), points)
            rows += [jnp.where(node == i, value, 0.0) for i in range(points)]
        plane_ref[...] = jnp.dot(
            jnp.concatenate(rows, axis=0).astype(BF16), spread_ref[...],
            preferred_element_type=F32)
        ended = held[FLOW_STEPS % 2]
        results = []
        for i in range(points):
            for part in range(2):
                columns = slice(part * LANES, (part + 1) * LANES)
                planes = [
                    plane_ref[pl.ds((m * points + i) * points, points), columns]
                    for m in range(reach + 1)
                ]
                for j in range(points):
                    at = pl.ds(i * face + j * points, points)
                    value = ended[part, at, :]
                    for m in range(reach + 1):
                        value = value + (
                            weights_ref[pl.ds((m * points + j) * points, points), :] * planes[m])
                    result_ref[at, columns] = value
            if i % 2:
                rows = pl.ds((i - 1) * face, 2 * face)
                results.append(pltpu.make_async_copy(
                    result_ref.at[rows], out_ref.at[rows], out_sem.at[i // 2]))
                results[-1].start()

        for offset in range(1, learners):
            remote(count_ref.at[me], count_ref.at[me], count_send.at[offset], count_recv.at[me],
                   {"solver": peer_s(offset)}).wait_send()
            where, copy = part_copy(offset)
            when_owner(where, copy.wait_send)

        def drain_owned():
            at = clamp(me)
            for offset in range(1, groups):
                remote(cross_ref.at[mine], cross_ref.at[mine], cross_send.at[offset],
                       cross_recv.at[mine], {"group": peer_g(offset)}).wait_send()
            for offset in range(1, learners):
                remote(total_ref.at[at], total_ref.at[at], total_send.at[offset],
                       total_recv.at[at], {"solver": peer_s(offset)}).wait_send()

        when_owner(me, drain_owned)
        for copy in results + updates:
            copy.wait()
        for copy in stress_copies:
            copy.wait_send()
        for step in range(FLOW_STEPS):
            for copy in copies(step):
                copy.wait_send()

    dma = pltpu.SemaphoreType.DMA
    scratch = [
        pltpu.VMEM((points, width), BF16),
        pltpu.VMEM((1, width), BF16),
        pltpu.VMEM(small_shapes[0], jnp.int32),
        pltpu.VMEM(small_shapes[1], jnp.int32),
        pltpu.VMEM(small_shapes[2], jnp.int32),
        pltpu.VMEM((points, width), BF16),
        pltpu.VMEM((1, width), BF16),
        pltpu.VMEM((2, 2, nodes, LANES), F32),
        pltpu.VMEM((nodes, nodes), BF16),
        pltpu.VMEM((nodes, nodes), BF16),
        *[pltpu.VMEM(table.shape, table.dtype) for table in tables],
        pltpu.VMEM((nodes, elements), F32),
        pltpu.VMEM((pairs, width, 2 * LANES), BF16),
        pltpu.VMEM((pairs, width, 2 * LANES), BF16),
        pltpu.VMEM((pairs, points, 2 * LANES), F32),
        pltpu.VMEM((points * walls + walls, LANES), F32),
        pltpu.VMEM((lane_rows, LANES), F32),
        pltpu.VMEM((lane_rows, LANES), F32),
        pltpu.VMEM((lane_rows, LANES), F32),
        pltpu.VMEM((width, LANES), F32),
        pltpu.VMEM((learners, learners, LANES), F32),
        pltpu.VMEM((owners, rows_sent, owned), F32),
        pltpu.VMEM((learners, rows_sent, owned), F32),
        pltpu.VMEM((groups, rows_sent, owned), F32),
        pltpu.VMEM((owners, rows_sent, owned), F32),
        pltpu.VMEM((3, 2 * lane_rows, LANES), F32),
        pltpu.VMEM((2 * LANES, EZL * LANES), BF16),
        pltpu.VMEM((FLOW_STEPS * face, 2 * LANES), F32),
        pltpu.VMEM((owners, points, owned), F32),
        pltpu.VMEM((owners, points, owned), F32),
        pltpu.VMEM((FLOW_STEPS, 2, face // 2, LANES), F32),
        pltpu.VMEM((FLOW_STEPS, 2, face // 2, LANES), F32),
        pltpu.VMEM((FLOW_STEPS, 2, 2, points, LANES), F32),
        pltpu.VMEM((FLOW_STEPS, 2, 2, points, LANES), F32),
        dma((9 + len(tables),)), dma((points // 2 + 2,)),
        dma((learners,)), dma((learners,)), dma((learners,)), dma((learners,)),
        dma((groups,)), dma((groups,)), dma((learners,)), dma((owners,)),
        dma((len(around),)), dma((len(around),)),
        dma((FLOW_STEPS, 2)), dma((FLOW_STEPS, 2)), dma((FLOW_STEPS, 2)), dma((FLOW_STEPS, 2)),
    ]
    return kernel, scratch


def finish(
    field_ref, first_ref, second_ref, out_ref, new_first_ref, new_second_ref,
    held_ref, held_first_ref, held_second_ref, in_sem, out_sem
):
    size = field_ref.shape[0] // CHUNKS
    ways = [(first_ref, held_first_ref, new_first_ref), (second_ref, held_second_ref, new_second_ref)]
    for chunk in range(CHUNKS):
        rows = pl.ds(chunk * size, size)
        ways.append((field_ref.at[rows], held_ref.at[rows], out_ref.at[rows]))
    loads = [
        pltpu.make_async_copy(way[0], way[1], in_sem.at[at]) for at, way in enumerate(ways)
    ]
    stores = [
        pltpu.make_async_copy(way[1], way[2], out_sem.at[at]) for at, way in enumerate(ways)
    ]
    for copy in loads:
        copy.start()
    for load, store in zip(loads, stores):
        load.wait()
        store.start()
    for copy in stores:
        copy.wait()


def shards(field, first_weight, second_weight, face_edges, sample_index, route):
    points = field.shape[0]
    elements = field.shape[3]
    nodes = points**3
    width = first_weight.shape[1]
    learners = lax.axis_size("solver")
    groups = lax.axis_size("group")
    deriv, end_weight = gll_tables(points)
    gain = 2.0 / end_weight
    high, low = element_operator(deriv, gain)
    tables = response_tables(deriv, gain)
    kernel, scratch = make_kernel(
        learners, groups, points, width, deriv, gain, tables,
        (face_edges.shape, (1, sample_index.size), (1, route.size)))
    hbm = pl.BlockSpec(memory_space=pltpu.HBM)
    new_field, new_first, new_second = pl.pallas_call(
        kernel,
        out_shape=(
            jax.ShapeDtypeStruct((nodes, elements), F32),
            jax.ShapeDtypeStruct(first_weight.shape, BF16),
            jax.ShapeDtypeStruct((1, width), BF16),
        ),
        in_specs=[hbm] * (8 + len(tables)),
        out_specs=(hbm, hbm, hbm),
        scratch_shapes=scratch,
        compiler_params=pltpu.CompilerParams(
            collective_id=0, has_side_effects=True, vmem_limit_bytes=67_043_328
        ),
        name="step",
    )(
        field.reshape(nodes, elements),
        first_weight,
        second_weight.reshape(1, width),
        face_edges,
        sample_index.reshape(1, -1),
        route.reshape(1, -1),
        jnp.asarray(high),
        jnp.asarray(low),
        *[jnp.asarray(table) for table in tables],
    )
    new_field, new_first, new_second = pl.pallas_call(
        finish,
        out_shape=tuple(
            jax.ShapeDtypeStruct(value.shape, value.dtype)
            for value in (new_field, new_first, new_second)),
        in_specs=[hbm, hbm, hbm],
        out_specs=(hbm, hbm, hbm),
        scratch_shapes=[
            pltpu.VMEM((nodes, elements), F32),
            pltpu.VMEM(new_first.shape, BF16),
            pltpu.VMEM(new_second.shape, BF16),
            pltpu.SemaphoreType.DMA((CHUNKS + 2,)),
            pltpu.SemaphoreType.DMA((CHUNKS + 2,)),
        ],
        compiler_params=pltpu.CompilerParams(vmem_limit_bytes=67_043_328),
        name="finish",
    )(new_field, new_first, new_second)
    return (new_field.reshape(field.shape), new_first, new_second.reshape(second_weight.shape))


def solution(mesh):
    return jax.shard_map(
        shards,
        mesh=mesh,
        in_specs=(
            P(None, None, None, ("solver", "group")),
            P(),
            P(),
            P(),
            P(("solver", "group")),
            P(("solver", "group"), None),
        ),
        out_specs=(P(None, None, None, ("solver", "group")), P(), P()),
        check_vma=False,
    )
```

```python
import math

import jax
import jax.numpy as jnp
import numpy as np
from jax import lax
from jax.experimental import pallas as pl
from jax.experimental.pallas import tpu as pltpu
from jax.sharding import PartitionSpec as P

FLOW_STEPS = 5
EXL = 4
EZL = 8
EY = 8

HIGH = lax.Precision.HIGHEST
TIME_STEP = 0.002
VISCOSITY = 0.01
VELOCITY = 1.0
PENALTY = 1.0
STRESS_SCALE = 0.1
LEARN_RATE = 0.05
LANES = 128
CHUNKS = 4
F32 = jnp.float32
BF16 = jnp.bfloat16


def legendre_table(points_x, points):
    table = np.zeros((points_x.shape[0], points))
    table[:, 0] = 1.0
    table[:, 1] = points_x
    for degree in range(2, points):
        table[:, degree] = (
            (2 * degree - 1) * points_x * table[:, degree - 1] - (degree - 1) * table[:, degree - 2]
        ) / degree
    return table


def gll_tables(points):
    order = points - 1
    guess = np.cos(np.pi * np.arange(points) / order)
    for sweep in range(100):
        table = legendre_table(guess, points)
        guess = guess - (guess * table[:, order] - table[:, order - 1]) / (points * table[:, order])
    nodes = guess[::-1]
    values = legendre_table(nodes, points)[:, order]
    matrix = np.zeros((points, points))
    for row in range(points):
        for column in range(points):
            if row != column:
                matrix[row, column] = values[row] / (values[column] * (nodes[row] - nodes[column]))
    matrix[0, 0] = -order * (order + 1) / 4.0
    matrix[order, order] = order * (order + 1) / 4.0
    return matrix.astype(np.float32), 2.0 / (order * (order + 1))


def element_operator(deriv, gain):
    points = deriv.shape[0]
    last = points - 1
    deriv = deriv.astype(np.float64)
    second = 4.0 * VISCOSITY * (deriv @ deriv)
    along_i = -2.0 * VELOCITY * deriv + second
    along_i[0, 0] -= gain * (VELOCITY + PENALTY)
    along_i[last, last] -= gain * PENALTY
    other = second.copy()
    other[0, 0] -= gain * PENALTY
    other[last, last] -= gain * PENALTY
    eye = np.eye(points)
    whole = (
        np.kron(np.kron(along_i, eye), eye)
        + np.kron(np.kron(eye, other), eye)
        + np.kron(np.kron(eye, eye), other)
    )
    whole = (TIME_STEP * whole).astype(np.float32)
    high = whole.astype(jnp.bfloat16)
    low = (whole - high.astype(np.float32)).astype(jnp.bfloat16)
    return high, low


def split_np(value):
    value = value.astype(np.float32)
    high = value.astype(jnp.bfloat16)
    return high, (value - high.astype(np.float32)).astype(jnp.bfloat16)


def chain(local, from_before, from_after, count):
    points = local.shape[0]
    whole = np.kron(np.eye(count), local)
    for e in range(1, count):
        whole[e * points, e * points - 1] += from_before
        whole[e * points - 1, e * points] += from_after
    return whole


def response_tables(deriv, gain):
    points = deriv.shape[0]
    last = points - 1
    reach = FLOW_STEPS - 1
    deriv = deriv.astype(np.float64)
    second = TIME_STEP * 4.0 * VISCOSITY * (deriv @ deriv)
    one = TIME_STEP * gain * PENALTY
    two = TIME_STEP * gain * (VELOCITY + PENALTY)
    x_local = -TIME_STEP * 2.0 * VELOCITY * deriv + second
    x_local[0, 0] -= two
    x_local[last, last] -= one
    z_local = second.copy()
    z_local[0, 0] -= one
    z_local[last, last] -= one
    x_whole = chain(x_local, two, one, 3 * EXL)
    z_whole = np.eye(2 * EZL * points) + chain(z_local, one, one, 2 * EZL)
    y_whole = chain(z_local, one, one, EY)
    y_whole[0, 0] += one
    wide = LANES
    x_points = EXL * points
    z_points = EZL * points
    x_middle = slice(x_points, 2 * x_points)
    z_middle = slice(z_points // 2, z_points // 2 + z_points)
    z_left = np.concatenate(
        [np.linalg.matrix_power(z_whole, c)[z_middle] for c in range(reach + 1)], axis=0)
    x_right = np.zeros((reach + 1, wide, 2 * LANES))
    for m in range(reach + 1):
        for c in range(m + 1):
            power = np.linalg.matrix_power(x_whole, m - c)[x_middle]
            x_right[c, :3 * x_points, m * x_points:(m + 1) * x_points] = (
                math.comb(m, m - c) * power.T)
    x_right = x_right.reshape((reach + 1) * wide, 2 * LANES)
    first = np.zeros(EY * points)
    first[0] = one
    weights = np.zeros((reach + 1, EY * points))
    for m in range(reach + 1):
        value = first.copy()
        for b in range(reach - m + 1):
            weights[m] += math.comb(m + b, b) * value
            value = y_whole @ value
    weights = weights.reshape(reach + 1, EY, points).transpose(0, 2, 1)
    weights = np.tile(weights, (1, 1, LANES // EY))
    weights = np.repeat(weights.reshape(-1, 1, LANES), points, axis=1).reshape(-1, LANES)
    z_high, z_low = split_np(z_left)
    x_high, x_low = split_np(x_right)
    ez, k = np.divmod(np.arange(2 * EZL * points), points)
    q, rest = np.divmod(np.arange(EZL * 2 * points * points), 2 * points * points)
    h, rest = np.divmod(rest, points * points)
    gather = (ez[:, None] == (2 * q + h)[None]) & (k[:, None] == (rest % points)[None])
    row_z, rest = np.divmod(np.arange(EZL * EXL * points), EXL * points)
    row_x = rest // points
    col_x, rest = np.divmod(np.arange(EXL * EZL * EY), EZL * EY)
    col_z = rest // EY
    spread = (row_z[:, None] == col_z[None]) & (row_x[:, None] == col_x[None])
    return (
        gather.astype(jnp.bfloat16),
        np.concatenate([z_high, z_high, z_low], axis=1),
        np.concatenate([x_high, x_high, x_low], axis=0),
        np.concatenate([spread, spread], axis=0).astype(jnp.bfloat16),
        weights.astype(np.float32),
    )


def make_kernel(learners, groups, points, width, deriv, gain, tables, small_shapes):
    face = points * points
    last = points - 1
    nodes = face * points
    walls = EXL * EZL
    elements = walls * EY
    pairs = walls * face // (2 * LANES)
    owners = min(learners, width // LANES)
    owned = width // owners
    devices = learners * groups
    block = EZL * EY
    half = LANES // 2
    step_gain = float(TIME_STEP * gain * PENALTY)
    step_gain_x = float(TIME_STEP * gain * (VELOCITY + PENALTY))
    first_row = [float(value) for value in deriv[0]]

    def roll(value, shift):
        shift = shift % LANES
        return value if shift == 0 else pltpu.roll(value, shift, 1)

    rows_sent = points + 1
    reach = FLOW_STEPS - 1
    fused = FLOW_STEPS - 2
    corners = [(dx, dz) for dx in (1, -1) for dz in (1, -1)]
    around = [(dx, dz) for dz in (1, -1, 0) for dx in (1, -1, 0) if dx or dz]
    lane_rows = walls * face // LANES

    def kernel(
        field_ref, first_hbm, second_hbm, edges_hbm, index_hbm, route_hbm, high_hbm, low_hbm,
        gather_hbm, zleft_hbm, xright_hbm, spread_hbm, weights_hbm,
        out_ref, new_first_hbm, new_second_hbm,
        first_ref, second_ref, edges_ref, index_ref, route_ref, new_first_ref, new_second_ref,
        u_ref, high_ref, low_ref, gather_ref, zleft_ref, xright_ref, spread_ref, weights_ref,
        result_ref, mask_ref, mixed_ref, feat_ref, turn_ref, z_ref, g_ref, e_ref, w2_ref,
        count_ref, tile_ref, part_ref, cross_ref, total_ref, stress_ref, place_ref, plane_ref,
        xs_ref, xr_ref, zs_ref, zr_ref, line_ref,
        load_sem, out_sem, count_send, count_recv, part_send, part_recv, cross_send, cross_recv,
        total_send, total_recv, stress_send, stress_recv, xs_send, xr_recv, zs_send, zr_recv,
        line_send, line_recv,
    ):
        me = lax.axis_index("solver")
        mine = lax.axis_index("group")

        def peer_s(offset):
            return lax.rem(me + offset, learners)

        def peer_g(offset):
            return lax.rem(mine + offset, groups)

        loads = [
            pltpu.make_async_copy(
                field_ref.at[:, pl.ds(part * LANES, LANES)], u_ref.at[0, part], load_sem.at[part])
            for part in range(2)
        ]
        loads.append(pltpu.make_async_copy(high_hbm, high_ref, load_sem.at[2]))
        loads.append(pltpu.make_async_copy(low_hbm, low_ref, load_sem.at[3]))
        for at, (table, held_table) in enumerate((
            (gather_hbm, gather_ref), (zleft_hbm, zleft_ref), (xright_hbm, xright_ref),
            (spread_hbm, spread_ref), (weights_hbm, weights_ref),
        )):
            loads.append(pltpu.make_async_copy(table, held_table, load_sem.at[4 + at]))
        small_loads = [
            pltpu.make_async_copy(array, held_array, load_sem.at[4 + len(tables) + at])
            for at, (array, held_array) in enumerate((
                (edges_hbm, edges_ref), (route_hbm, route_ref), (first_hbm, first_ref),
                (second_hbm, second_ref), (index_hbm, index_ref),
            ))
        ]
        for load in loads[:2] + small_loads + loads[2:]:
            load.start()

        barrier = pltpu.get_barrier_semaphore()
        for offset in range(1, learners):
            pl.semaphore_signal(
                barrier, inc=1, device_id={"solver": peer_s(offset)},
                device_id_type=pl.DeviceIdType.MESH,
            )
        for offset in range(1, groups):
            pl.semaphore_signal(
                barrier, inc=1, device_id={"group": peer_g(offset)},
                device_id_type=pl.DeviceIdType.MESH,
            )
        for dx, dz in around:
            if dx and dz:
                pl.semaphore_signal(
                    barrier, inc=1,
                    device_id={"solver": peer_s(dx % learners), "group": peer_g(dz % groups)},
                    device_id_type=pl.DeviceIdType.MESH,
                )

        def remote(source, target, send, recv, where):
            return pltpu.make_async_remote_copy(
                src_ref=source, dst_ref=target, send_sem=send, recv_sem=recv,
                device_id=where, device_id_type=pl.DeviceIdType.MESH,
            )

        lane = lax.broadcasted_iota(jnp.int32, (1, LANES), 1)
        low_half = lane < half
        slot = lax.rem(lane, block) // EY
        level = lax.rem(lane, EY)
        contract = (((1,), (1,)), ((), ()))

        for load in small_loads:
            load.wait()
        learner_rows = lax.broadcasted_iota(jnp.int32, (learners, route_ref.shape[1]), 0)
        hits = (route_ref[...] == learner_rows).astype(F32)
        count_ref[me] = jnp.broadcast_to(jnp.sum(hits, axis=1, keepdims=True), (learners, LANES))

        big = 2 * LANES
        edge_rows = lax.rem(
            lax.broadcasted_iota(jnp.int32, (big, edges_ref.shape[1]), 0), face)
        source = (edges_ref[0:1, :] == edge_rows).astype(F32).astype(BF16)
        sink = (edges_ref[1:2, :] == edge_rows).astype(F32).astype(BF16)
        node_rows = lax.broadcasted_iota(jnp.int32, (big, big), 0)
        node_cols = lax.broadcasted_iota(jnp.int32, (big, big), 1)
        graph = 0.25 * lax.dot_general(source, sink, contract, preferred_element_type=F32)
        graph = jnp.where(node_rows // face == node_cols // face, graph, 0.0)
        graph = graph + (node_rows == node_cols).astype(F32)
        graph = graph.astype(BF16)
        small = graph[:LANES, :LANES]
        first = first_ref[...].astype(F32)
        second = second_ref[...].astype(F32)
        places = 2 * lax.broadcasted_iota(jnp.int32, (lane_rows, index_ref.shape[1]), 0)
        taken = index_ref[...]
        taken = 2 * (lax.rem(taken, EZL) // 2 * EXL + taken // EZL) + lax.rem(taken, 2)
        chosen = (taken == places).astype(F32)
        even = lax.dot_general(chosen, hits, contract, preferred_element_type=F32)
        chosen = (taken == places + 1).astype(F32)
        odd = lax.dot_general(chosen, hits, contract, preferred_element_type=F32)
        times = [
            jnp.where(low_half, even[:, learner:learner + 1], odd[:, learner:learner + 1])
            for learner in range(learners)
        ]

        def prepare(first, second):
            w2_ref[...] = jnp.transpose(jnp.broadcast_to(second, (LANES, width)))
            return jnp.transpose(first).astype(BF16)

        turned = prepare(first, second)

        def through_graph(value, axis):
            pieces = []
            for piece in range(3):
                pieces.append(value.astype(BF16))
                value = value - pieces[-1].astype(F32)
            result = lax.dot_general(
                jnp.concatenate(pieces, axis=0), small, (((1,), (axis,)), ((), ())),
                preferred_element_type=F32)
            return result[:lane_rows] + result[lane_rows:2 * lane_rows] + result[2 * lane_rows:]


        def copies(step):
            right, left = {"solver": peer_s(1)}, {"solver": peer_s(learners - 1)}
            up, down = {"group": peer_g(1)}, {"group": peer_g(groups - 1)}
            result = []
            at = step if step < fused else pl.ds(fused, 2)
            for side, where in ((0, right), (1, left)):
                result.append(remote(
                    xs_ref.at[at, side], xr_ref.at[at, side],
                    xs_send.at[step, side], xr_recv.at[step, side], where))
            for side, where in ((0, up), (1, down)):
                result.append(remote(
                    zs_ref.at[at, side], zr_ref.at[at, side],
                    zs_send.at[step, side], zr_recv.at[step, side], where))
            if step == fused:
                for way, (dx, dz) in enumerate(corners):
                    result.append(remote(
                        line_ref.at[0, way], line_ref.at[1, way], line_send.at[way], line_recv.at[way],
                        {"solver": peer_s(dx % learners), "group": peer_g(dz % groups)}))
            return result

        half_face = face // 2

        def near(i):
            return pl.ds(i * face, points, stride=points)

        def far(i):
            return pl.ds(i * face + last, points, stride=points)

        def pack_z(step, bottoms, tops):
            for part in range(2):
                high_pack = jnp.zeros((points, LANES), F32)
                low_pack = jnp.zeros((points, LANES), F32)
                for i in range(points):
                    high_pack = jnp.where(slot == i, roll(tops[part][i], EY * (i + 1)), high_pack)
                    low_pack = jnp.where(slot == i, roll(bottoms[part][i], EY * i), low_pack)
                zs_ref[step, 0, part] = high_pack
                zs_ref[step, 1, part] = low_pack

        def pack_x(step, u):
            upper = u[1, pl.ds(nodes - face, face), :]
            xs_ref[step, 0] = jnp.where(low_half, roll(upper[:half_face], half), upper[half_face:])
            lower = u[0, pl.ds(0, face), :]
            xs_ref[step, 1] = jnp.where(low_half, lower[:half_face], roll(lower[half_face:], half))

        def pack_faces(step, u):
            pack_z(step, [[u[part, near(i), :] for i in range(points)] for part in range(2)],
                   [[u[part, far(i), :] for i in range(points)] for part in range(2)])
            pack_x(step, u)

        def send_faces(step):
            every = copies(step)
            for copy in every[4:] + every[2:4] + every[:2]:
                copy.start()

        start = u_ref.at[0]
        for load in loads[:2]:
            load.wait()

        def face_rows(value_of):
            rows = jnp.concatenate([value_of(i) for i in range(points)], axis=0)
            return jnp.concatenate([rows, rows], axis=0).astype(BF16)

        def plane(i, j):
            at = pl.ds(i * face + j * points, points)
            return jnp.concatenate([start[0, at, :], start[1, at, :]], axis=1)

        def slope(i):
            total = None
            for j in range(points):
                term = first_row[j] * plane(i, j)
                total = term if total is None else total + term
            return STRESS_SCALE * total

        wall_rows = lax.broadcasted_iota(jnp.int32, (walls, elements), 0)
        wall_cols = lax.broadcasted_iota(jnp.int32, (walls, elements), 1)
        wall_at = (
            lax.rem(wall_rows // 2, EXL) * EZL + wall_rows // (2 * EXL) * 2 + lax.rem(wall_rows, 2))
        select = (wall_cols == wall_at * EY).astype(F32).astype(BF16)
        for j in range(points):
            turn_ref[pl.ds(j * walls, walls), :] = lax.dot_general(
                select, face_rows(lambda i: plane(i, j)), contract, preferred_element_type=F32)
        turn_ref[pl.ds(points * walls, walls), :] = lax.dot_general(
            select, face_rows(slope), contract, preferred_element_type=F32)
        for row in range(lane_rows):
            even = turn_ref[pl.ds(2 * row, points, stride=walls), :]
            odd = turn_ref[pl.ds(2 * row + 1, points, stride=walls), :]
            feat_ref[row // 2, :, pl.ds((row % 2) * LANES, LANES)] = jnp.where(low_half, even, odd)
        target = jnp.where(
            low_half,
            turn_ref[pl.ds(points * walls, lane_rows, stride=2), :],
            turn_ref[pl.ds(points * walls + 1, lane_rows, stride=2), :],
        )

        pack_faces(0, start)
        pl.semaphore_wait(barrier, learners + groups + 2)
        for offset in range(1, learners):
            remote(count_ref.at[me], count_ref.at[me], count_send.at[offset], count_recv.at[me],
                   {"solver": peer_s(offset)}).start()
        send_faces(0)

        def network(turned, learn):
            def one(pair, carry):
                before = jnp.dot(turned, feat_ref[pair].astype(BF16), preferred_element_type=F32)
                hidden = jnp.maximum(before, 0.0)
                if learn:
                    mask_ref[pair] = jnp.where(before > 0.0, 1.0, 0.0).astype(BF16)
                    mixed = jnp.dot(
                        hidden.astype(BF16), graph, preferred_element_type=F32).astype(BF16)
                    mixed_ref[pair] = mixed
                    hidden = mixed.astype(F32)
                weight = w2_ref[...]
                z_ref[pl.ds(2 * pair, 1), :] = jnp.sum(
                    hidden[:, :LANES] * weight, axis=0, keepdims=True)
                z_ref[pl.ds(2 * pair + 1, 1), :] = jnp.sum(
                    hidden[:, LANES:] * weight, axis=0, keepdims=True)
                return carry

            lax.fori_loop(0, pairs, one, 0, unroll=pairs)
            return z_ref[...]

        output = network(turned, True)

        for offset in range(1, learners):
            origin = peer_s(offset)
            remote(count_ref.at[me], count_ref.at[origin], count_send.at[offset],
                   count_recv.at[origin], {"solver": origin}).wait_recv()
        counts = count_ref[0]
        for other in range(1, learners):
            counts = counts + count_ref[other]
        inverse = 1.0 / (jnp.maximum(counts, 1.0) * devices)
        difference = output - target
        error = jnp.zeros((lane_rows, LANES), F32)
        for learner in range(learners):
            single = (difference * inverse[learner:learner + 1]).astype(BF16).astype(F32)
            error = error + times[learner] * single
        e_ref[...] = error
        g_ref[...] = through_graph(error, 1)

        def split(value):
            upper = value.astype(BF16).astype(F32)
            return jnp.concatenate([upper, value - upper], axis=0).astype(BF16)

        def row_pair(ref, pair):
            return jnp.concatenate([ref[pl.ds(2 * pair, 1), :], ref[pl.ds(2 * pair + 1, 1), :]], axis=1)

        moment = None
        for pair in range(pairs):
            term = lax.dot_general(
                split(feat_ref[pair] * row_pair(g_ref, pair)), mask_ref[pair], contract,
                preferred_element_type=F32)
            moment = term if moment is None else moment + term
        moment = moment[0:points] + moment[points:2 * points]
        error_rows = [
            jnp.broadcast_to(e_ref[pl.ds(row, 1), :], (16, LANES)) for row in range(lane_rows)
        ]
        for t in range(owners):
            blocks = []
            for at in range(t * owned, (t + 1) * owned, 16):
                total = None
                for row in range(lane_rows):
                    mixed = mixed_ref[
                        row // 2, pl.ds(at, 16), pl.ds(row % 2 * LANES, LANES)].astype(F32)
                    total = mixed * error_rows[row] if total is None else (
                        total + mixed * error_rows[row])
                blocks.append(total)
            turned = jnp.transpose(jnp.concatenate(blocks, axis=0))
            tile_ref[t, pl.ds(points, 1), :] = jnp.sum(turned, axis=0, keepdims=True)
            tile_ref[t, pl.ds(0, points), :] = moment[:, t * owned:(t + 1) * owned]

        def when_owner(which, action):
            if owners == learners:
                action()
            else:
                pl.when(which < owners)(action)

        def clamp(which):
            return which if owners == learners else jnp.minimum(which, owners - 1)

        def part_copy(offset):
            where = peer_s(offset)
            return where, remote(tile_ref.at[clamp(where)], part_ref.at[me], part_send.at[offset],
                                 part_recv.at[me], {"solver": where})

        for offset in range(1, learners):
            where, copy = part_copy(offset)
            when_owner(where, copy.start)

        def local(source, target):
            u = jnp.concatenate([source[0], source[1]], axis=1)
            upper = u.astype(BF16)
            lower = (u - upper.astype(F32)).astype(BF16)
            u = u + (
                jnp.dot(high_ref[...], upper, preferred_element_type=F32)
                + jnp.dot(high_ref[...], lower, preferred_element_type=F32)
                + jnp.dot(low_ref[...], upper, preferred_element_type=F32)
            )
            for part in range(2):
                target[part] = u[:, part * LANES:(part + 1) * LANES]
            for part in range(2):
                for i in range(points):
                    base = i * face
                    bottom = source[part, pl.ds(base, points), :]
                    top = source[part, pl.ds(base + face - points, points), :]
                    below = jnp.where(level == 0, bottom, roll(top, 1))
                    above = jnp.where(level == EY - 1, 0.0, roll(bottom, -1))
                    target[part, pl.ds(base, points), :] += step_gain * below
                    target[part, pl.ds(base + face - points, points), :] += step_gain * above
            low0 = roll(source[0, pl.ds(nodes - face, face), :], half)
            low1 = roll(source[1, pl.ds(nodes - face, face), :], half)
            target[0, pl.ds(0, face), :] += step_gain_x * jnp.where(low_half, 0.0, low0)
            target[1, pl.ds(0, face), :] += step_gain_x * jnp.where(low_half, low0, low1)
            high0 = roll(source[0, pl.ds(0, face), :], half)
            high1 = roll(source[1, pl.ds(0, face), :], half)
            target[0, pl.ds(nodes - face, face), :] += step_gain * jnp.where(low_half, high0, high1)
            target[1, pl.ds(nodes - face, face), :] += step_gain * jnp.where(low_half, high1, 0.0)
            for part in range(2):
                for i in range(points):
                    before = jnp.where(slot == 0, 0.0, roll(source[part, far(i), :], EY))
                    after = jnp.where(slot == EZL - 1, 0.0, roll(source[part, near(i), :], -EY))
                    target[part, near(i), :] = target[part, near(i), :] + step_gain * before
                    target[part, far(i), :] = target[part, far(i), :] + step_gain * after

        def reflect():
            before, after = fused, fused + 1
            xr_ref[after, 1] += step_gain_x * xs_ref[before, 0]
            xr_ref[after, 0] += step_gain * xs_ref[before, 1]
            for part in range(2):
                zr_ref[after, 1, part] += step_gain * roll(zs_ref[before, 0, part], half)
                zr_ref[after, 0, part] += step_gain * roll(zs_ref[before, 1, part], half)
            group_at = lane // EY
            end = EZL - 1
            for way, (dx, dz) in enumerate(corners):
                tile = line_ref[1, way]
                held_at = (EZL if dx == 1 else 0) + (end if dz == 1 else 0)

                def to(group):
                    return jnp.where(group_at == group, roll(tile, (group - held_at) * EY), 0.0)

                first_half = 0 if dz == 1 else end
                side, rows = (0 if dx == 1 else 1), pl.ds(0 if dz == 1 else last, points // 2, stride=points)
                xr_ref[after, side, rows, :] = xr_ref[after, side, rows, :] + step_gain * (
                    to(first_half)[:points // 2] + to(EZL + first_half)[points // 2:])
                if dx == 1:
                    part, rate, group = 0, step_gain_x, 0
                else:
                    part, rate, group = 1, step_gain, 2 * EZL - 1
                if dz == 1:
                    group = (group + EZL) % (2 * EZL)
                zr_ref[after, 0 if dz == 1 else 1, part] += rate * to(group)

        def halo(step, target):
            every = copies(step) if step <= fused else []
            for copy in every:
                copy.wait_recv()
            ghost = xr_ref[step, 0]
            ghost = jnp.concatenate([ghost, roll(ghost, half)], axis=0)
            target[0, pl.ds(0, face), :] += step_gain_x * jnp.where(low_half, ghost, 0.0)
            ghost = xr_ref[step, 1]
            ghost = jnp.concatenate([roll(ghost, half), ghost], axis=0)
            target[1, pl.ds(nodes - face, face), :] += step_gain * jnp.where(low_half, 0.0, ghost)
            bottoms, tops = [], []
            for part in range(2):
                before_pack = step_gain * zr_ref[step, 0, part]
                after_pack = step_gain * zr_ref[step, 1, part]
                for i in range(points):
                    before = jnp.where(slot == 0, roll(before_pack, half - EY * i), 0.0)
                    after = jnp.where(
                        slot == EZL - 1, roll(after_pack, EY * (EZL - 1 - i)), 0.0)
                    bottoms.append(target[part, near(i), :] + before)
                    tops.append(target[part, far(i), :] + after)
                    target[part, near(i), :] = bottoms[-1]
                    target[part, far(i), :] = tops[-1]
            if step == fused:
                reflect()
            if step < fused:
                pack_z(step + 1, [bottoms[:points], bottoms[points:]], [tops[:points], tops[points:]])
                pack_x(step + 1, target)
                if step + 1 == fused:
                    beyond = held[step % 2]
                    local(target, beyond)
                    pack_faces(step + 2, beyond)
                    for way, (dx, dz) in enumerate(corners):
                        part, i = (1, last) if dx == 1 else (0, 0)
                        line_ref[0, way] = target[part, far(i) if dz == 1 else near(i), :]
                send_faces(step + 1)

        place_ref[...] = jnp.zeros_like(place_ref)
        for load in loads[2:]:
            load.wait()
        held = [start, u_ref.at[1]]

        def flow(step):
            source, target = held[step % 2], held[(step + 1) % 2]
            if step != fused:
                local(source, target)
            halo(step, target)

        flow(0)

        def reduce_part():
            total = tile_ref[clamp(me)]
            for offset in range(1, learners):
                origin = peer_s(offset)
                remote(tile_ref.at[0], part_ref.at[origin], part_send.at[offset],
                       part_recv.at[origin], {"solver": origin}).wait_recv()
            for offset in range(1, learners):
                total = total + part_ref[peer_s(offset)]
            cross_ref[mine] = total
            for offset in range(1, groups):
                remote(cross_ref.at[mine], cross_ref.at[mine], cross_send.at[offset],
                       cross_recv.at[mine], {"group": peer_g(offset)}).start()

        def reduce_cross():
            for offset in range(1, groups):
                origin = peer_g(offset)
                remote(cross_ref.at[mine], cross_ref.at[origin], cross_send.at[offset],
                       cross_recv.at[origin], {"group": origin}).wait_recv()
            total = cross_ref[0]
            for origin in range(1, groups):
                total = total + cross_ref[origin]
            at = clamp(me)
            total_ref[at] = total
            for offset in range(1, learners):
                remote(total_ref.at[at], total_ref.at[at], total_send.at[offset],
                       total_recv.at[at], {"solver": peer_s(offset)}).start()

        when_owner(me, reduce_part)
        flow(1)
        when_owner(me, reduce_cross)
        flow(2)
        for offset in range(1, learners):
            origin = peer_s(offset)
            at = clamp(origin)
            copy = remote(total_ref.at[at], total_ref.at[at], total_send.at[offset],
                          total_recv.at[at], {"solver": origin})
            when_owner(origin, copy.wait_recv)

        sums = jnp.concatenate([total_ref[t] for t in range(owners)], axis=1)
        new_first = (first - LEARN_RATE * (sums[0:points] * second)).astype(BF16)
        new_second = (second - LEARN_RATE * sums[points:points + 1]).astype(BF16)
        new_first_ref[...] = new_first
        new_second_ref[...] = new_second
        updates = [
            pltpu.make_async_copy(new_first_ref, new_first_hbm, out_sem.at[points // 2]),
            pltpu.make_async_copy(new_second_ref, new_second_hbm, out_sem.at[points // 2 + 1]),
        ]
        for copy in updates:
            copy.start()

        middle = pl.ds(lane_rows // 2, lane_rows)
        plain = network(prepare(new_first.astype(F32), new_second.astype(F32)), False)
        stress_ref[1, middle, :] = through_graph(plain, 0)
        stress_copies = []
        for way, (dx, dz) in enumerate(around):
            rows = {
                0: (middle, middle),
                1: (pl.ds(lane_rows, lane_rows // 2), pl.ds(0, lane_rows // 2)),
                -1: (pl.ds(lane_rows // 2, lane_rows // 2), pl.ds(3 * lane_rows // 2, lane_rows // 2)),
            }[dz]
            stress_copies.append(remote(
                stress_ref.at[1, rows[0]], stress_ref.at[1 - dx, rows[1]],
                stress_send.at[way], stress_recv.at[way],
                {"solver": peer_s(dx % learners), "group": peer_g(dz % groups)}))
        for copy in stress_copies:
            copy.start()
        for step in range(3, FLOW_STEPS):
            flow(step)
        for copy in stress_copies:
            copy.wait_recv()

        def halves(value):
            upper = value.astype(BF16)
            return upper, (value - upper.astype(F32)).astype(BF16)

        within = lax.rem(lane, face) // points
        sub = lax.broadcasted_iota(jnp.int32, (points, LANES), 0)
        own_row = within == sub
        for q in range(EZL):
            for e in range(0, 3 * EXL, 2):
                blocks = []
                for at in (e, e + 1):
                    row = stress_ref[at // EXL, pl.ds(q * EXL + at % EXL, 1), :]
                    blocks.append(jnp.where(own_row, jnp.broadcast_to(row, (points, LANES)), 0.0))
                upper, lower = halves(jnp.concatenate(blocks, axis=0))
                columns = pl.ds(q * LANES, LANES)
                place_ref[pl.ds(e * points, 2 * points), columns] = upper
                place_ref[pl.ds(LANES + e * points, 2 * points), columns] = lower
        both = lax.dot_general(
            gather_ref[...], place_ref[...], contract, preferred_element_type=F32)
        upper, lower = halves(both[:, :LANES] + both[:, LANES:])
        ladder = jnp.dot(
            zleft_ref[...], jnp.concatenate([upper, lower, upper], axis=0),
            preferred_element_type=F32)
        z_points = EZL * points
        upper, lower = halves(jnp.concatenate(
            [ladder[c * z_points:(c + 1) * z_points] for c in range(reach + 1)], axis=1))
        plane_t = jnp.dot(
            jnp.concatenate([upper, lower, upper], axis=1), xright_ref[...],
            preferred_element_type=F32)
        span = EXL * points
        per = LANES // span
        quarter = lane // span
        rows = []
        for m in range(reach + 1):
            sides = []
            for t in range(EZL // per):
                value = None
                for e in range(per):
                    z_at = (t * per + e) * points
                    piece = roll(
                        plane_t[z_at:z_at + points, (m // per) * LANES:(m // per + 1) * LANES],
                        (e - m % per) * span)
                    value = piece if value is None else jnp.where(quarter == e, piece, value)
                sides.append(value)
            value = jnp.concatenate(sides, axis=1)
            upper = value.astype(BF16).astype(F32)
            value = jnp.concatenate([upper, value - upper], axis=1)
            node = lax.rem(lax.broadcasted_iota(jnp.int32, value.shape, 1), points)
            rows += [jnp.where(node == i, value, 0.0) for i in range(points)]
        plane_ref[...] = jnp.dot(
            jnp.concatenate(rows, axis=0).astype(BF16), spread_ref[...],
            preferred_element_type=F32)
        ended = held[FLOW_STEPS % 2]
        results = []
        for i in range(points):
            for part in range(2):
                columns = slice(part * LANES, (part + 1) * LANES)
                planes = [
                    plane_ref[pl.ds((m * points + i) * points, points), columns]
                    for m in range(reach + 1)
                ]
                for j in range(points):
                    at = pl.ds(i * face + j * points, points)
                    value = ended[part, at, :]
                    for m in range(reach + 1):
                        value = value + (
                            weights_ref[pl.ds((m * points + j) * points, points), :] * planes[m])
                    result_ref[at, columns] = value
            if i % 2:
                rows = pl.ds((i - 1) * face, 2 * face)
                results.append(pltpu.make_async_copy(
                    result_ref.at[rows], out_ref.at[rows], out_sem.at[i // 2]))
                results[-1].start()

        for offset in range(1, learners):
            remote(count_ref.at[me], count_ref.at[me], count_send.at[offset], count_recv.at[me],
                   {"solver": peer_s(offset)}).wait_send()
            where, copy = part_copy(offset)
            when_owner(where, copy.wait_send)

        def drain_owned():
            at = clamp(me)
            for offset in range(1, groups):
                remote(cross_ref.at[mine], cross_ref.at[mine], cross_send.at[offset],
                       cross_recv.at[mine], {"group": peer_g(offset)}).wait_send()
            for offset in range(1, learners):
                remote(total_ref.at[at], total_ref.at[at], total_send.at[offset],
                       total_recv.at[at], {"solver": peer_s(offset)}).wait_send()

        when_owner(me, drain_owned)
        for copy in results + updates:
            copy.wait()
        for copy in stress_copies:
            copy.wait_send()
        for step in range(fused + 1):
            for copy in copies(step):
                copy.wait_send()

    dma = pltpu.SemaphoreType.DMA
    scratch = [
        pltpu.VMEM((points, width), BF16),
        pltpu.VMEM((1, width), BF16),
        pltpu.VMEM(small_shapes[0], jnp.int32),
        pltpu.VMEM(small_shapes[1], jnp.int32),
        pltpu.VMEM(small_shapes[2], jnp.int32),
        pltpu.VMEM((points, width), BF16),
        pltpu.VMEM((1, width), BF16),
        pltpu.VMEM((2, 2, nodes, LANES), F32),
        pltpu.VMEM((nodes, nodes), BF16),
        pltpu.VMEM((nodes, nodes), BF16),
        *[pltpu.VMEM(table.shape, table.dtype) for table in tables],
        pltpu.VMEM((nodes, elements), F32),
        pltpu.VMEM((pairs, width, 2 * LANES), BF16),
        pltpu.VMEM((pairs, width, 2 * LANES), BF16),
        pltpu.VMEM((pairs, points, 2 * LANES), F32),
        pltpu.VMEM((points * walls + walls, LANES), F32),
        pltpu.VMEM((lane_rows, LANES), F32),
        pltpu.VMEM((lane_rows, LANES), F32),
        pltpu.VMEM((lane_rows, LANES), F32),
        pltpu.VMEM((width, LANES), F32),
        pltpu.VMEM((learners, learners, LANES), F32),
        pltpu.VMEM((owners, rows_sent, owned), F32),
        pltpu.VMEM((learners, rows_sent, owned), F32),
        pltpu.VMEM((groups, rows_sent, owned), F32),
        pltpu.VMEM((owners, rows_sent, owned), F32),
        pltpu.VMEM((3, 2 * lane_rows, LANES), F32),
        pltpu.VMEM((2 * LANES, EZL * LANES), BF16),
        pltpu.VMEM((FLOW_STEPS * face, 2 * LANES), F32),
        pltpu.VMEM((FLOW_STEPS, 2, face // 2, LANES), F32),
        pltpu.VMEM((FLOW_STEPS, 2, face // 2, LANES), F32),
        pltpu.VMEM((FLOW_STEPS, 2, 2, points, LANES), F32),
        pltpu.VMEM((FLOW_STEPS, 2, 2, points, LANES), F32),
        pltpu.VMEM((2, 4, points, LANES), F32),
        dma((9 + len(tables),)), dma((points // 2 + 2,)),
        dma((learners,)), dma((learners,)), dma((learners,)), dma((learners,)),
        dma((groups,)), dma((groups,)), dma((learners,)), dma((owners,)),
        dma((len(around),)), dma((len(around),)),
        dma((FLOW_STEPS, 2)), dma((FLOW_STEPS, 2)), dma((FLOW_STEPS, 2)), dma((FLOW_STEPS, 2)),
        dma((4,)), dma((4,)),
    ]
    return kernel, scratch


def finish(
    field_ref, first_ref, second_ref, out_ref, new_first_ref, new_second_ref,
    held_ref, held_first_ref, held_second_ref, in_sem, out_sem
):
    size = field_ref.shape[0] // CHUNKS
    ways = [(first_ref, held_first_ref, new_first_ref), (second_ref, held_second_ref, new_second_ref)]
    for chunk in range(CHUNKS):
        rows = pl.ds(chunk * size, size)
        ways.append((field_ref.at[rows], held_ref.at[rows], out_ref.at[rows]))
    loads = [
        pltpu.make_async_copy(way[0], way[1], in_sem.at[at]) for at, way in enumerate(ways)
    ]
    stores = [
        pltpu.make_async_copy(way[1], way[2], out_sem.at[at]) for at, way in enumerate(ways)
    ]
    for copy in loads:
        copy.start()
    for load, store in zip(loads, stores):
        load.wait()
        store.start()
    for copy in stores:
        copy.wait()


def shards(field, first_weight, second_weight, face_edges, sample_index, route):
    points = field.shape[0]
    elements = field.shape[3]
    nodes = points**3
    width = first_weight.shape[1]
    learners = lax.axis_size("solver")
    groups = lax.axis_size("group")
    deriv, end_weight = gll_tables(points)
    gain = 2.0 / end_weight
    high, low = element_operator(deriv, gain)
    tables = response_tables(deriv, gain)
    kernel, scratch = make_kernel(
        learners, groups, points, width, deriv, gain, tables,
        (face_edges.shape, (1, sample_index.size), (1, route.size)))
    hbm = pl.BlockSpec(memory_space=pltpu.HBM)
    new_field, new_first, new_second = pl.pallas_call(
        kernel,
        out_shape=(
            jax.ShapeDtypeStruct((nodes, elements), F32),
            jax.ShapeDtypeStruct(first_weight.shape, BF16),
            jax.ShapeDtypeStruct((1, width), BF16),
        ),
        in_specs=[hbm] * (8 + len(tables)),
        out_specs=(hbm, hbm, hbm),
        scratch_shapes=scratch,
        compiler_params=pltpu.CompilerParams(
            collective_id=0, has_side_effects=True, vmem_limit_bytes=67_043_328
        ),
        name="step",
    )(
        field.reshape(nodes, elements),
        first_weight,
        second_weight.reshape(1, width),
        face_edges,
        sample_index.reshape(1, -1),
        route.reshape(1, -1),
        jnp.asarray(high),
        jnp.asarray(low),
        *[jnp.asarray(table) for table in tables],
    )
    new_field, new_first, new_second = pl.pallas_call(
        finish,
        out_shape=tuple(
            jax.ShapeDtypeStruct(value.shape, value.dtype)
            for value in (new_field, new_first, new_second)),
        in_specs=[hbm, hbm, hbm],
        out_specs=(hbm, hbm, hbm),
        scratch_shapes=[
            pltpu.VMEM((nodes, elements), F32),
            pltpu.VMEM(new_first.shape, BF16),
            pltpu.VMEM(new_second.shape, BF16),
            pltpu.SemaphoreType.DMA((CHUNKS + 2,)),
            pltpu.SemaphoreType.DMA((CHUNKS + 2,)),
        ],
        compiler_params=pltpu.CompilerParams(vmem_limit_bytes=67_043_328),
        name="finish",
    )(new_field, new_first, new_second)
    return (new_field.reshape(field.shape), new_first, new_second.reshape(second_weight.shape))


def solution(mesh):
    return jax.shard_map(
        shards,
        mesh=mesh,
        in_specs=(
            P(None, None, None, ("solver", "group")),
            P(),
            P(),
            P(),
            P(("solver", "group")),
            P(("solver", "group"), None),
        ),
        out_specs=(P(None, None, None, ("solver", "group")), P(), P()),
        check_vma=False,
    )
```

```python
import math

import jax
import jax.numpy as jnp
import numpy as np
from jax import lax
from jax.experimental import pallas as pl
from jax.experimental.pallas import tpu as pltpu
from jax.sharding import PartitionSpec as P

FLOW_STEPS = 5
EXL = 4
EZL = 8
EY = 8

HIGH = lax.Precision.HIGHEST
TIME_STEP = 0.002
VISCOSITY = 0.01
VELOCITY = 1.0
PENALTY = 1.0
STRESS_SCALE = 0.1
LEARN_RATE = 0.05
LANES = 128
CHUNKS = 4
F32 = jnp.float32
BF16 = jnp.bfloat16


def legendre_table(points_x, points):
    table = np.zeros((points_x.shape[0], points))
    table[:, 0] = 1.0
    table[:, 1] = points_x
    for degree in range(2, points):
        table[:, degree] = (
            (2 * degree - 1) * points_x * table[:, degree - 1] - (degree - 1) * table[:, degree - 2]
        ) / degree
    return table


def gll_tables(points):
    order = points - 1
    guess = np.cos(np.pi * np.arange(points) / order)
    for sweep in range(100):
        table = legendre_table(guess, points)
        guess = guess - (guess * table[:, order] - table[:, order - 1]) / (points * table[:, order])
    nodes = guess[::-1]
    values = legendre_table(nodes, points)[:, order]
    matrix = np.zeros((points, points))
    for row in range(points):
        for column in range(points):
            if row != column:
                matrix[row, column] = values[row] / (values[column] * (nodes[row] - nodes[column]))
    matrix[0, 0] = -order * (order + 1) / 4.0
    matrix[order, order] = order * (order + 1) / 4.0
    return matrix.astype(np.float32), 2.0 / (order * (order + 1))


def element_operator(deriv, gain):
    points = deriv.shape[0]
    last = points - 1
    deriv = deriv.astype(np.float64)
    second = 4.0 * VISCOSITY * (deriv @ deriv)
    along_i = -2.0 * VELOCITY * deriv + second
    along_i[0, 0] -= gain * (VELOCITY + PENALTY)
    along_i[last, last] -= gain * PENALTY
    other = second.copy()
    other[0, 0] -= gain * PENALTY
    other[last, last] -= gain * PENALTY
    eye = np.eye(points)
    whole = (
        np.kron(np.kron(along_i, eye), eye)
        + np.kron(np.kron(eye, other), eye)
        + np.kron(np.kron(eye, eye), other)
    )
    whole = (TIME_STEP * whole).astype(np.float32)
    high = whole.astype(jnp.bfloat16)
    low = (whole - high.astype(np.float32)).astype(jnp.bfloat16)
    return high, low


def split_np(value):
    value = value.astype(np.float32)
    high = value.astype(jnp.bfloat16)
    return high, (value - high.astype(np.float32)).astype(jnp.bfloat16)


def chain(local, from_before, from_after, count):
    points = local.shape[0]
    whole = np.kron(np.eye(count), local)
    for e in range(1, count):
        whole[e * points, e * points - 1] += from_before
        whole[e * points - 1, e * points] += from_after
    return whole


def response_tables(deriv, gain):
    points = deriv.shape[0]
    last = points - 1
    reach = FLOW_STEPS - 1
    deriv = deriv.astype(np.float64)
    second = TIME_STEP * 4.0 * VISCOSITY * (deriv @ deriv)
    one = TIME_STEP * gain * PENALTY
    two = TIME_STEP * gain * (VELOCITY + PENALTY)
    x_local = -TIME_STEP * 2.0 * VELOCITY * deriv + second
    x_local[0, 0] -= two
    x_local[last, last] -= one
    z_local = second.copy()
    z_local[0, 0] -= one
    z_local[last, last] -= one
    x_whole = chain(x_local, two, one, 3 * EXL)
    z_whole = np.eye(2 * EZL * points) + chain(z_local, one, one, 2 * EZL)
    y_whole = chain(z_local, one, one, EY)
    y_whole[0, 0] += one
    wide = LANES
    x_points = EXL * points
    z_points = EZL * points
    x_middle = slice(x_points, 2 * x_points)
    z_middle = slice(z_points // 2, z_points // 2 + z_points)
    z_left = np.concatenate(
        [np.linalg.matrix_power(z_whole, c)[z_middle] for c in range(reach + 1)], axis=0)
    x_right = np.zeros((reach + 1, wide, 2 * LANES))
    for m in range(reach + 1):
        for c in range(m + 1):
            power = np.linalg.matrix_power(x_whole, m - c)[x_middle]
            x_right[c, :3 * x_points, m * x_points:(m + 1) * x_points] = (
                math.comb(m, m - c) * power.T)
    x_right = x_right.reshape((reach + 1) * wide, 2 * LANES)
    first = np.zeros(EY * points)
    first[0] = one
    weights = np.zeros((reach + 1, EY * points))
    for m in range(reach + 1):
        value = first.copy()
        for b in range(reach - m + 1):
            weights[m] += math.comb(m + b, b) * value
            value = y_whole @ value
    weights = weights.reshape(reach + 1, EY, points).transpose(0, 2, 1)
    weights = np.tile(weights, (1, 1, LANES // EY))
    weights = np.repeat(weights.reshape(-1, 1, LANES), points, axis=1).reshape(-1, LANES)
    z_high, z_low = split_np(z_left)
    x_high, x_low = split_np(x_right)
    ez, k = np.divmod(np.arange(2 * EZL * points), points)
    q, rest = np.divmod(np.arange(EZL * 2 * points * points), 2 * points * points)
    h, rest = np.divmod(rest, points * points)
    gather = (ez[:, None] == (2 * q + h)[None]) & (k[:, None] == (rest % points)[None])
    row_z, rest = np.divmod(np.arange(EZL * EXL * points), EXL * points)
    row_x = rest // points
    col_x, rest = np.divmod(np.arange(EXL * EZL * EY), EZL * EY)
    col_z = rest // EY
    spread = (row_z[:, None] == col_z[None]) & (row_x[:, None] == col_x[None])
    return (
        gather.astype(jnp.bfloat16),
        np.concatenate([z_high, z_high, z_low], axis=1),
        np.concatenate([x_high, x_low], axis=0),
        np.concatenate([spread, spread], axis=0).astype(jnp.bfloat16),
        weights.astype(np.float32),
    )


def make_kernel(learners, groups, points, width, deriv, gain, tables, small_shapes):
    face = points * points
    last = points - 1
    nodes = face * points
    walls = EXL * EZL
    elements = walls * EY
    pairs = walls * face // (2 * LANES)
    owners = min(learners, width // LANES)
    owned = width // owners
    devices = learners * groups
    block = EZL * EY
    half = LANES // 2
    step_gain = float(TIME_STEP * gain * PENALTY)
    step_gain_x = float(TIME_STEP * gain * (VELOCITY + PENALTY))
    first_row = [float(value) for value in deriv[0]]

    def roll(value, shift):
        shift = shift % LANES
        return value if shift == 0 else pltpu.roll(value, shift, 1)

    rows_sent = points + 1
    reach = FLOW_STEPS - 1
    fused = FLOW_STEPS - 2
    corners = [(dx, dz) for dx in (1, -1) for dz in (1, -1)]
    around = [(dx, dz) for dz in (1, -1, 0) for dx in (1, -1, 0) if dx or dz]
    lane_rows = walls * face // LANES

    def kernel(
        field_ref, first_hbm, second_hbm, edges_hbm, index_hbm, route_hbm, high_hbm, low_hbm,
        gather_hbm, zleft_hbm, xright_hbm, spread_hbm, weights_hbm,
        out_ref, new_first_hbm, new_second_hbm,
        first_ref, second_ref, edges_ref, index_ref, route_ref, new_first_ref, new_second_ref,
        u_ref, high_ref, low_ref, gather_ref, zleft_ref, xright_ref, spread_ref, weights_ref,
        result_ref, mask_ref, mixed_ref, feat_ref, feats_ref, turn_ref, z_ref, g_ref, e_ref, w2_ref,
        count_ref, tile_ref, part_ref, cross_ref, total_ref, stress_ref, place_ref, plane_ref,
        xs_ref, xr_ref, zs_ref, zr_ref, line_ref,
        load_sem, out_sem, count_send, count_recv, part_send, part_recv, cross_send, cross_recv,
        total_send, total_recv, stress_send, stress_recv, xs_send, xr_recv, zs_send, zr_recv,
        line_send, line_recv,
    ):
        me = lax.axis_index("solver")
        mine = lax.axis_index("group")

        def peer_s(offset):
            return lax.rem(me + offset, learners)

        def peer_g(offset):
            return lax.rem(mine + offset, groups)

        loads = [
            pltpu.make_async_copy(
                field_ref.at[:, pl.ds(part * LANES, LANES)], u_ref.at[0, part], load_sem.at[part])
            for part in range(2)
        ]
        loads.append(pltpu.make_async_copy(high_hbm, high_ref, load_sem.at[2]))
        loads.append(pltpu.make_async_copy(low_hbm, low_ref, load_sem.at[3]))
        for at, (table, held_table) in enumerate((
            (gather_hbm, gather_ref), (zleft_hbm, zleft_ref), (xright_hbm, xright_ref),
            (spread_hbm, spread_ref), (weights_hbm, weights_ref),
        )):
            loads.append(pltpu.make_async_copy(table, held_table, load_sem.at[4 + at]))
        small_loads = [
            pltpu.make_async_copy(array, held_array, load_sem.at[4 + len(tables) + at])
            for at, (array, held_array) in enumerate((
                (edges_hbm, edges_ref), (route_hbm, route_ref), (first_hbm, first_ref),
                (second_hbm, second_ref), (index_hbm, index_ref),
            ))
        ]
        for load in loads[:2] + small_loads + loads[2:]:
            load.start()

        barrier = pltpu.get_barrier_semaphore()
        for offset in range(1, learners):
            pl.semaphore_signal(
                barrier, inc=1, device_id={"solver": peer_s(offset)},
                device_id_type=pl.DeviceIdType.MESH,
            )
        for offset in range(1, groups):
            pl.semaphore_signal(
                barrier, inc=1, device_id={"group": peer_g(offset)},
                device_id_type=pl.DeviceIdType.MESH,
            )
        for dx, dz in around:
            if dx and dz:
                pl.semaphore_signal(
                    barrier, inc=1,
                    device_id={"solver": peer_s(dx % learners), "group": peer_g(dz % groups)},
                    device_id_type=pl.DeviceIdType.MESH,
                )

        def remote(source, target, send, recv, where):
            return pltpu.make_async_remote_copy(
                src_ref=source, dst_ref=target, send_sem=send, recv_sem=recv,
                device_id=where, device_id_type=pl.DeviceIdType.MESH,
            )

        lane = lax.broadcasted_iota(jnp.int32, (1, LANES), 1)
        low_half = lane < half
        slot = lax.rem(lane, block) // EY
        level = lax.rem(lane, EY)
        contract = (((1,), (1,)), ((), ()))

        for load in small_loads:
            load.wait()
        learner_rows = lax.broadcasted_iota(jnp.int32, (learners, route_ref.shape[1]), 0)
        hits = (route_ref[...] == learner_rows).astype(F32)
        count_ref[me] = jnp.broadcast_to(jnp.sum(hits, axis=1, keepdims=True), (learners, LANES))

        big = 2 * LANES
        edge_rows = lax.rem(
            lax.broadcasted_iota(jnp.int32, (big, edges_ref.shape[1]), 0), face)
        source = (edges_ref[0:1, :] == edge_rows).astype(F32).astype(BF16)
        sink = (edges_ref[1:2, :] == edge_rows).astype(F32).astype(BF16)
        node_rows = lax.broadcasted_iota(jnp.int32, (big, big), 0)
        node_cols = lax.broadcasted_iota(jnp.int32, (big, big), 1)
        graph = 0.25 * lax.dot_general(source, sink, contract, preferred_element_type=F32)
        graph = jnp.where(node_rows // face == node_cols // face, graph, 0.0)
        graph = graph + (node_rows == node_cols).astype(F32)
        graph = graph.astype(BF16)
        small = graph[:LANES, :LANES]
        first = first_ref[...].astype(F32)
        second = second_ref[...].astype(F32)
        places = 2 * lax.broadcasted_iota(jnp.int32, (lane_rows, index_ref.shape[1]), 0)
        taken = index_ref[...]
        taken = 2 * (lax.rem(taken, EZL) // 2 * EXL + taken // EZL) + lax.rem(taken, 2)
        chosen = (taken == places).astype(F32)
        even = lax.dot_general(chosen, hits, contract, preferred_element_type=F32)
        chosen = (taken == places + 1).astype(F32)
        odd = lax.dot_general(chosen, hits, contract, preferred_element_type=F32)
        times = [
            jnp.where(low_half, even[:, learner:learner + 1], odd[:, learner:learner + 1])
            for learner in range(learners)
        ]

        def prepare(first, second):
            padding = jnp.zeros((LANES - points - 1, width), F32)
            both = jnp.transpose(jnp.concatenate([first, second, padding], axis=0))
            w2_ref[...] = jnp.broadcast_to(both[:, points:points + 1], (width, LANES))
            return both.astype(BF16)

        turned = prepare(first, second)
        feats_ref[...] = jnp.zeros_like(feats_ref)

        def through_graph(value, axis):
            pieces = []
            for piece in range(3):
                pieces.append(value.astype(BF16))
                value = value - pieces[-1].astype(F32)
            result = lax.dot_general(
                jnp.concatenate(pieces, axis=0), small, (((1,), (axis,)), ((), ())),
                preferred_element_type=F32)
            return result[:lane_rows] + result[lane_rows:2 * lane_rows] + result[2 * lane_rows:]


        def copies(step):
            right, left = {"solver": peer_s(1)}, {"solver": peer_s(learners - 1)}
            up, down = {"group": peer_g(1)}, {"group": peer_g(groups - 1)}
            result = []
            at = step if step < fused else pl.ds(fused, 2)
            for side, where in ((0, right), (1, left)):
                result.append(remote(
                    xs_ref.at[at, side], xr_ref.at[at, side],
                    xs_send.at[step, side], xr_recv.at[step, side], where))
            for side, where in ((0, up), (1, down)):
                result.append(remote(
                    zs_ref.at[at, side], zr_ref.at[at, side],
                    zs_send.at[step, side], zr_recv.at[step, side], where))
            if step == fused:
                for way, (dx, dz) in enumerate(corners):
                    result.append(remote(
                        line_ref.at[0, way], line_ref.at[1, way], line_send.at[way], line_recv.at[way],
                        {"solver": peer_s(dx % learners), "group": peer_g(dz % groups)}))
            return result

        half_face = face // 2

        def near(i):
            return pl.ds(i * face, points, stride=points)

        def far(i):
            return pl.ds(i * face + last, points, stride=points)

        def pack_z(step, bottoms, tops):
            for part in range(2):
                high_pack = jnp.zeros((points, LANES), F32)
                low_pack = jnp.zeros((points, LANES), F32)
                for i in range(points):
                    high_pack = jnp.where(slot == i, roll(tops[part][i], EY * (i + 1)), high_pack)
                    low_pack = jnp.where(slot == i, roll(bottoms[part][i], EY * i), low_pack)
                zs_ref[step, 0, part] = high_pack
                zs_ref[step, 1, part] = low_pack

        def pack_x(step, u):
            upper = u[1, pl.ds(nodes - face, face), :]
            xs_ref[step, 0] = jnp.where(low_half, roll(upper[:half_face], half), upper[half_face:])
            lower = u[0, pl.ds(0, face), :]
            xs_ref[step, 1] = jnp.where(low_half, lower[:half_face], roll(lower[half_face:], half))

        def pack_faces(step, u):
            pack_z(step, [[u[part, near(i), :] for i in range(points)] for part in range(2)],
                   [[u[part, far(i), :] for i in range(points)] for part in range(2)])
            pack_x(step, u)

        def send_faces(step):
            every = copies(step)
            for copy in every[4:] + every[2:4] + every[:2]:
                copy.start()

        start = u_ref.at[0]
        for load in loads[:2]:
            load.wait()

        def face_rows(value_of):
            rows = jnp.concatenate([value_of(i) for i in range(points)], axis=0)
            return jnp.concatenate([rows, rows], axis=0).astype(BF16)

        def plane(i, j):
            at = pl.ds(i * face + j * points, points)
            return jnp.concatenate([start[0, at, :], start[1, at, :]], axis=1)

        def slope(i):
            total = None
            for j in range(points):
                term = first_row[j] * plane(i, j)
                total = term if total is None else total + term
            return STRESS_SCALE * total

        wall_rows = lax.broadcasted_iota(jnp.int32, (walls, elements), 0)
        wall_cols = lax.broadcasted_iota(jnp.int32, (walls, elements), 1)
        wall_at = (
            lax.rem(wall_rows // 2, EXL) * EZL + wall_rows // (2 * EXL) * 2 + lax.rem(wall_rows, 2))
        select = (wall_cols == wall_at * EY).astype(F32).astype(BF16)
        for j in range(points):
            turn_ref[pl.ds(j * walls, walls), :] = lax.dot_general(
                select, face_rows(lambda i: plane(i, j)), contract, preferred_element_type=F32)
        turn_ref[pl.ds(points * walls, walls), :] = lax.dot_general(
            select, face_rows(slope), contract, preferred_element_type=F32)
        for row in range(lane_rows):
            even = turn_ref[pl.ds(2 * row, points, stride=walls), :]
            odd = turn_ref[pl.ds(2 * row + 1, points, stride=walls), :]
            feat_ref[row // 2, :, pl.ds((row % 2) * LANES, LANES)] = jnp.where(low_half, even, odd)
        for pair in range(pairs):
            feats_ref[pair, pl.ds(0, 2 * points), :] = jnp.concatenate(
                [feat_ref[pair], jnp.zeros((points, 2 * LANES), F32)], axis=0).astype(BF16)
        target = jnp.where(
            low_half,
            turn_ref[pl.ds(points * walls, lane_rows, stride=2), :],
            turn_ref[pl.ds(points * walls + 1, lane_rows, stride=2), :],
        )

        pack_faces(0, start)
        pl.semaphore_wait(barrier, learners + groups + 2)
        for offset in range(1, learners):
            remote(count_ref.at[me], count_ref.at[me], count_send.at[offset], count_recv.at[me],
                   {"solver": peer_s(offset)}).start()
        send_faces(0)

        def network(turned, learn):
            def one(pair, carry):
                before = jnp.dot(turned, feats_ref[pair], preferred_element_type=F32)
                hidden = jnp.maximum(before, 0.0)
                if learn:
                    mask_ref[pair] = jnp.where(before > 0.0, 1.0, 0.0).astype(BF16)
                    mixed = jnp.dot(
                        hidden.astype(BF16), graph, preferred_element_type=F32).astype(BF16)
                    mixed_ref[pair] = mixed
                    hidden = mixed.astype(F32)
                weight = w2_ref[...]
                z_ref[pl.ds(2 * pair, 1), :] = jnp.sum(
                    hidden[:, :LANES] * weight, axis=0, keepdims=True)
                z_ref[pl.ds(2 * pair + 1, 1), :] = jnp.sum(
                    hidden[:, LANES:] * weight, axis=0, keepdims=True)
                return carry

            lax.fori_loop(0, pairs, one, 0, unroll=pairs)
            return z_ref[...]

        output = network(turned, True)

        for offset in range(1, learners):
            origin = peer_s(offset)
            remote(count_ref.at[me], count_ref.at[origin], count_send.at[offset],
                   count_recv.at[origin], {"solver": origin}).wait_recv()
        counts = count_ref[0]
        for other in range(1, learners):
            counts = counts + count_ref[other]
        inverse = 1.0 / (jnp.maximum(counts, 1.0) * devices)
        difference = output - target
        error = jnp.zeros((lane_rows, LANES), F32)
        for learner in range(learners):
            single = (difference * inverse[learner:learner + 1]).astype(BF16).astype(F32)
            error = error + times[learner] * single
        e_ref[...] = error
        g_ref[...] = through_graph(error, 1)

        def split(value):
            upper = value.astype(BF16).astype(F32)
            return jnp.concatenate([upper, value - upper], axis=0).astype(BF16)

        def row_pair(ref, pair):
            return jnp.concatenate([ref[pl.ds(2 * pair, 1), :], ref[pl.ds(2 * pair + 1, 1), :]], axis=1)

        moment = None
        for pair in range(pairs):
            term = lax.dot_general(
                split(feat_ref[pair] * row_pair(g_ref, pair)), mask_ref[pair], contract,
                preferred_element_type=F32)
            moment = term if moment is None else moment + term
        moment = moment[0:points] + moment[points:2 * points]
        error_rows = [
            jnp.broadcast_to(e_ref[pl.ds(row, 1), :], (16, LANES)) for row in range(lane_rows)
        ]
        for t in range(owners):
            blocks = []
            for at in range(t * owned, (t + 1) * owned, 16):
                total = None
                for row in range(lane_rows):
                    mixed = mixed_ref[
                        row // 2, pl.ds(at, 16), pl.ds(row % 2 * LANES, LANES)].astype(F32)
                    total = mixed * error_rows[row] if total is None else (
                        total + mixed * error_rows[row])
                blocks.append(total)
            turned = jnp.transpose(jnp.concatenate(blocks, axis=0))
            tile_ref[t, pl.ds(points, 1), :] = jnp.sum(turned, axis=0, keepdims=True)
            tile_ref[t, pl.ds(0, points), :] = moment[:, t * owned:(t + 1) * owned]

        def when_owner(which, action):
            if owners == learners:
                action()
            else:
                pl.when(which < owners)(action)

        def clamp(which):
            return which if owners == learners else jnp.minimum(which, owners - 1)

        def part_copy(offset):
            where = peer_s(offset)
            return where, remote(tile_ref.at[clamp(where)], part_ref.at[me], part_send.at[offset],
                                 part_recv.at[me], {"solver": where})

        for offset in range(1, learners):
            where, copy = part_copy(offset)
            when_owner(where, copy.start)

        def local(source, target):
            u = jnp.concatenate([source[0], source[1]], axis=1)
            upper = u.astype(BF16)
            lower = (u - upper.astype(F32)).astype(BF16)
            u = u + (
                jnp.dot(high_ref[...], upper, preferred_element_type=F32)
                + jnp.dot(high_ref[...], lower, preferred_element_type=F32)
                + jnp.dot(low_ref[...], upper, preferred_element_type=F32)
            )
            for part in range(2):
                target[part] = u[:, part * LANES:(part + 1) * LANES]
            for part in range(2):
                for i in range(points):
                    base = i * face
                    bottom = source[part, pl.ds(base, points), :]
                    top = source[part, pl.ds(base + face - points, points), :]
                    below = jnp.where(level == 0, bottom, roll(top, 1))
                    above = jnp.where(level == EY - 1, 0.0, roll(bottom, -1))
                    target[part, pl.ds(base, points), :] += step_gain * below
                    target[part, pl.ds(base + face - points, points), :] += step_gain * above
            low0 = roll(source[0, pl.ds(nodes - face, face), :], half)
            low1 = roll(source[1, pl.ds(nodes - face, face), :], half)
            target[0, pl.ds(0, face), :] += step_gain_x * jnp.where(low_half, 0.0, low0)
            target[1, pl.ds(0, face), :] += step_gain_x * jnp.where(low_half, low0, low1)
            high0 = roll(source[0, pl.ds(0, face), :], half)
            high1 = roll(source[1, pl.ds(0, face), :], half)
            target[0, pl.ds(nodes - face, face), :] += step_gain * jnp.where(low_half, high0, high1)
            target[1, pl.ds(nodes - face, face), :] += step_gain * jnp.where(low_half, high1, 0.0)
            for part in range(2):
                for i in range(points):
                    before = jnp.where(slot == 0, 0.0, roll(source[part, far(i), :], EY))
                    after = jnp.where(slot == EZL - 1, 0.0, roll(source[part, near(i), :], -EY))
                    target[part, near(i), :] = target[part, near(i), :] + step_gain * before
                    target[part, far(i), :] = target[part, far(i), :] + step_gain * after

        def reflect():
            before, after = fused, fused + 1
            xr_ref[after, 1] += step_gain_x * xs_ref[before, 0]
            xr_ref[after, 0] += step_gain * xs_ref[before, 1]
            for part in range(2):
                zr_ref[after, 1, part] += step_gain * roll(zs_ref[before, 0, part], half)
                zr_ref[after, 0, part] += step_gain * roll(zs_ref[before, 1, part], half)
            group_at = lane // EY
            end = EZL - 1
            for way, (dx, dz) in enumerate(corners):
                tile = line_ref[1, way]
                held_at = (EZL if dx == 1 else 0) + (end if dz == 1 else 0)

                def to(group):
                    return jnp.where(group_at == group, roll(tile, (group - held_at) * EY), 0.0)

                first_half = 0 if dz == 1 else end
                side, rows = (0 if dx == 1 else 1), pl.ds(0 if dz == 1 else last, points // 2, stride=points)
                xr_ref[after, side, rows, :] = xr_ref[after, side, rows, :] + step_gain * (
                    to(first_half)[:points // 2] + to(EZL + first_half)[points // 2:])
                if dx == 1:
                    part, rate, group = 0, step_gain_x, 0
                else:
                    part, rate, group = 1, step_gain, 2 * EZL - 1
                if dz == 1:
                    group = (group + EZL) % (2 * EZL)
                zr_ref[after, 0 if dz == 1 else 1, part] += rate * to(group)

        def halo(step, target):
            every = copies(step) if step <= fused else []
            for copy in every:
                copy.wait_recv()
            ghost = xr_ref[step, 0]
            ghost = jnp.concatenate([ghost, roll(ghost, half)], axis=0)
            target[0, pl.ds(0, face), :] += step_gain_x * jnp.where(low_half, ghost, 0.0)
            ghost = xr_ref[step, 1]
            ghost = jnp.concatenate([roll(ghost, half), ghost], axis=0)
            target[1, pl.ds(nodes - face, face), :] += step_gain * jnp.where(low_half, 0.0, ghost)
            bottoms, tops = [], []
            for part in range(2):
                before_pack = step_gain * zr_ref[step, 0, part]
                after_pack = step_gain * zr_ref[step, 1, part]
                for i in range(points):
                    before = jnp.where(slot == 0, roll(before_pack, half - EY * i), 0.0)
                    after = jnp.where(
                        slot == EZL - 1, roll(after_pack, EY * (EZL - 1 - i)), 0.0)
                    bottoms.append(target[part, near(i), :] + before)
                    tops.append(target[part, far(i), :] + after)
                    target[part, near(i), :] = bottoms[-1]
                    target[part, far(i), :] = tops[-1]
            if step == fused:
                reflect()
            if step < fused:
                pack_z(step + 1, [bottoms[:points], bottoms[points:]], [tops[:points], tops[points:]])
                pack_x(step + 1, target)
                if step + 1 == fused:
                    beyond = held[step % 2]
                    local(target, beyond)
                    pack_faces(step + 2, beyond)
                    for way, (dx, dz) in enumerate(corners):
                        part, i = (1, last) if dx == 1 else (0, 0)
                        line_ref[0, way] = target[part, far(i) if dz == 1 else near(i), :]
                send_faces(step + 1)

        place_ref[...] = jnp.zeros_like(place_ref)
        for load in loads[2:]:
            load.wait()
        held = [start, u_ref.at[1]]

        def flow(step):
            source, target = held[step % 2], held[(step + 1) % 2]
            if step != fused:
                local(source, target)
            halo(step, target)

        flow(0)

        def reduce_part():
            total = tile_ref[clamp(me)]
            for offset in range(1, learners):
                origin = peer_s(offset)
                remote(tile_ref.at[0], part_ref.at[origin], part_send.at[offset],
                       part_recv.at[origin], {"solver": origin}).wait_recv()
            for offset in range(1, learners):
                total = total + part_ref[peer_s(offset)]
            cross_ref[mine] = total
            for offset in range(1, groups):
                remote(cross_ref.at[mine], cross_ref.at[mine], cross_send.at[offset],
                       cross_recv.at[mine], {"group": peer_g(offset)}).start()

        def reduce_cross():
            for offset in range(1, groups):
                origin = peer_g(offset)
                remote(cross_ref.at[mine], cross_ref.at[origin], cross_send.at[offset],
                       cross_recv.at[origin], {"group": origin}).wait_recv()
            total = cross_ref[0]
            for origin in range(1, groups):
                total = total + cross_ref[origin]
            at = clamp(me)
            total_ref[at] = total
            for offset in range(1, learners):
                remote(total_ref.at[at], total_ref.at[at], total_send.at[offset],
                       total_recv.at[at], {"solver": peer_s(offset)}).start()

        when_owner(me, reduce_part)
        flow(1)
        when_owner(me, reduce_cross)
        flow(2)
        for offset in range(1, learners):
            origin = peer_s(offset)
            at = clamp(origin)
            copy = remote(total_ref.at[at], total_ref.at[at], total_send.at[offset],
                          total_recv.at[at], {"solver": origin})
            when_owner(origin, copy.wait_recv)

        sums = jnp.concatenate([total_ref[t] for t in range(owners)], axis=1)
        new_first = (first - LEARN_RATE * (sums[0:points] * second)).astype(BF16)
        new_second = (second - LEARN_RATE * sums[points:points + 1]).astype(BF16)
        new_first_ref[...] = new_first
        new_second_ref[...] = new_second
        updates = [
            pltpu.make_async_copy(new_first_ref, new_first_hbm, out_sem.at[points // 2]),
            pltpu.make_async_copy(new_second_ref, new_second_hbm, out_sem.at[points // 2 + 1]),
        ]
        for copy in updates:
            copy.start()

        middle = pl.ds(lane_rows // 2, lane_rows)
        plain = network(prepare(new_first.astype(F32), new_second.astype(F32)), False)
        stress_ref[1, middle, :] = through_graph(plain, 0)
        stress_copies = []
        for way, (dx, dz) in enumerate(around):
            rows = {
                0: (middle, middle),
                1: (pl.ds(lane_rows, lane_rows // 2), pl.ds(0, lane_rows // 2)),
                -1: (pl.ds(lane_rows // 2, lane_rows // 2), pl.ds(3 * lane_rows // 2, lane_rows // 2)),
            }[dz]
            stress_copies.append(remote(
                stress_ref.at[1, rows[0]], stress_ref.at[1 - dx, rows[1]],
                stress_send.at[way], stress_recv.at[way],
                {"solver": peer_s(dx % learners), "group": peer_g(dz % groups)}))
        for copy in stress_copies:
            copy.start()
        for step in range(3, FLOW_STEPS):
            flow(step)
        for copy in stress_copies:
            copy.wait_recv()

        def halves(value):
            upper = value.astype(BF16)
            return upper, (value - upper.astype(F32)).astype(BF16)

        within = lax.rem(lane, face) // points
        sub = lax.broadcasted_iota(jnp.int32, (points, LANES), 0)
        own_row = within == sub
        for q in range(EZL):
            for e in range(0, 3 * EXL, 2):
                blocks = []
                for at in (e, e + 1):
                    row = stress_ref[at // EXL, pl.ds(q * EXL + at % EXL, 1), :]
                    blocks.append(jnp.where(own_row, jnp.broadcast_to(row, (points, LANES)), 0.0))
                upper, lower = halves(jnp.concatenate(blocks, axis=0))
                columns = pl.ds(q * LANES, LANES)
                place_ref[pl.ds(e * points, 2 * points), columns] = upper
                place_ref[pl.ds(LANES + e * points, 2 * points), columns] = lower
        both = lax.dot_general(
            gather_ref[...], place_ref[...], contract, preferred_element_type=F32)
        upper, lower = halves(both[:, :LANES] + both[:, LANES:])
        ladder = jnp.dot(
            zleft_ref[...], jnp.concatenate([upper, lower, upper], axis=0),
            preferred_element_type=F32)
        z_points = EZL * points
        upper, lower = halves(jnp.concatenate(
            [ladder[c * z_points:(c + 1) * z_points] for c in range(reach + 1)], axis=1))
        depth = (reach + 1) * LANES
        plane_t = jnp.dot(
            jnp.concatenate([upper, lower], axis=0), xright_ref[pl.ds(0, depth), :],
            preferred_element_type=F32)
        plane_t = plane_t[:z_points] + plane_t[z_points:] + jnp.dot(
            upper, xright_ref[pl.ds(depth, depth), :], preferred_element_type=F32)
        span = EXL * points
        per = LANES // span
        quarter = lane // span
        rows = []
        for m in range(reach + 1):
            sides = []
            for t in range(EZL // per):
                value = None
                for e in range(per):
                    z_at = (t * per + e) * points
                    piece = roll(
                        plane_t[z_at:z_at + points, (m // per) * LANES:(m // per + 1) * LANES],
                        (e - m % per) * span)
                    value = piece if value is None else jnp.where(quarter == e, piece, value)
                sides.append(value)
            value = jnp.concatenate(sides, axis=1)
            upper = value.astype(BF16).astype(F32)
            value = jnp.concatenate([upper, value - upper], axis=1)
            node = lax.rem(lax.broadcasted_iota(jnp.int32, value.shape, 1), points)
            rows += [jnp.where(node == i, value, 0.0) for i in range(points)]
        plane_ref[...] = jnp.dot(
            jnp.concatenate(rows, axis=0).astype(BF16), spread_ref[...],
            preferred_element_type=F32)
        ended = held[FLOW_STEPS % 2]
        results = []
        for i in range(points):
            for part in range(2):
                columns = slice(part * LANES, (part + 1) * LANES)
                planes = [
                    plane_ref[pl.ds((m * points + i) * points, points), columns]
                    for m in range(reach + 1)
                ]
                for j in range(points):
                    at = pl.ds(i * face + j * points, points)
                    value = ended[part, at, :]
                    for m in range(reach + 1):
                        value = value + (
                            weights_ref[pl.ds((m * points + j) * points, points), :] * planes[m])
                    result_ref[at, columns] = value
            if i % 2:
                rows = pl.ds((i - 1) * face, 2 * face)
                results.append(pltpu.make_async_copy(
                    result_ref.at[rows], out_ref.at[rows], out_sem.at[i // 2]))
                results[-1].start()

        for offset in range(1, learners):
            remote(count_ref.at[me], count_ref.at[me], count_send.at[offset], count_recv.at[me],
                   {"solver": peer_s(offset)}).wait_send()
            where, copy = part_copy(offset)
            when_owner(where, copy.wait_send)

        def drain_owned():
            at = clamp(me)
            for offset in range(1, groups):
                remote(cross_ref.at[mine], cross_ref.at[mine], cross_send.at[offset],
                       cross_recv.at[mine], {"group": peer_g(offset)}).wait_send()
            for offset in range(1, learners):
                remote(total_ref.at[at], total_ref.at[at], total_send.at[offset],
                       total_recv.at[at], {"solver": peer_s(offset)}).wait_send()

        when_owner(me, drain_owned)
        for copy in results + updates:
            copy.wait()
        for copy in stress_copies:
            copy.wait_send()
        for step in range(fused + 1):
            for copy in copies(step):
                copy.wait_send()

    dma = pltpu.SemaphoreType.DMA
    scratch = [
        pltpu.VMEM((points, width), BF16),
        pltpu.VMEM((1, width), BF16),
        pltpu.VMEM(small_shapes[0], jnp.int32),
        pltpu.VMEM(small_shapes[1], jnp.int32),
        pltpu.VMEM(small_shapes[2], jnp.int32),
        pltpu.VMEM((points, width), BF16),
        pltpu.VMEM((1, width), BF16),
        pltpu.VMEM((2, 2, nodes, LANES), F32),
        pltpu.VMEM((nodes, nodes), BF16),
        pltpu.VMEM((nodes, nodes), BF16),
        *[pltpu.VMEM(table.shape, table.dtype) for table in tables],
        pltpu.VMEM((nodes, elements), F32),
        pltpu.VMEM((pairs, width, 2 * LANES), BF16),
        pltpu.VMEM((pairs, width, 2 * LANES), BF16),
        pltpu.VMEM((pairs, points, 2 * LANES), F32),
        pltpu.VMEM((pairs, LANES, 2 * LANES), BF16),
        pltpu.VMEM((points * walls + walls, LANES), F32),
        pltpu.VMEM((lane_rows, LANES), F32),
        pltpu.VMEM((lane_rows, LANES), F32),
        pltpu.VMEM((lane_rows, LANES), F32),
        pltpu.VMEM((width, LANES), F32),
        pltpu.VMEM((learners, learners, LANES), F32),
        pltpu.VMEM((owners, rows_sent, owned), F32),
        pltpu.VMEM((learners, rows_sent, owned), F32),
        pltpu.VMEM((groups, rows_sent, owned), F32),
        pltpu.VMEM((owners, rows_sent, owned), F32),
        pltpu.VMEM((3, 2 * lane_rows, LANES), F32),
        pltpu.VMEM((2 * LANES, EZL * LANES), BF16),
        pltpu.VMEM((FLOW_STEPS * face, 2 * LANES), F32),
        pltpu.VMEM((FLOW_STEPS, 2, face // 2, LANES), F32),
        pltpu.VMEM((FLOW_STEPS, 2, face // 2, LANES), F32),
        pltpu.VMEM((FLOW_STEPS, 2, 2, points, LANES), F32),
        pltpu.VMEM((FLOW_STEPS, 2, 2, points, LANES), F32),
        pltpu.VMEM((2, 4, points, LANES), F32),
        dma((9 + len(tables),)), dma((points // 2 + 2,)),
        dma((learners,)), dma((learners,)), dma((learners,)), dma((learners,)),
        dma((groups,)), dma((groups,)), dma((learners,)), dma((owners,)),
        dma((len(around),)), dma((len(around),)),
        dma((FLOW_STEPS, 2)), dma((FLOW_STEPS, 2)), dma((FLOW_STEPS, 2)), dma((FLOW_STEPS, 2)),
        dma((4,)), dma((4,)),
    ]
    return kernel, scratch


def finish(
    field_ref, first_ref, second_ref, out_ref, new_first_ref, new_second_ref,
    held_ref, held_first_ref, held_second_ref, in_sem, out_sem
):
    size = field_ref.shape[0] // CHUNKS
    ways = [(first_ref, held_first_ref, new_first_ref), (second_ref, held_second_ref, new_second_ref)]
    for chunk in range(CHUNKS):
        rows = pl.ds(chunk * size, size)
        ways.append((field_ref.at[rows], held_ref.at[rows], out_ref.at[rows]))
    loads = [
        pltpu.make_async_copy(way[0], way[1], in_sem.at[at]) for at, way in enumerate(ways)
    ]
    stores = [
        pltpu.make_async_copy(way[1], way[2], out_sem.at[at]) for at, way in enumerate(ways)
    ]
    for copy in loads:
        copy.start()
    for load, store in zip(loads, stores):
        load.wait()
        store.start()
    for copy in stores:
        copy.wait()


def shards(field, first_weight, second_weight, face_edges, sample_index, route):
    points = field.shape[0]
    elements = field.shape[3]
    nodes = points**3
    width = first_weight.shape[1]
    learners = lax.axis_size("solver")
    groups = lax.axis_size("group")
    deriv, end_weight = gll_tables(points)
    gain = 2.0 / end_weight
    high, low = element_operator(deriv, gain)
    tables = response_tables(deriv, gain)
    kernel, scratch = make_kernel(
        learners, groups, points, width, deriv, gain, tables,
        (face_edges.shape, (1, sample_index.size), (1, route.size)))
    hbm = pl.BlockSpec(memory_space=pltpu.HBM)
    new_field, new_first, new_second = pl.pallas_call(
        kernel,
        out_shape=(
            jax.ShapeDtypeStruct((nodes, elements), F32),
            jax.ShapeDtypeStruct(first_weight.shape, BF16),
            jax.ShapeDtypeStruct((1, width), BF16),
        ),
        in_specs=[hbm] * (8 + len(tables)),
        out_specs=(hbm, hbm, hbm),
        scratch_shapes=scratch,
        compiler_params=pltpu.CompilerParams(
            collective_id=0, has_side_effects=True, vmem_limit_bytes=67_043_328
        ),
        name="step",
    )(
        field.reshape(nodes, elements),
        first_weight,
        second_weight.reshape(1, width),
        face_edges,
        sample_index.reshape(1, -1),
        route.reshape(1, -1),
        jnp.asarray(high),
        jnp.asarray(low),
        *[jnp.asarray(table) for table in tables],
    )
    new_field, new_first, new_second = pl.pallas_call(
        finish,
        out_shape=tuple(
            jax.ShapeDtypeStruct(value.shape, value.dtype)
            for value in (new_field, new_first, new_second)),
        in_specs=[hbm, hbm, hbm],
        out_specs=(hbm, hbm, hbm),
        scratch_shapes=[
            pltpu.VMEM((nodes, elements), F32),
            pltpu.VMEM(new_first.shape, BF16),
            pltpu.VMEM(new_second.shape, BF16),
            pltpu.SemaphoreType.DMA((CHUNKS + 2,)),
            pltpu.SemaphoreType.DMA((CHUNKS + 2,)),
        ],
        compiler_params=pltpu.CompilerParams(vmem_limit_bytes=67_043_328),
        name="finish",
    )(new_field, new_first, new_second)
    return (new_field.reshape(field.shape), new_first, new_second.reshape(second_weight.shape))


def solution(mesh):
    return jax.shard_map(
        shards,
        mesh=mesh,
        in_specs=(
            P(None, None, None, ("solver", "group")),
            P(),
            P(),
            P(),
            P(("solver", "group")),
            P(("solver", "group"), None),
        ),
        out_specs=(P(None, None, None, ("solver", "group")), P(), P()),
        check_vma=False,
    )
```

```python
import functools
import math

import jax
import jax.numpy as jnp
import numpy as np
from jax import lax
from jax.experimental import pallas as pl
from jax.experimental.pallas import tpu as pltpu
from jax.sharding import PartitionSpec as P

FLOW_STEPS = 5
EXL = 4
EZL = 8
EY = 8

HIGH = lax.Precision.HIGHEST
TIME_STEP = 0.002
VISCOSITY = 0.01
VELOCITY = 1.0
PENALTY = 1.0
STRESS_SCALE = 0.1
LEARN_RATE = 0.05
LANES = 128
CHUNKS = 4
F32 = jnp.float32
BF16 = jnp.bfloat16


def legendre_table(points_x, points):
    table = np.zeros((points_x.shape[0], points))
    table[:, 0] = 1.0
    table[:, 1] = points_x
    for degree in range(2, points):
        table[:, degree] = (
            (2 * degree - 1) * points_x * table[:, degree - 1] - (degree - 1) * table[:, degree - 2]
        ) / degree
    return table


def gll_tables(points):
    order = points - 1
    guess = np.cos(np.pi * np.arange(points) / order)
    for sweep in range(100):
        table = legendre_table(guess, points)
        guess = guess - (guess * table[:, order] - table[:, order - 1]) / (points * table[:, order])
    nodes = guess[::-1]
    values = legendre_table(nodes, points)[:, order]
    matrix = np.zeros((points, points))
    for row in range(points):
        for column in range(points):
            if row != column:
                matrix[row, column] = values[row] / (values[column] * (nodes[row] - nodes[column]))
    matrix[0, 0] = -order * (order + 1) / 4.0
    matrix[order, order] = order * (order + 1) / 4.0
    return matrix.astype(np.float32), 2.0 / (order * (order + 1))


def element_operator(deriv, gain):
    points = deriv.shape[0]
    last = points - 1
    deriv = deriv.astype(np.float64)
    second = 4.0 * VISCOSITY * (deriv @ deriv)
    along_i = -2.0 * VELOCITY * deriv + second
    along_i[0, 0] -= gain * (VELOCITY + PENALTY)
    along_i[last, last] -= gain * PENALTY
    other = second.copy()
    other[0, 0] -= gain * PENALTY
    other[last, last] -= gain * PENALTY
    eye = np.eye(points)
    whole = (
        np.kron(np.kron(along_i, eye), eye)
        + np.kron(np.kron(eye, other), eye)
        + np.kron(np.kron(eye, eye), other)
    )
    whole = (TIME_STEP * whole).astype(np.float32)
    high = whole.astype(jnp.bfloat16)
    low = (whole - high.astype(np.float32)).astype(jnp.bfloat16)
    return high, low


def split_np(value):
    value = value.astype(np.float32)
    high = value.astype(jnp.bfloat16)
    return high, (value - high.astype(np.float32)).astype(jnp.bfloat16)


def chain(local, from_before, from_after, count):
    points = local.shape[0]
    whole = np.kron(np.eye(count), local)
    for e in range(1, count):
        whole[e * points, e * points - 1] += from_before
        whole[e * points - 1, e * points] += from_after
    return whole


def response_tables(deriv, gain):
    points = deriv.shape[0]
    last = points - 1
    reach = FLOW_STEPS - 1
    deriv = deriv.astype(np.float64)
    second = TIME_STEP * 4.0 * VISCOSITY * (deriv @ deriv)
    one = TIME_STEP * gain * PENALTY
    two = TIME_STEP * gain * (VELOCITY + PENALTY)
    x_local = -TIME_STEP * 2.0 * VELOCITY * deriv + second
    x_local[0, 0] -= two
    x_local[last, last] -= one
    z_local = second.copy()
    z_local[0, 0] -= one
    z_local[last, last] -= one
    x_whole = chain(x_local, two, one, 3 * EXL)
    z_whole = np.eye(2 * EZL * points) + chain(z_local, one, one, 2 * EZL)
    y_whole = chain(z_local, one, one, EY)
    y_whole[0, 0] += one
    wide = LANES
    x_points = EXL * points
    z_points = EZL * points
    x_middle = slice(x_points, 2 * x_points)
    z_middle = slice(z_points // 2, z_points // 2 + z_points)
    z_left = np.concatenate(
        [np.linalg.matrix_power(z_whole, c)[z_middle] for c in range(reach + 1)], axis=0)
    x_right = np.zeros((reach + 1, wide, 2 * LANES))
    for m in range(reach + 1):
        for c in range(m + 1):
            power = np.linalg.matrix_power(x_whole, m - c)[x_middle]
            x_right[c, :3 * x_points, m * x_points:(m + 1) * x_points] = (
                math.comb(m, m - c) * power.T)
    x_right = x_right.reshape((reach + 1) * wide, 2 * LANES)
    first = np.zeros(EY * points)
    first[0] = one
    weights = np.zeros((reach + 1, EY * points))
    for m in range(reach + 1):
        value = first.copy()
        for b in range(reach - m + 1):
            weights[m] += math.comb(m + b, b) * value
            value = y_whole @ value
    weights = weights.reshape(reach + 1, EY, points).transpose(0, 2, 1)
    weights = np.tile(weights, (1, 1, LANES // EY))
    weights = np.repeat(weights.reshape(-1, 1, LANES), points, axis=1).reshape(-1, LANES)
    z_high, z_low = split_np(z_left)
    x_high, x_low = split_np(x_right)
    ez, k = np.divmod(np.arange(2 * EZL * points), points)
    q, rest = np.divmod(np.arange(EZL * 2 * points * points), 2 * points * points)
    h, rest = np.divmod(rest, points * points)
    gather = (ez[:, None] == (2 * q + h)[None]) & (k[:, None] == (rest % points)[None])
    row_z, rest = np.divmod(np.arange(EZL * EXL * points), EXL * points)
    row_x = rest // points
    col_x, rest = np.divmod(np.arange(EXL * EZL * EY), EZL * EY)
    col_z = rest // EY
    spread = (row_z[:, None] == col_z[None]) & (row_x[:, None] == col_x[None])
    return (
        gather.astype(jnp.bfloat16),
        np.concatenate([z_high, z_high, z_low], axis=1),
        np.concatenate([x_high, x_low], axis=0),
        np.concatenate([spread, spread], axis=0).astype(jnp.bfloat16),
        weights.astype(np.float32),
    )


def make_kernel(learners, groups, points, width, deriv, gain, tables, small_shapes):
    face = points * points
    last = points - 1
    nodes = face * points
    walls = EXL * EZL
    elements = walls * EY
    pairs = walls * face // (2 * LANES)
    owners = min(learners, width // LANES)
    owned = width // owners
    devices = learners * groups
    block = EZL * EY
    half = LANES // 2
    step_gain = float(TIME_STEP * gain * PENALTY)
    step_gain_x = float(TIME_STEP * gain * (VELOCITY + PENALTY))
    first_row = [float(value) for value in deriv[0]]

    def roll(value, shift):
        shift = shift % LANES
        return value if shift == 0 else pltpu.roll(value, shift, 1)

    rows_sent = points + 1
    reach = FLOW_STEPS - 1
    fused = FLOW_STEPS - 2
    corners = [(dx, dz) for dx in (1, -1) for dz in (1, -1)]
    around = [(dx, dz) for dz in (1, -1, 0) for dx in (1, -1, 0) if dx or dz]
    lane_rows = walls * face // LANES

    def kernel(
        field_ref, first_hbm, second_hbm, edges_hbm, index_hbm, route_hbm, high_hbm, low_hbm,
        gather_hbm, zleft_hbm, xright_hbm, spread_hbm,
        out_ref, plane_hbm, new_first_hbm, new_second_hbm,
        first_ref, second_ref, edges_ref, index_ref, route_ref, new_first_ref, new_second_ref,
        u_ref, high_ref, low_ref, gather_ref, zleft_ref, xright_ref, spread_ref,
        mask_ref, mixed_ref, feat_ref, feats_ref, turn_ref, z_ref, g_ref, e_ref, w2_ref,
        count_ref, tile_ref, part_ref, cross_ref, total_ref, stress_ref, place_ref, plane_ref,
        xs_ref, xr_ref, zs_ref, zr_ref, line_ref,
        load_sem, out_sem, count_send, count_recv, part_send, part_recv, cross_send, cross_recv,
        total_send, total_recv, stress_send, stress_recv, xs_send, xr_recv, zs_send, zr_recv,
        line_send, line_recv,
    ):
        me = lax.axis_index("solver")
        mine = lax.axis_index("group")

        def peer_s(offset):
            return lax.rem(me + offset, learners)

        def peer_g(offset):
            return lax.rem(mine + offset, groups)

        loads = [
            pltpu.make_async_copy(
                field_ref.at[:, pl.ds(part * LANES, LANES)], u_ref.at[0, part], load_sem.at[part])
            for part in range(2)
        ]
        loads.append(pltpu.make_async_copy(high_hbm, high_ref, load_sem.at[2]))
        loads.append(pltpu.make_async_copy(low_hbm, low_ref, load_sem.at[3]))
        for at, (table, held_table) in enumerate((
            (gather_hbm, gather_ref), (zleft_hbm, zleft_ref), (xright_hbm, xright_ref),
            (spread_hbm, spread_ref),
        )):
            loads.append(pltpu.make_async_copy(table, held_table, load_sem.at[4 + at]))
        small_loads = [
            pltpu.make_async_copy(array, held_array, load_sem.at[4 + len(tables) + at])
            for at, (array, held_array) in enumerate((
                (edges_hbm, edges_ref), (route_hbm, route_ref), (first_hbm, first_ref),
                (second_hbm, second_ref), (index_hbm, index_ref),
            ))
        ]
        for load in loads[:2] + small_loads + loads[2:]:
            load.start()

        barrier = pltpu.get_barrier_semaphore()
        for offset in range(1, learners):
            pl.semaphore_signal(
                barrier, inc=1, device_id={"solver": peer_s(offset)},
                device_id_type=pl.DeviceIdType.MESH,
            )
        for offset in range(1, groups):
            pl.semaphore_signal(
                barrier, inc=1, device_id={"group": peer_g(offset)},
                device_id_type=pl.DeviceIdType.MESH,
            )
        for dx, dz in around:
            if dx and dz:
                pl.semaphore_signal(
                    barrier, inc=1,
                    device_id={"solver": peer_s(dx % learners), "group": peer_g(dz % groups)},
                    device_id_type=pl.DeviceIdType.MESH,
                )

        def remote(source, target, send, recv, where):
            return pltpu.make_async_remote_copy(
                src_ref=source, dst_ref=target, send_sem=send, recv_sem=recv,
                device_id=where, device_id_type=pl.DeviceIdType.MESH,
            )

        lane = lax.broadcasted_iota(jnp.int32, (1, LANES), 1)
        low_half = lane < half
        slot = lax.rem(lane, block) // EY
        level = lax.rem(lane, EY)
        contract = (((1,), (1,)), ((), ()))

        for load in small_loads:
            load.wait()
        learner_rows = lax.broadcasted_iota(jnp.int32, (learners, route_ref.shape[1]), 0)
        hits = (route_ref[...] == learner_rows).astype(F32)
        count_ref[me] = jnp.broadcast_to(jnp.sum(hits, axis=1, keepdims=True), (learners, LANES))

        big = 2 * LANES
        edge_rows = lax.rem(
            lax.broadcasted_iota(jnp.int32, (big, edges_ref.shape[1]), 0), face)
        source = (edges_ref[0:1, :] == edge_rows).astype(F32).astype(BF16)
        sink = (edges_ref[1:2, :] == edge_rows).astype(F32).astype(BF16)
        node_rows = lax.broadcasted_iota(jnp.int32, (big, big), 0)
        node_cols = lax.broadcasted_iota(jnp.int32, (big, big), 1)
        graph = 0.25 * lax.dot_general(source, sink, contract, preferred_element_type=F32)
        graph = jnp.where(node_rows // face == node_cols // face, graph, 0.0)
        graph = graph + (node_rows == node_cols).astype(F32)
        graph = graph.astype(BF16)
        small = graph[:LANES, :LANES]
        first = first_ref[...].astype(F32)
        second = second_ref[...].astype(F32)
        places = 2 * lax.broadcasted_iota(jnp.int32, (lane_rows, index_ref.shape[1]), 0)
        taken = index_ref[...]
        taken = 2 * (lax.rem(taken, EZL) // 2 * EXL + taken // EZL) + lax.rem(taken, 2)
        chosen = (taken == places).astype(F32)
        even = lax.dot_general(chosen, hits, contract, preferred_element_type=F32)
        chosen = (taken == places + 1).astype(F32)
        odd = lax.dot_general(chosen, hits, contract, preferred_element_type=F32)
        times = [
            jnp.where(low_half, even[:, learner:learner + 1], odd[:, learner:learner + 1])
            for learner in range(learners)
        ]

        def prepare(first, second):
            padding = jnp.zeros((LANES - points - 1, width), F32)
            both = jnp.transpose(jnp.concatenate([first, second, padding], axis=0))
            w2_ref[...] = jnp.broadcast_to(both[:, points:points + 1], (width, LANES))
            return both.astype(BF16)

        turned = prepare(first, second)
        feats_ref[...] = jnp.zeros_like(feats_ref)

        def through_graph(value, axis):
            pieces = []
            for piece in range(3):
                pieces.append(value.astype(BF16))
                value = value - pieces[-1].astype(F32)
            result = lax.dot_general(
                jnp.concatenate(pieces, axis=0), small, (((1,), (axis,)), ((), ())),
                preferred_element_type=F32)
            return result[:lane_rows] + result[lane_rows:2 * lane_rows] + result[2 * lane_rows:]


        def copies(step):
            right, left = {"solver": peer_s(1)}, {"solver": peer_s(learners - 1)}
            up, down = {"group": peer_g(1)}, {"group": peer_g(groups - 1)}
            result = []
            at = step if step < fused else pl.ds(fused, 2)
            for side, where in ((0, right), (1, left)):
                result.append(remote(
                    xs_ref.at[at, side], xr_ref.at[at, side],
                    xs_send.at[step, side], xr_recv.at[step, side], where))
            for side, where in ((0, up), (1, down)):
                result.append(remote(
                    zs_ref.at[at, side], zr_ref.at[at, side],
                    zs_send.at[step, side], zr_recv.at[step, side], where))
            if step == fused:
                for way, (dx, dz) in enumerate(corners):
                    result.append(remote(
                        line_ref.at[0, way], line_ref.at[1, way], line_send.at[way], line_recv.at[way],
                        {"solver": peer_s(dx % learners), "group": peer_g(dz % groups)}))
            return result

        half_face = face // 2

        def near(i):
            return pl.ds(i * face, points, stride=points)

        def far(i):
            return pl.ds(i * face + last, points, stride=points)

        def pack_z(step, bottoms, tops):
            for part in range(2):
                high_pack = jnp.zeros((points, LANES), F32)
                low_pack = jnp.zeros((points, LANES), F32)
                for i in range(points):
                    high_pack = jnp.where(slot == i, roll(tops[part][i], EY * (i + 1)), high_pack)
                    low_pack = jnp.where(slot == i, roll(bottoms[part][i], EY * i), low_pack)
                zs_ref[step, 0, part] = high_pack
                zs_ref[step, 1, part] = low_pack

        def pack_x(step, u):
            upper = u[1, pl.ds(nodes - face, face), :]
            xs_ref[step, 0] = jnp.where(low_half, roll(upper[:half_face], half), upper[half_face:])
            lower = u[0, pl.ds(0, face), :]
            xs_ref[step, 1] = jnp.where(low_half, lower[:half_face], roll(lower[half_face:], half))

        def pack_faces(step, u):
            pack_z(step, [[u[part, near(i), :] for i in range(points)] for part in range(2)],
                   [[u[part, far(i), :] for i in range(points)] for part in range(2)])
            pack_x(step, u)

        def send_faces(step):
            every = copies(step)
            for copy in every[4:] + every[2:4] + every[:2]:
                copy.start()

        start = u_ref.at[0]
        for load in loads[:2]:
            load.wait()

        def face_rows(value_of):
            rows = jnp.concatenate([value_of(i) for i in range(points)], axis=0)
            return jnp.concatenate([rows, rows], axis=0).astype(BF16)

        def plane(i, j):
            at = pl.ds(i * face + j * points, points)
            return jnp.concatenate([start[0, at, :], start[1, at, :]], axis=1)

        def slope(i):
            total = None
            for j in range(points):
                term = first_row[j] * plane(i, j)
                total = term if total is None else total + term
            return STRESS_SCALE * total

        wall_rows = lax.broadcasted_iota(jnp.int32, (walls, elements), 0)
        wall_cols = lax.broadcasted_iota(jnp.int32, (walls, elements), 1)
        wall_at = (
            lax.rem(wall_rows // 2, EXL) * EZL + wall_rows // (2 * EXL) * 2 + lax.rem(wall_rows, 2))
        select = (wall_cols == wall_at * EY).astype(F32).astype(BF16)
        for j in range(points):
            turn_ref[pl.ds(j * walls, walls), :] = lax.dot_general(
                select, face_rows(lambda i: plane(i, j)), contract, preferred_element_type=F32)
        turn_ref[pl.ds(points * walls, walls), :] = lax.dot_general(
            select, face_rows(slope), contract, preferred_element_type=F32)
        for row in range(lane_rows):
            even = turn_ref[pl.ds(2 * row, points, stride=walls), :]
            odd = turn_ref[pl.ds(2 * row + 1, points, stride=walls), :]
            feat_ref[row // 2, :, pl.ds((row % 2) * LANES, LANES)] = jnp.where(low_half, even, odd)
        for pair in range(pairs):
            feats_ref[pair, pl.ds(0, 2 * points), :] = jnp.concatenate(
                [feat_ref[pair], jnp.zeros((points, 2 * LANES), F32)], axis=0).astype(BF16)
        target = jnp.where(
            low_half,
            turn_ref[pl.ds(points * walls, lane_rows, stride=2), :],
            turn_ref[pl.ds(points * walls + 1, lane_rows, stride=2), :],
        )

        pack_faces(0, start)
        pl.semaphore_wait(barrier, learners + groups + 2)
        for offset in range(1, learners):
            remote(count_ref.at[me], count_ref.at[me], count_send.at[offset], count_recv.at[me],
                   {"solver": peer_s(offset)}).start()
        send_faces(0)

        def network(turned, learn):
            def one(pair, carry):
                before = jnp.dot(turned, feats_ref[pair], preferred_element_type=F32)
                hidden = jnp.maximum(before, 0.0)
                if learn:
                    mask_ref[pair] = jnp.where(before > 0.0, 1.0, 0.0).astype(BF16)
                    mixed = jnp.dot(
                        hidden.astype(BF16), graph, preferred_element_type=F32).astype(BF16)
                    mixed_ref[pair] = mixed
                    hidden = mixed.astype(F32)
                weight = w2_ref[...]
                z_ref[pl.ds(2 * pair, 1), :] = jnp.sum(
                    hidden[:, :LANES] * weight, axis=0, keepdims=True)
                z_ref[pl.ds(2 * pair + 1, 1), :] = jnp.sum(
                    hidden[:, LANES:] * weight, axis=0, keepdims=True)
                return carry

            lax.fori_loop(0, pairs, one, 0, unroll=pairs)
            return z_ref[...]

        output = network(turned, True)

        for offset in range(1, learners):
            origin = peer_s(offset)
            remote(count_ref.at[me], count_ref.at[origin], count_send.at[offset],
                   count_recv.at[origin], {"solver": origin}).wait_recv()
        counts = count_ref[0]
        for other in range(1, learners):
            counts = counts + count_ref[other]
        inverse = 1.0 / (jnp.maximum(counts, 1.0) * devices)
        difference = output - target
        error = jnp.zeros((lane_rows, LANES), F32)
        for learner in range(learners):
            single = (difference * inverse[learner:learner + 1]).astype(BF16).astype(F32)
            error = error + times[learner] * single
        e_ref[...] = error
        g_ref[...] = through_graph(error, 1)

        def split(value):
            upper = value.astype(BF16).astype(F32)
            return jnp.concatenate([upper, value - upper], axis=0).astype(BF16)

        def row_pair(ref, pair):
            return jnp.concatenate([ref[pl.ds(2 * pair, 1), :], ref[pl.ds(2 * pair + 1, 1), :]], axis=1)

        moment = None
        for pair in range(pairs):
            term = lax.dot_general(
                split(feat_ref[pair] * row_pair(g_ref, pair)), mask_ref[pair], contract,
                preferred_element_type=F32)
            moment = term if moment is None else moment + term
        moment = moment[0:points] + moment[points:2 * points]
        error_rows = [
            jnp.broadcast_to(e_ref[pl.ds(row, 1), :], (16, LANES)) for row in range(lane_rows)
        ]
        for t in range(owners):
            blocks = []
            for at in range(t * owned, (t + 1) * owned, 16):
                total = None
                for row in range(lane_rows):
                    mixed = mixed_ref[
                        row // 2, pl.ds(at, 16), pl.ds(row % 2 * LANES, LANES)].astype(F32)
                    total = mixed * error_rows[row] if total is None else (
                        total + mixed * error_rows[row])
                blocks.append(total)
            turned = jnp.transpose(jnp.concatenate(blocks, axis=0))
            tile_ref[t, pl.ds(points, 1), :] = jnp.sum(turned, axis=0, keepdims=True)
            tile_ref[t, pl.ds(0, points), :] = moment[:, t * owned:(t + 1) * owned]

        def when_owner(which, action):
            if owners == learners:
                action()
            else:
                pl.when(which < owners)(action)

        def clamp(which):
            return which if owners == learners else jnp.minimum(which, owners - 1)

        def part_copy(offset):
            where = peer_s(offset)
            return where, remote(tile_ref.at[clamp(where)], part_ref.at[me], part_send.at[offset],
                                 part_recv.at[me], {"solver": where})

        for offset in range(1, learners):
            where, copy = part_copy(offset)
            when_owner(where, copy.start)

        def local(source, target):
            u = jnp.concatenate([source[0], source[1]], axis=1)
            upper = u.astype(BF16)
            lower = (u - upper.astype(F32)).astype(BF16)
            u = u + (
                jnp.dot(high_ref[...], upper, preferred_element_type=F32)
                + jnp.dot(high_ref[...], lower, preferred_element_type=F32)
                + jnp.dot(low_ref[...], upper, preferred_element_type=F32)
            )
            for part in range(2):
                target[part] = u[:, part * LANES:(part + 1) * LANES]
            for part in range(2):
                for i in range(points):
                    base = i * face
                    bottom = source[part, pl.ds(base, points), :]
                    top = source[part, pl.ds(base + face - points, points), :]
                    below = jnp.where(level == 0, bottom, roll(top, 1))
                    above = jnp.where(level == EY - 1, 0.0, roll(bottom, -1))
                    target[part, pl.ds(base, points), :] += step_gain * below
                    target[part, pl.ds(base + face - points, points), :] += step_gain * above
            low0 = roll(source[0, pl.ds(nodes - face, face), :], half)
            low1 = roll(source[1, pl.ds(nodes - face, face), :], half)
            target[0, pl.ds(0, face), :] += step_gain_x * jnp.where(low_half, 0.0, low0)
            target[1, pl.ds(0, face), :] += step_gain_x * jnp.where(low_half, low0, low1)
            high0 = roll(source[0, pl.ds(0, face), :], half)
            high1 = roll(source[1, pl.ds(0, face), :], half)
            target[0, pl.ds(nodes - face, face), :] += step_gain * jnp.where(low_half, high0, high1)
            target[1, pl.ds(nodes - face, face), :] += step_gain * jnp.where(low_half, high1, 0.0)
            for part in range(2):
                for i in range(points):
                    before = jnp.where(slot == 0, 0.0, roll(source[part, far(i), :], EY))
                    after = jnp.where(slot == EZL - 1, 0.0, roll(source[part, near(i), :], -EY))
                    target[part, near(i), :] = target[part, near(i), :] + step_gain * before
                    target[part, far(i), :] = target[part, far(i), :] + step_gain * after

        def reflect():
            before, after = fused, fused + 1
            xr_ref[after, 1] += step_gain_x * xs_ref[before, 0]
            xr_ref[after, 0] += step_gain * xs_ref[before, 1]
            for part in range(2):
                zr_ref[after, 1, part] += step_gain * roll(zs_ref[before, 0, part], half)
                zr_ref[after, 0, part] += step_gain * roll(zs_ref[before, 1, part], half)
            group_at = lane // EY
            end = EZL - 1
            for way, (dx, dz) in enumerate(corners):
                tile = line_ref[1, way]
                held_at = (EZL if dx == 1 else 0) + (end if dz == 1 else 0)

                def to(group):
                    return jnp.where(group_at == group, roll(tile, (group - held_at) * EY), 0.0)

                first_half = 0 if dz == 1 else end
                side, rows = (0 if dx == 1 else 1), pl.ds(0 if dz == 1 else last, points // 2, stride=points)
                xr_ref[after, side, rows, :] = xr_ref[after, side, rows, :] + step_gain * (
                    to(first_half)[:points // 2] + to(EZL + first_half)[points // 2:])
                if dx == 1:
                    part, rate, group = 0, step_gain_x, 0
                else:
                    part, rate, group = 1, step_gain, 2 * EZL - 1
                if dz == 1:
                    group = (group + EZL) % (2 * EZL)
                zr_ref[after, 0 if dz == 1 else 1, part] += rate * to(group)

        def halo(step, target):
            every = copies(step) if step <= fused else []
            for copy in every:
                copy.wait_recv()
            ghost = xr_ref[step, 0]
            ghost = jnp.concatenate([ghost, roll(ghost, half)], axis=0)
            target[0, pl.ds(0, face), :] += step_gain_x * jnp.where(low_half, ghost, 0.0)
            ghost = xr_ref[step, 1]
            ghost = jnp.concatenate([roll(ghost, half), ghost], axis=0)
            target[1, pl.ds(nodes - face, face), :] += step_gain * jnp.where(low_half, 0.0, ghost)
            bottoms, tops = [], []
            for part in range(2):
                before_pack = step_gain * zr_ref[step, 0, part]
                after_pack = step_gain * zr_ref[step, 1, part]
                for i in range(points):
                    before = jnp.where(slot == 0, roll(before_pack, half - EY * i), 0.0)
                    after = jnp.where(
                        slot == EZL - 1, roll(after_pack, EY * (EZL - 1 - i)), 0.0)
                    bottoms.append(target[part, near(i), :] + before)
                    tops.append(target[part, far(i), :] + after)
                    target[part, near(i), :] = bottoms[-1]
                    target[part, far(i), :] = tops[-1]
            if step == fused:
                reflect()
            if step < fused:
                pack_z(step + 1, [bottoms[:points], bottoms[points:]], [tops[:points], tops[points:]])
                pack_x(step + 1, target)
                if step + 1 == fused:
                    beyond = held[step % 2]
                    local(target, beyond)
                    pack_faces(step + 2, beyond)
                    for way, (dx, dz) in enumerate(corners):
                        part, i = (1, last) if dx == 1 else (0, 0)
                        line_ref[0, way] = target[part, far(i) if dz == 1 else near(i), :]
                send_faces(step + 1)

        place_ref[...] = jnp.zeros_like(place_ref)
        for load in loads[2:]:
            load.wait()
        held = [start, u_ref.at[1]]

        def flow(step):
            source, target = held[step % 2], held[(step + 1) % 2]
            if step != fused:
                local(source, target)
            halo(step, target)

        flow(0)

        def reduce_part():
            total = tile_ref[clamp(me)]
            for offset in range(1, learners):
                origin = peer_s(offset)
                remote(tile_ref.at[0], part_ref.at[origin], part_send.at[offset],
                       part_recv.at[origin], {"solver": origin}).wait_recv()
            for offset in range(1, learners):
                total = total + part_ref[peer_s(offset)]
            cross_ref[mine] = total
            for offset in range(1, groups):
                remote(cross_ref.at[mine], cross_ref.at[mine], cross_send.at[offset],
                       cross_recv.at[mine], {"group": peer_g(offset)}).start()

        def reduce_cross():
            for offset in range(1, groups):
                origin = peer_g(offset)
                remote(cross_ref.at[mine], cross_ref.at[origin], cross_send.at[offset],
                       cross_recv.at[origin], {"group": origin}).wait_recv()
            total = cross_ref[0]
            for origin in range(1, groups):
                total = total + cross_ref[origin]
            at = clamp(me)
            total_ref[at] = total
            for offset in range(1, learners):
                remote(total_ref.at[at], total_ref.at[at], total_send.at[offset],
                       total_recv.at[at], {"solver": peer_s(offset)}).start()

        when_owner(me, reduce_part)
        flow(1)
        when_owner(me, reduce_cross)
        flow(2)
        for offset in range(1, learners):
            origin = peer_s(offset)
            at = clamp(origin)
            copy = remote(total_ref.at[at], total_ref.at[at], total_send.at[offset],
                          total_recv.at[at], {"solver": origin})
            when_owner(origin, copy.wait_recv)

        sums = jnp.concatenate([total_ref[t] for t in range(owners)], axis=1)
        new_first = (first - LEARN_RATE * (sums[0:points] * second)).astype(BF16)
        new_second = (second - LEARN_RATE * sums[points:points + 1]).astype(BF16)
        new_first_ref[...] = new_first
        new_second_ref[...] = new_second
        updates = [
            pltpu.make_async_copy(new_first_ref, new_first_hbm, out_sem.at[points // 2]),
            pltpu.make_async_copy(new_second_ref, new_second_hbm, out_sem.at[points // 2 + 1]),
        ]
        for copy in updates:
            copy.start()

        middle = pl.ds(lane_rows // 2, lane_rows)
        plain = network(prepare(new_first.astype(F32), new_second.astype(F32)), False)
        stress_ref[1, middle, :] = through_graph(plain, 0)
        stress_copies = []
        for way, (dx, dz) in enumerate(around):
            rows = {
                0: (middle, middle),
                1: (pl.ds(lane_rows, lane_rows // 2), pl.ds(0, lane_rows // 2)),
                -1: (pl.ds(lane_rows // 2, lane_rows // 2), pl.ds(3 * lane_rows // 2, lane_rows // 2)),
            }[dz]
            stress_copies.append(remote(
                stress_ref.at[1, rows[0]], stress_ref.at[1 - dx, rows[1]],
                stress_send.at[way], stress_recv.at[way],
                {"solver": peer_s(dx % learners), "group": peer_g(dz % groups)}))
        for copy in stress_copies:
            copy.start()
        for step in range(3, FLOW_STEPS):
            flow(step)
        results = [pltpu.make_async_copy(held[FLOW_STEPS % 2], out_ref, out_sem.at[1])]
        results[0].start()
        for copy in stress_copies:
            copy.wait_recv()

        def halves(value):
            upper = value.astype(BF16)
            return upper, (value - upper.astype(F32)).astype(BF16)

        within = lax.rem(lane, face) // points
        sub = lax.broadcasted_iota(jnp.int32, (points, LANES), 0)
        own_row = within == sub
        for q in range(EZL):
            for e in range(0, 3 * EXL, 2):
                blocks = []
                for at in (e, e + 1):
                    row = stress_ref[at // EXL, pl.ds(q * EXL + at % EXL, 1), :]
                    blocks.append(jnp.where(own_row, jnp.broadcast_to(row, (points, LANES)), 0.0))
                upper, lower = halves(jnp.concatenate(blocks, axis=0))
                columns = pl.ds(q * LANES, LANES)
                place_ref[pl.ds(e * points, 2 * points), columns] = upper
                place_ref[pl.ds(LANES + e * points, 2 * points), columns] = lower
        both = lax.dot_general(
            gather_ref[...], place_ref[...], contract, preferred_element_type=F32)
        upper, lower = halves(both[:, :LANES] + both[:, LANES:])
        ladder = jnp.dot(
            zleft_ref[...], jnp.concatenate([upper, lower, upper], axis=0),
            preferred_element_type=F32)
        z_points = EZL * points
        upper, lower = halves(jnp.concatenate(
            [ladder[c * z_points:(c + 1) * z_points] for c in range(reach + 1)], axis=1))
        depth = (reach + 1) * LANES
        plane_t = jnp.dot(
            jnp.concatenate([upper, lower], axis=0), xright_ref[pl.ds(0, depth), :],
            preferred_element_type=F32)
        plane_t = plane_t[:z_points] + plane_t[z_points:] + jnp.dot(
            upper, xright_ref[pl.ds(depth, depth), :], preferred_element_type=F32)
        span = EXL * points
        per = LANES // span
        quarter = lane // span
        rows = []
        for m in range(reach + 1):
            sides = []
            for t in range(EZL // per):
                value = None
                for e in range(per):
                    z_at = (t * per + e) * points
                    piece = roll(
                        plane_t[z_at:z_at + points, (m // per) * LANES:(m // per + 1) * LANES],
                        (e - m % per) * span)
                    value = piece if value is None else jnp.where(quarter == e, piece, value)
                sides.append(value)
            value = jnp.concatenate(sides, axis=1)
            upper = value.astype(BF16).astype(F32)
            value = jnp.concatenate([upper, value - upper], axis=1)
            node = lax.rem(lax.broadcasted_iota(jnp.int32, value.shape, 1), points)
            rows += [jnp.where(node == i, value, 0.0) for i in range(points)]
        plane_ref[...] = jnp.dot(
            jnp.concatenate(rows, axis=0).astype(BF16), spread_ref[...],
            preferred_element_type=F32)
        results.append(pltpu.make_async_copy(plane_ref, plane_hbm, out_sem.at[0]))
        results[-1].start()

        for offset in range(1, learners):
            remote(count_ref.at[me], count_ref.at[me], count_send.at[offset], count_recv.at[me],
                   {"solver": peer_s(offset)}).wait_send()
            where, copy = part_copy(offset)
            when_owner(where, copy.wait_send)

        def drain_owned():
            at = clamp(me)
            for offset in range(1, groups):
                remote(cross_ref.at[mine], cross_ref.at[mine], cross_send.at[offset],
                       cross_recv.at[mine], {"group": peer_g(offset)}).wait_send()
            for offset in range(1, learners):
                remote(total_ref.at[at], total_ref.at[at], total_send.at[offset],
                       total_recv.at[at], {"solver": peer_s(offset)}).wait_send()

        when_owner(me, drain_owned)
        for copy in results + updates:
            copy.wait()
        for copy in stress_copies:
            copy.wait_send()
        for step in range(fused + 1):
            for copy in copies(step):
                copy.wait_send()

    dma = pltpu.SemaphoreType.DMA
    scratch = [
        pltpu.VMEM((points, width), BF16),
        pltpu.VMEM((1, width), BF16),
        pltpu.VMEM(small_shapes[0], jnp.int32),
        pltpu.VMEM(small_shapes[1], jnp.int32),
        pltpu.VMEM(small_shapes[2], jnp.int32),
        pltpu.VMEM((points, width), BF16),
        pltpu.VMEM((1, width), BF16),
        pltpu.VMEM((2, 2, nodes, LANES), F32),
        pltpu.VMEM((nodes, nodes), BF16),
        pltpu.VMEM((nodes, nodes), BF16),
        *[pltpu.VMEM(table.shape, table.dtype) for table in tables],
        pltpu.VMEM((pairs, width, 2 * LANES), BF16),
        pltpu.VMEM((pairs, width, 2 * LANES), BF16),
        pltpu.VMEM((pairs, points, 2 * LANES), F32),
        pltpu.VMEM((pairs, LANES, 2 * LANES), BF16),
        pltpu.VMEM((points * walls + walls, LANES), F32),
        pltpu.VMEM((lane_rows, LANES), F32),
        pltpu.VMEM((lane_rows, LANES), F32),
        pltpu.VMEM((lane_rows, LANES), F32),
        pltpu.VMEM((width, LANES), F32),
        pltpu.VMEM((learners, learners, LANES), F32),
        pltpu.VMEM((owners, rows_sent, owned), F32),
        pltpu.VMEM((learners, rows_sent, owned), F32),
        pltpu.VMEM((groups, rows_sent, owned), F32),
        pltpu.VMEM((owners, rows_sent, owned), F32),
        pltpu.VMEM((3, 2 * lane_rows, LANES), F32),
        pltpu.VMEM((2 * LANES, EZL * LANES), BF16),
        pltpu.VMEM((FLOW_STEPS * face, 2 * LANES), F32),
        pltpu.VMEM((FLOW_STEPS, 2, face // 2, LANES), F32),
        pltpu.VMEM((FLOW_STEPS, 2, face // 2, LANES), F32),
        pltpu.VMEM((FLOW_STEPS, 2, 2, points, LANES), F32),
        pltpu.VMEM((FLOW_STEPS, 2, 2, points, LANES), F32),
        pltpu.VMEM((2, 4, points, LANES), F32),
        dma((9 + len(tables),)), dma((points // 2 + 2,)),
        dma((learners,)), dma((learners,)), dma((learners,)), dma((learners,)),
        dma((groups,)), dma((groups,)), dma((learners,)), dma((owners,)),
        dma((len(around),)), dma((len(around),)),
        dma((FLOW_STEPS, 2)), dma((FLOW_STEPS, 2)), dma((FLOW_STEPS, 2)), dma((FLOW_STEPS, 2)),
        dma((4,)), dma((4,)),
    ]
    return kernel, scratch


def finish(
    points, free_hbm, plane_hbm, weights_hbm, first_ref, second_ref,
    out_ref, new_first_ref, new_second_ref,
    free_ref, plane_ref, weights_ref, result_ref, held_first_ref, held_second_ref, in_sem, out_sem
):
    face = points * points
    ways = [
        (plane_hbm, plane_ref), (weights_hbm, weights_ref), (free_hbm, free_ref),
        (first_ref, held_first_ref), (second_ref, held_second_ref),
    ]
    loads = [pltpu.make_async_copy(way[0], way[1], in_sem.at[at]) for at, way in enumerate(ways)]
    for load in loads:
        load.start()
    for load in loads:
        load.wait()
    stores = [
        pltpu.make_async_copy(held_first_ref, new_first_ref, out_sem.at[CHUNKS]),
        pltpu.make_async_copy(held_second_ref, new_second_ref, out_sem.at[CHUNKS + 1]),
    ]
    for store in stores:
        store.start()
    each = points // CHUNKS
    for chunk in range(CHUNKS):
        for i in range(chunk * each, (chunk + 1) * each):
            for part in range(2):
                columns = slice(part * LANES, (part + 1) * LANES)
                planes = [
                    plane_ref[pl.ds((m * points + i) * points, points), columns]
                    for m in range(FLOW_STEPS)
                ]
                for j in range(points):
                    at = pl.ds(i * face + j * points, points)
                    value = free_ref[part, at, :]
                    for m in range(FLOW_STEPS):
                        value = value + (
                            weights_ref[pl.ds((m * points + j) * points, points), :] * planes[m])
                    result_ref[at, columns] = value
        rows = pl.ds(chunk * each * face, each * face)
        stores.append(
            pltpu.make_async_copy(result_ref.at[rows], out_ref.at[rows], out_sem.at[chunk]))
        stores[-1].start()
    for store in stores:
        store.wait()


def shards(field, first_weight, second_weight, face_edges, sample_index, route):
    points = field.shape[0]
    elements = field.shape[3]
    nodes = points**3
    width = first_weight.shape[1]
    learners = lax.axis_size("solver")
    groups = lax.axis_size("group")
    deriv, end_weight = gll_tables(points)
    gain = 2.0 / end_weight
    high, low = element_operator(deriv, gain)
    *tables, weights = response_tables(deriv, gain)
    kernel, scratch = make_kernel(
        learners, groups, points, width, deriv, gain, tables,
        (face_edges.shape, (1, sample_index.size), (1, route.size)))
    hbm = pl.BlockSpec(memory_space=pltpu.HBM)
    free, planes, new_first, new_second = pl.pallas_call(
        kernel,
        out_shape=(
            jax.ShapeDtypeStruct((2, nodes, LANES), F32),
            jax.ShapeDtypeStruct((FLOW_STEPS * points * points, 2 * LANES), F32),
            jax.ShapeDtypeStruct(first_weight.shape, BF16),
            jax.ShapeDtypeStruct((1, width), BF16),
        ),
        in_specs=[hbm] * (8 + len(tables)),
        out_specs=(hbm,) * 4,
        scratch_shapes=scratch,
        compiler_params=pltpu.CompilerParams(
            collective_id=0, has_side_effects=True, vmem_limit_bytes=67_043_328
        ),
        name="step",
    )(
        field.reshape(nodes, elements),
        first_weight,
        second_weight.reshape(1, width),
        face_edges,
        sample_index.reshape(1, -1),
        route.reshape(1, -1),
        jnp.asarray(high),
        jnp.asarray(low),
        *[jnp.asarray(table) for table in tables],
    )
    dma = pltpu.SemaphoreType.DMA
    new_field, new_first, new_second = pl.pallas_call(
        functools.partial(finish, points),
        out_shape=(
            jax.ShapeDtypeStruct((nodes, elements), F32),
            jax.ShapeDtypeStruct(new_first.shape, BF16),
            jax.ShapeDtypeStruct(new_second.shape, BF16),
        ),
        in_specs=[hbm] * 5,
        out_specs=(hbm, hbm, hbm),
        scratch_shapes=[
            pltpu.VMEM(free.shape, F32),
            pltpu.VMEM(planes.shape, F32),
            pltpu.VMEM(weights.shape, F32),
            pltpu.VMEM((nodes, elements), F32),
            pltpu.VMEM(new_first.shape, BF16),
            pltpu.VMEM(new_second.shape, BF16),
            dma((5,)),
            dma((CHUNKS + 2,)),
        ],
        compiler_params=pltpu.CompilerParams(vmem_limit_bytes=67_043_328),
        name="finish",
    )(free, planes, jnp.asarray(weights), new_first, new_second)
    return (new_field.reshape(field.shape), new_first, new_second.reshape(second_weight.shape))


def solution(mesh):
    return jax.shard_map(
        shards,
        mesh=mesh,
        in_specs=(
            P(None, None, None, ("solver", "group")),
            P(),
            P(),
            P(),
            P(("solver", "group")),
            P(("solver", "group"), None),
        ),
        out_specs=(P(None, None, None, ("solver", "group")), P(), P()),
        check_vma=False,
    )
```
